32 devices in a mesh: groups: 2 (over x), dp: 4 (over y, core), expert: 4 (over z).
Axes of the slice: x: 2, y: 2, z: 4, core: 2. Of those that a mesh axis runs over, the one named last changes fastest.
Arguments:
- query: bfloat16 [128, 4096], P(('groups', 'dp', 'expert')), parts along dimension 0, may hold values from -27 to 27
- fresh_kv: bfloat16 [128, 512], P(('groups', 'dp', 'expert')), parts along dimension 0, may hold values from -16 to 16
- cache: bfloat16 [128, 512, 512], P(('groups', 'dp', 'expert')), parts along dimension 0, may hold values from -6 to 6
- lengths: int32 [128], P(('groups', 'dp', 'expert')), parts along dimension 0, may hold values from 2 to 512, as said below
- moves: int32 [8, 4], P('groups'), parts along dimension 0, may hold values from 0 to 3, as said below
- residual: bfloat16 [128, 4096], P(('groups', 'dp', 'expert')), parts along dimension 0, may hold values from -4 to 4
- out_weight: bfloat16 [4096, 4096], P('expert'), may hold values from -0.09375 to 0.09375
- norm_gain: float32 [4096], replicated, may hold values from 0.1 to 1.9
- w_gate: bfloat16 [4, 4096, 1536], P('dp', None, 'expert'), may hold values from -0.09375 to 0.09375
- w_up: bfloat16 [4, 4096, 1536], P('dp', None, 'expert'), may hold values from -0.09375 to 0.09375
- w_down: bfloat16 [4, 1536, 4096], P('dp', 'expert'), may hold values from -0.15625 to 0.15625
- routes: int32 [128, 2], P(('groups', 'dp', 'expert')), parts along dimension 0, may hold values from 0 to 3, all different within a row; in each aligned block of 4 rows (0 to 3, 4 to 7, ...) at most 3 rows name the same one
- gates: float32 [128, 2], P(('groups', 'dp', 'expert')), parts along dimension 0, may hold values from 0.05 to 0.5
Outputs:
- layer_out: bfloat16 [128, 4096], P(('groups', 'dp', 'expert')), parts along dimension 0
The draws below stay inside these ranges and needn't reach their ends.
There are 2 independent parts, one for each index of `groups`. The reference program is written for one: setup_inputs(seed, part) draws one part's arguments, and reference() takes and returns one part's arrays. A program takes and returns all parts, laid end to end along the dimension named above; an argument that names none is the same for every part. Nothing has to cross between parts.
Inputs may be any that keep to these rules, and one draw needn't show every extreme that they name: `lengths`: slot 0 of every device (the first of its 4 rows) holds 512 cached positions; other requests 2 to 512. For each expert index e, d -> moves[e, d] is one cycle through all 4 dp indices. `routes`: each row names 2 different experts; in the 4 rows of one device no expert is named by more than 3 rows, and in some device one expert is named by exactly 3.
All inputs are finite; a program needn't handle non-finite values.
Results may differ from the reference program's by a relative error of at most 0.0055.
Values may be sent and summed in bfloat16 or wider, within the bound.
No kernel may reach another device: no remote copies, remote signals or barrier semaphores. Data moves between devices by JAX's collectives and lax.ppermute only.
A program may use at most 128 MiB of HBM per device.

```python
import math
import jax
import jax.numpy as jnp
import numpy as np
from jax import lax

D = 4096
HD = 128
QH = 32
KVH = 2
FF = 1536
CTX = 512
REQ_DEV = 4
CAP = 3
EXPERTS = 4
TOP = 2
SLOTS = 64
N_DP = 4
N_EXPERT = 4


def draw_cache(key, part):
    base_draw = jnp.clip(jax.random.normal(jax.random.fold_in(key, 21), (SLOTS, CTX, 2 * KVH * HD), jnp.float32), -6.0, 6.0)
    return base_draw.astype(jnp.bfloat16)


def draw_query(key, part):
    base_draw = jnp.clip(jax.random.normal(jax.random.fold_in(key, 31), (SLOTS, QH * HD), jnp.float32), -6.0, 6.0)
    return base_draw.astype(jnp.bfloat16)


def draw_lengths(key, part):
    drawn = jax.random.randint(jax.random.fold_in(key, 41), (SLOTS,), 2, CTX + 1, jnp.int32)
    return jnp.where(jnp.arange(SLOTS, dtype=jnp.int32) % REQ_DEV == 0, CTX, drawn).astype(jnp.int32)


def draw_moves(key, part):
    key_list = jax.random.split(jax.random.fold_in(key, 51), N_EXPERT)
    orders = jax.vmap(lambda single: jax.random.permutation(single, N_DP))(key_list).astype(jnp.int32)
    shifted = jnp.roll(orders, -1, axis=1)
    row_ids = jnp.arange(N_EXPERT, dtype=jnp.int32)[:, None]
    return jnp.zeros((N_EXPERT, N_DP), jnp.int32).at[row_ids, orders].set(shifted)


def level_of(rng, dims, shards, least, top_value):
    def one(position, parts):
        heights = jax.random.uniform(jax.random.fold_in(jax.random.fold_in(rng, 6), position), (parts,), jnp.float32, least / len(shards), top_value / len(shards))
        return jnp.repeat(jnp.exp(heights), dims[position] // parts).reshape((-1,) + (1,) * (len(dims) - position - 1))

    level = one(*shards[0])
    for cut in shards[1:]:
        level = level * one(*cut)
    return level


def deal_out(own_key, own, number, rows, count, top, reach, lean):
    order = jax.random.permutation(own_key, count)
    crowded, common = shares(count, rows * top, reach, lean, True), shares(count, rows * top, reach, lean, False)
    places = jnp.arange(count)

    def named(tallies, rotation):
        used = int((tallies > 0).sum())
        fixed = max(1, used // 4)
        moved = fixed + (places - fixed + rotation * (used - fixed)) % max(1, count - fixed)
        return jnp.zeros((count,), jnp.int32).at[order[jnp.where(places < fixed, places, moved)]].set(jnp.asarray(tallies, jnp.int32))

    tallies = jnp.where(number % 4 == 0, named(crowded, number // 4), named(common, number - number // 4 - 1))
    mixed = jax.random.permutation(jax.random.fold_in(own, 3), count)
    giver, receiver = mixed[0:count // 2 * 2:2], mixed[1:count // 2 * 2:2]
    margin = jnp.minimum(tallies[giver] - 1, reach - tallies[receiver]) // 2
    margin = jnp.where((giver == order[0]) | (receiver == order[0]) | (tallies[receiver] == 0), 0, jnp.maximum(margin, 0))
    moved = jax.random.randint(jax.random.fold_in(own, 4), (count // 2,), 0, 1 << 20) % (margin + 1)
    tallies = tallies.at[giver].add(-moved).at[receiver].add(moved)
    items = jnp.searchsorted(jnp.cumsum(tallies), jnp.arange(rows * top), side="right").astype(jnp.int32)
    listing = items.reshape(top, rows).T
    listing = listing[jax.random.permutation(jax.random.fold_in(own, 1), rows)]
    rotation = jax.random.randint(jax.random.fold_in(own, 2), (rows, 1), 0, top)
    return jnp.take_along_axis(listing, (jnp.arange(top)[None, :] + rotation) % top, axis=1)


def shares(amount, total, most, lean, full):
    loads = [(1 << 20) // math.isqrt(grade ** lean) + 1 for grade in range(1, amount + 1)]
    largest = most if full else min(most, max(-(-total // amount), total * loads[0] // sum(loads)))
    least = 1 if total - largest >= amount - 1 else 0
    holding, surplus = [largest] + [least] * (amount - 1), total - largest - least * (amount - 1)
    while surplus > 0:
        movable = [i for i in range(1, amount) if holding[i] < largest] or [i for i in range(1, amount) if holding[i] < most]
        pool, left = sum([loads[i] for i in movable]), surplus
        for i in movable:
            extra = min(most - holding[i], max(1, left * loads[i] // pool), surplus)
            holding[i] = holding[i] + extra
            surplus = surplus - extra
    return np.array(holding)


def gaussian(key, extent, deviation, most, cuts=(), kind=jnp.bfloat16):
    result = jax.random.normal(key, extent, jnp.float32) * deviation
    if len(cuts) > 0:
        result = level_of(key, extent, cuts, -0.22, 0.18) * result
    return jnp.clip(result, min=-most, max=most).astype(kind)


def setup_inputs(seed: int = 0, part: int = 0) -> dict:
    streams_of = jax.random.split(jax.random.key(seed), 14)
    part_splits = jax.random.split(jax.random.fold_in(streams_of[13], part), 14)
    query = draw_query(jax.random.fold_in(jax.random.fold_in(streams_of[13], part), 71), part)
    fresh_kv = gaussian(part_splits[1], (SLOTS, 2 * KVH * HD), 3.0, 16.0, ((0, 16),))
    cache = draw_cache(jax.random.fold_in(jax.random.fold_in(streams_of[13], part), 71), part)
    lengths = draw_lengths(jax.random.fold_in(jax.random.fold_in(streams_of[13], part), 71), part)
    moves = draw_moves(jax.random.fold_in(jax.random.fold_in(streams_of[13], part), 71), part)
    residual = gaussian(part_splits[5], (SLOTS, D), 0.5, 4.0, ((0, 16),))
    out_weight = gaussian(streams_of[6], (QH * HD, D), (QH * HD) ** -0.5, 0.09375, ((0, 4),))
    norm_gain = jnp.clip(1.0 + 0.18 * jax.random.normal(streams_of[7], (D,), jnp.float32), 0.1, 1.9)
    w_gate = gaussian(streams_of[8], (EXPERTS, D, FF), D ** -0.5, 0.09375, ((0, 4), (2, 4)))
    w_up = gaussian(streams_of[9], (EXPERTS, D, FF), D ** -0.5, 0.09375, ((0, 4), (2, 4)))
    w_down = gaussian(streams_of[10], (EXPERTS, FF, D), FF ** -0.5, 0.15625, ((0, 4), (1, 4)))
    routes_keys = jax.random.split(jax.random.fold_in(part_splits[11], 1), SLOTS // REQ_DEV)
    routes_turns = jax.random.permutation(jax.random.fold_in(part_splits[11], 3), SLOTS // REQ_DEV)
    routes = jax.vmap(lambda own, number: deal_out(jax.random.fold_in(part_splits[11], 2), own, number, REQ_DEV, EXPERTS, TOP, CAP, 2))(routes_keys, routes_turns).reshape((SLOTS, TOP))
    gates = jnp.clip(jnp.exp(math.log(0.5) - 2.3025851 * jax.random.uniform(part_splits[12], (SLOTS, TOP), jnp.float32) ** level_of(part_splits[12], (SLOTS, TOP), ((0, 16),), -0.2, 0.2)), 0.05, 0.5)
    return dict(query=query, fresh_kv=fresh_kv, cache=cache, lengths=lengths, moves=moves, residual=residual, out_weight=out_weight, norm_gain=norm_gain, w_gate=w_gate, w_up=w_up, w_down=w_down, routes=routes, gates=gates)


norm_eps = 1e-06

def cache_part(queries, entries, lengths_used):
    count_rows = queries.shape[0]
    group_size = QH // KVH
    query_heads = queries.astype(jnp.float32).reshape(count_rows, KVH, group_size, HD)
    keys_all = entries[:, :, :KVH * HD].astype(jnp.float32).reshape(count_rows, CTX, KVH, HD)
    values_all = entries[:, :, KVH * HD:].astype(jnp.float32).reshape(count_rows, CTX, KVH, HD)
    scores = jnp.einsum('nhgd,nchd->nhgc', query_heads, keys_all) * HD ** (-0.5)
    valid_mask = (jnp.arange(CTX, dtype=jnp.int32)[None, :] < lengths_used[:, None])[:, None, None, :]
    scores = jnp.where(valid_mask, scores, -1e+30)
    row_max = lax.optimization_barrier(jnp.max(scores, axis=-1))
    weights_raw = jnp.where(valid_mask, jnp.exp(scores - row_max[..., None]), 0.0)
    row_sum = lax.optimization_barrier(jnp.sum(weights_raw, axis=-1))
    rounded = lax.optimization_barrier(weights_raw.astype(jnp.bfloat16)).astype(jnp.float32)
    out_cache = jnp.einsum('nhgc,nchd->nhgd', rounded, values_all)
    return (out_cache.reshape(count_rows, QH * HD), row_max.reshape(count_rows, QH), row_sum.reshape(count_rows, QH))

def combine_own(out_cache, row_max, row_sum, queries, fresh):
    count_rows = queries.shape[0]
    group_size = QH // KVH
    query_heads = queries.astype(jnp.float32).reshape(count_rows, KVH, group_size, HD)
    own_keys = fresh[:, :KVH * HD].astype(jnp.float32).reshape(count_rows, KVH, 1, HD)
    own_values = fresh[:, KVH * HD:].astype(jnp.float32).reshape(count_rows, KVH, 1, HD)
    own_score = lax.optimization_barrier(jnp.sum(query_heads * own_keys, axis=-1)) * HD ** (-0.5)
    max_heads = row_max.reshape(count_rows, KVH, group_size)
    sum_heads = row_sum.reshape(count_rows, KVH, group_size)
    top_score = jnp.maximum(max_heads, own_score)
    cache_factor = jnp.exp(max_heads - top_score)
    own_factor = jnp.exp(own_score - top_score)
    numer = cache_factor[..., None] * out_cache.reshape(count_rows, KVH, group_size, HD) + own_factor[..., None] * own_values
    denom = cache_factor * sum_heads + own_factor
    return (numer / denom[..., None]).reshape(count_rows, QH * HD).astype(jnp.bfloat16)

def reference(query, fresh_kv, cache, lengths, moves, residual, out_weight, norm_gain, w_gate, w_up, w_down, routes, gates):
    slot_ids = jnp.arange(SLOTS, dtype=jnp.int32)
    local_ids = slot_ids % REQ_DEV
    device_ids = slot_ids // REQ_DEV
    dp_ids = device_ids // N_EXPERT
    ex_ids = device_ids % N_EXPERT
    target = moves[ex_ids, dp_ids].astype(jnp.int32)
    new_of_old = jnp.where(local_ids == 0, (target * N_EXPERT + ex_ids) * REQ_DEV, slot_ids).astype(jnp.int32)
    old_of_new = jnp.zeros((SLOTS,), jnp.int32).at[new_of_old].set(slot_ids)
    query_old = query[new_of_old]
    block_count = SLOTS // REQ_DEV

    def one_block(items):
        return cache_part(items[0], items[1], items[2])
    out_all, max_all, sum_all = lax.map(one_block, (query_old.reshape(block_count, REQ_DEV, QH * HD), cache.reshape(block_count, REQ_DEV, CTX, 2 * KVH * HD), lengths.reshape(block_count, REQ_DEV)))
    out_new = out_all.reshape(SLOTS, QH * HD)[old_of_new]
    max_new = max_all.reshape(SLOTS, QH)[old_of_new]
    sum_new = sum_all.reshape(SLOTS, QH)[old_of_new]
    attended = combine_own(out_new, max_new, sum_new, query, fresh_kv)
    projected = jnp.dot(attended, out_weight, preferred_element_type=jnp.float32)
    hidden = residual.astype(jnp.float32) + projected
    normed = (hidden * lax.rsqrt(lax.optimization_barrier(jnp.mean(hidden * hidden, axis=-1, keepdims=True)) + norm_eps) * norm_gain.astype(jnp.float32)).astype(jnp.bfloat16)

    def expert_step(total, items):
        gate_w, up_w, down_w, expert_id = items
        gate_val = jnp.dot(normed, gate_w, preferred_element_type=jnp.float32)
        up_val = jnp.dot(normed, up_w, preferred_element_type=jnp.float32)
        activation = (jax.nn.silu(gate_val) * up_val).astype(jnp.bfloat16)
        expert_out = jnp.dot(activation, down_w, preferred_element_type=jnp.float32)
        weight_sel = lax.optimization_barrier(jnp.sum(jnp.where(routes == expert_id, gates.astype(jnp.float32), 0.0), axis=-1))
        return (total + weight_sel[:, None] * expert_out, None)
    mixture, _ = lax.scan(expert_step, jnp.zeros((SLOTS, D), jnp.float32), (w_gate, w_up, w_down, jnp.arange(EXPERTS, dtype=jnp.int32)))
    return (hidden + mixture).astype(jnp.bfloat16)
```

```python
import functools

import jax
import jax.numpy as jnp
from jax import lax
from jax.experimental import pallas as pl
from jax.experimental.pallas import tpu as pltpu
from jax.sharding import PartitionSpec as P

HD = 128
LANES = 128
NORM_EPS = 1e-06
F32 = jnp.float32
BF16 = jnp.bfloat16


def split3(value):
    high = lax.reduce_precision(value, 8, 7)
    rest = value - high
    middle = lax.reduce_precision(rest, 8, 7)
    return high, middle, rest - middle


def xor_exchange(blocks, axis, count):
    moved = list(blocks)
    for step in range(count - 1, 0, -1):
        moved[step] = lax.ppermute(blocks[step], axis, [(j, j ^ step) for j in range(count)])
    return moved


def spec(space=pltpu.VMEM):
    return pl.BlockSpec(memory_space=space)


def call(kernel, outs, ins, scratch=(), limit=None, flops=0, moved=0):
    many = isinstance(outs, (list, tuple))
    return pl.pallas_call(
        kernel,
        out_shape=outs,
        in_specs=ins,
        out_specs=[spec()] * len(outs) if many else spec(),
        scratch_shapes=list(scratch),
        compiler_params=pltpu.CompilerParams(vmem_limit_bytes=limit),
        cost_estimate=pl.CostEstimate(flops=flops, bytes_accessed=moved, transcendentals=0),
    )


def attend(q_row, fresh_row, keys_values, length, q_scr, put, kv_heads):
    heads = q_row.shape[1] // HD
    group = heads // kv_heads
    for h in range(heads):
        q_scr[h : h + 1, :] = q_row[:, h * HD : (h + 1) * HD].astype(F32)
    width = kv_heads * HD
    context = keys_values.shape[0]
    for g in range(kv_heads):
        q = q_scr[g * group : (g + 1) * group, :]
        keys = keys_values[:, g * HD : (g + 1) * HD]
        values = keys_values[:, width + g * HD : width + (g + 1) * HD]
        scores = (
            lax.dot_general(
                q.astype(BF16), keys, (((1,), (1,)), ((), ())), preferred_element_type=F32
            )
            * HD ** (-0.5)
        )
        valid = lax.broadcasted_iota(jnp.int32, (group, context), 1) < length
        scores = jnp.where(valid, scores, -1e30)
        top_cache = jnp.max(scores, axis=-1, keepdims=True)
        weights = jnp.where(valid, jnp.exp(scores - top_cache), 0.0)
        total = jnp.sum(weights, axis=-1, keepdims=True)
        mixed = jnp.dot(weights.astype(BF16), values, preferred_element_type=F32)
        own_key = fresh_row[:, g * HD : (g + 1) * HD].astype(F32)
        own_value = fresh_row[:, width + g * HD : width + (g + 1) * HD].astype(F32)
        own = jnp.sum(q * own_key, axis=-1, keepdims=True) * HD ** (-0.5)
        top = jnp.maximum(top_cache, own)
        cache_factor = jnp.exp(top_cache - top)
        own_factor = jnp.exp(own - top)
        done = (cache_factor * mixed + own_factor * own_value) / (
            cache_factor * total + own_factor
        )
        for j in range(group):
            put(g * group + j, done[j : j + 1, :])


def local_kernel(n_ex, kv_heads, len_ref, q_ref, fresh_ref, cache_ref, att_ref, kv0_ref, kv, q_scr, sems):
    _, tokens, part = att_ref.shape
    copies = [
        pltpu.make_async_copy(
            cache_ref.at[t], kv0_ref if t == 0 else kv.at[t - 1], sems.at[t]
        )
        for t in range(tokens)
    ]
    for t in range(1, tokens):
        copies[t].start()
    copies[0].start()
    per = part // HD
    for t in range(1, tokens):
        copies[t].wait()

        def put(head, row, t=t):
            att_ref[head // per, t : t + 1, (head % per) * HD : (head % per + 1) * HD] = row

        attend(
            q_ref[t : t + 1, :], fresh_ref[t : t + 1, :], kv[t - 1], len_ref[t],
            q_scr.at[t], put, kv_heads,
        )
    for s in range(n_ex):
        att_ref[s, 0:1, :] = jnp.zeros((1, part), F32)
    copies[0].wait()


def moved_kernel(n_dp, n_ex, kv_heads, width, *refs):
    len_ref, moves_ref = refs[:2]
    rows = refs[2 : 2 + n_dp]
    att_ref, kv0_ref, res_ref, ext_ref = refs[2 + n_dp : 6 + n_dp]
    outs = refs[6 + n_dp : 6 + n_dp + n_ex]
    base_ref, ext_out, row_scr, q_scr, full = refs[6 + n_dp + n_ex :]
    dp = lax.axis_index("dp")
    ex = lax.axis_index("expert")
    rel = moves_ref[ex, dp] ^ dp
    row = rows[0][...]
    for r in range(1, n_dp):
        row = jnp.where(rel == r, rows[r][...], row)
    row_scr[...] = row.astype(F32)
    model = res_ref.shape[1]
    full[...] = att_ref[...]
    part = full.shape[2]
    per = part // HD

    def put(head, value):
        full[head // per, 0:1, (head % per) * HD : (head % per + 1) * HD] = value

    fresh_at = q_len = model
    attend(
        row_scr[:, :q_len], row_scr[:, fresh_at : fresh_at + width], kv0_ref[...],
        len_ref[0], q_scr, put, kv_heads,
    )
    for s in range(n_ex):
        outs[s][...] = full[s ^ ex].astype(BF16)
    first = lax.broadcasted_iota(jnp.int32, (res_ref.shape[0], 1), 0) == 0
    base_ref[...] = jnp.where(first, row_scr[:, model + width : 2 * model + width], res_ref[...].astype(F32))
    ext_out[...] = jnp.where(first, row_scr[:, 2 * model + width :], ext_ref[...].astype(F32))


def project_kernel(n_ex, *refs):
    blocks, w_ref, outs, lhs = refs[:n_ex], refs[n_ex], refs[n_ex + 1 : 2 * n_ex + 1], refs[-1]
    tokens = blocks[0].shape[0]
    for s in range(n_ex):
        lhs[s * tokens : (s + 1) * tokens, :] = blocks[s][...].astype(F32)
    left = lhs[...].astype(BF16)
    model = w_ref.shape[1]
    chunk = min(1024, model)
    for at in range(0, model, chunk):
        out = jnp.dot(left, w_ref[:, at : at + chunk], preferred_element_type=F32)
        for s in range(n_ex):
            outs[s][:, at : at + chunk] = out[s * tokens : (s + 1) * tokens, :].astype(outs[s].dtype)


def norm_kernel(n_ex, n_dp, *refs):
    parts, base_ref, ext_ref, gain_ref = refs[:n_ex], *refs[n_ex : n_ex + 3]
    hid_ref, pay_ref = refs[n_ex + 3 :]
    hidden = base_ref[...]
    for s in range(n_ex):
        hidden = hidden + parts[s][...].astype(F32)
    hid_ref[...] = hidden
    model = hidden.shape[1]
    mean = jnp.mean(hidden * hidden, axis=-1, keepdims=True) + NORM_EPS
    normed = hidden * lax.rsqrt(mean) * gain_ref[...]
    pay_ref[:, :model] = normed.astype(BF16)
    ext = ext_ref[...]
    root = jnp.sqrt(mean)
    high = root.astype(BF16).astype(F32)
    middle = (root - high).astype(BF16).astype(F32)
    low = root - high - middle
    lane = lax.broadcasted_iota(jnp.int32, ext.shape, 1)
    at = 3 * n_dp
    ext = jnp.where(lane == at, high, ext)
    ext = jnp.where(lane == at + 1, middle, ext)
    ext = jnp.where(lane == at + 2, low, ext)
    pay_ref[:, model:] = ext.astype(BF16)


def expert_kernel(n_dp, n_ex, tokens, *refs):
    moves_ref = refs[0]
    pieces = refs[1 : 1 + n_dp]
    gate_ref, up_ref, down_ref, gain_ref, hid_ref = refs[1 + n_dp : 6 + n_dp]
    outs = refs[6 + n_dp : 6 + 2 * n_dp]
    real_ref, lhs, act_scr, new_scr = refs[6 + 2 * n_dp :]
    dp = lax.axis_index("dp")
    ex = lax.axis_index("expert")
    model = gain_ref.shape[1]
    rows = n_ex * tokens
    coef = []
    source = 0
    for d in range(n_dp):
        source = jnp.where(moves_ref[ex, d] == dp, d, source)
    rel = source ^ dp
    carried = jnp.zeros((1, pieces[0].shape[1]), F32)
    for r in range(n_dp):
        lhs[r * rows : (r + 1) * rows, :] = pieces[r][:, :model]
        ext = pieces[r][:, model:].astype(F32)
        lane = lax.broadcasted_iota(jnp.int32, ext.shape, 1)
        mine = (lane == dp) | (lane == dp + n_dp) | (lane == dp + 2 * n_dp)
        coef.append(jnp.sum(jnp.where(mine, ext, 0.0), axis=-1, keepdims=True))
        carried = jnp.where(rel == r, pieces[r][0:tokens, :].astype(F32)[0:1, :], carried)
    tail = carried[:, model:]
    lane = lax.broadcasted_iota(jnp.int32, tail.shape, 1)
    root = jnp.sum(
        jnp.where((lane >= 3 * n_dp) & (lane < 3 * n_dp + 3), tail, 0.0), axis=-1, keepdims=True
    )
    first = lax.broadcasted_iota(jnp.int32, (tokens, 1), 0) == 0
    real_ref[...] = jnp.where(first, carried[:, :model] * root / gain_ref[...], hid_ref[...])
    x = lhs[...]
    gate = jnp.dot(x, gate_ref[0], preferred_element_type=F32)
    up = jnp.dot(x, up_ref[0], preferred_element_type=F32)
    act = gate / (1.0 + jnp.exp(-gate)) * up
    for r in range(n_dp):
        act_scr[r * rows : (r + 1) * rows, :] = coef[r] * act[r * rows : (r + 1) * rows, :]
    new_scr[...] = act_scr[...]
    for r in range(n_dp):
        for s in range(n_ex):
            to = ((moves_ref[ex ^ s, dp ^ r] ^ dp) * n_ex + s) * tokens
            at = (r * n_ex + s) * tokens
            new_scr[pl.ds(to, 1), :] = act_scr[at : at + 1, :]
    left = new_scr[...].astype(BF16)
    chunk = min(1024, model)
    for at in range(0, model, chunk):
        out = jnp.dot(left, down_ref[0, :, at : at + chunk], preferred_element_type=F32)
        for r in range(n_dp):
            outs[r][:, at : at + chunk] = out[r * rows : (r + 1) * rows, :].astype(outs[r].dtype)


def per_device(
    query, fresh_kv, cache, lengths, moves, residual, out_weight, norm_gain,
    w_gate, w_up, w_down, routes, gates,
):
    n_dp = lax.axis_size("dp")
    n_ex = lax.axis_size("expert")
    tokens, model = query.shape
    width = fresh_kv.shape[1] // 2
    kv_heads = width // HD
    part = out_weight.shape[0]
    context = cache.shape[1]
    shape = jax.ShapeDtypeStruct

    experts = jnp.arange(n_dp, dtype=jnp.int32)
    share = jnp.sum(
        jnp.where(routes[:, :, None] == experts[None, None, :], gates[:, :, None], 0.0), axis=1
    )
    ext = jnp.concatenate(split3(share), axis=1)
    ext_width = -(-(3 * n_dp + 3) // LANES) * LANES
    ext = jnp.pad(ext, ((0, 0), (0, ext_width - 3 * n_dp))).astype(BF16)
    row = jnp.concatenate([query[:1], fresh_kv[:1], residual[:1], ext[:1]], axis=1)
    rows = xor_exchange([row] * n_dp, "dp", n_dp)

    att, kv0 = call(
        functools.partial(local_kernel, n_ex, kv_heads),
        [shape((n_ex, tokens, part), F32), shape(cache.shape[1:], BF16)],
        [spec(pltpu.SMEM), spec(), spec(), spec(pl.ANY)],
        scratch=[
            pltpu.VMEM((tokens - 1,) + cache.shape[1:], BF16),
            pltpu.VMEM((tokens, model // HD, HD), F32),
            pltpu.SemaphoreType.DMA((tokens,)),
        ],
        limit=8 << 20,
        flops=4 * tokens * model * context,
        moved=cache.size * 2,
    )(lengths, query, fresh_kv, cache)

    moved = call(
        functools.partial(moved_kernel, n_dp, n_ex, kv_heads, 2 * width),
        [shape((tokens, part), BF16)] * n_ex
        + [shape((tokens, model), F32), shape((tokens, ext_width), F32)],
        [spec(pltpu.SMEM), spec(pltpu.SMEM)] + [spec()] * (n_dp + 4),
        scratch=[
            pltpu.VMEM(row.shape, F32),
            pltpu.VMEM((model // HD, HD), F32),
            pltpu.VMEM((n_ex, tokens, part), F32),
        ],
        limit=6 << 20,
        flops=4 * model * context,
        moved=cache.size // tokens * 2,
    )(lengths, moves, *rows, att, kv0, residual, ext)
    blocks = xor_exchange(moved[:n_ex], "expert", n_ex)
    base, ext_all = moved[n_ex:]

    partials = call(
        functools.partial(project_kernel, n_ex),
        [shape((tokens, model), F32)] + [shape((tokens, model), BF16)] * (n_ex - 1),
        [spec()] * (n_ex + 1),
        scratch=[pltpu.VMEM((n_ex * tokens, part), F32)],
        limit=16 << 20,
        flops=2 * n_ex * tokens * part * model,
        moved=out_weight.size * 2,
    )(*blocks, out_weight)
    partials = xor_exchange(partials, "expert", n_ex)

    hidden, payload = call(
        functools.partial(norm_kernel, n_ex, n_dp),
        [shape((tokens, model), F32), shape((tokens, model + ext_width), BF16)],
        [spec()] * (n_ex + 3),
        limit=4 << 20,
        flops=10 * tokens * model,
        moved=tokens * model * 16,
    )(*partials, base, ext_all, norm_gain[None])
    gathered = xor_exchange([payload] * n_ex, "expert", n_ex)
    pieces = {0: jnp.concatenate(gathered, axis=0)}
    bits = [1 << b for b in range(n_dp.bit_length() - 1)]
    for bit in reversed(bits):
        for r in list(pieces):
            pieces[r | bit] = lax.ppermute(
                pieces[r], "dp", [(j, j ^ bit) for j in range(n_dp)]
            )

    group_rows = n_ex * tokens
    all_rows = n_dp * group_rows
    hidden_units = w_down.shape[1]
    weights_bytes = (w_gate.size + w_up.size + w_down.size) * 2
    done = call(
        functools.partial(expert_kernel, n_dp, n_ex, tokens),
        [shape((group_rows, model), BF16)] * n_dp + [shape((tokens, model), F32)],
        [spec(pltpu.SMEM)] + [spec()] * (n_dp + 5),
        scratch=[
            pltpu.VMEM((all_rows, model), BF16),
            pltpu.VMEM((all_rows, hidden_units), F32),
            pltpu.VMEM((all_rows, hidden_units), F32),
        ],
        limit=weights_bytes + (6 << 20) + all_rows * model * 8,
        flops=6 * all_rows * model * hidden_units,
        moved=weights_bytes,
    )(moves, *[pieces[r] for r in range(n_dp)], w_gate, w_up, w_down, norm_gain[None], hidden)
    sums = {r: done[r] for r in range(n_dp)}
    real = done[n_dp]
    for bit in bits:
        for r in sorted((r for r in sums if r & bit), reverse=True):
            got = lax.ppermute(sums.pop(r), "dp", [(j, j ^ bit) for j in range(n_dp)])
            total = sums[r ^ bit].astype(F32) + got.astype(F32)
            sums[r ^ bit] = total.astype(BF16) if r ^ bit else total
    mixed = sums[0].reshape(n_ex, tokens, model)
    back = xor_exchange(
        [mixed[0]] + [mixed[s].astype(BF16) for s in range(1, n_ex)], "expert", n_ex
    )
    total = real
    for s in range(n_ex):
        total = total + back[s].astype(F32)
    return total.astype(BF16)


def solution(mesh):
    placed = (
        P(("groups", "dp", "expert"), None),
        P(("groups", "dp", "expert"), None),
        P(("groups", "dp", "expert"), None, None),
        P(("groups", "dp", "expert")),
        P("groups", None),
        P(("groups", "dp", "expert"), None),
        P("expert", None),
        P(),
        P("dp", None, "expert"),
        P("dp", None, "expert"),
        P("dp", "expert", None),
        P(("groups", "dp", "expert"), None),
        P(("groups", "dp", "expert"), None),
    )
    return jax.shard_map(
        per_device,
        mesh=mesh,
        in_specs=placed,
        out_specs=P(("groups", "dp", "expert"), None),
        check_vma=False,
    )
```

```python
import functools

import jax
import jax.numpy as jnp
from jax import lax
from jax.experimental import pallas as pl
from jax.experimental.pallas import tpu as pltpu
from jax.sharding import PartitionSpec as P


HD = 128
LANES = 128
NORM_EPS = 1e-06
F32 = jnp.float32
BF16 = jnp.bfloat16


def xor_exchange(blocks, axis, count):
    moved = list(blocks)
    for step in range(count - 1, 0, -1):
        moved[step] = lax.ppermute(blocks[step], axis, [(j, j ^ step) for j in range(count)])
    return moved


def spec(space=pltpu.VMEM):
    return pl.BlockSpec(memory_space=space)


def call(kernel, outs, ins, scratch=(), limit=None, flops=0, moved=0):
    many = isinstance(outs, (list, tuple))
    return pl.pallas_call(
        kernel,
        out_shape=outs,
        in_specs=ins,
        out_specs=[spec()] * len(outs) if many else spec(),
        scratch_shapes=list(scratch),
        compiler_params=pltpu.CompilerParams(vmem_limit_bytes=limit),
        cost_estimate=pl.CostEstimate(flops=flops, bytes_accessed=moved, transcendentals=0),
    )


def attend(q_row, fresh_row, keys_values, length, q_scr, put, kv_heads):
    heads = q_row.shape[1] // HD
    group = heads // kv_heads
    for h in range(heads):
        q_scr[h : h + 1, :] = q_row[:, h * HD : (h + 1) * HD].astype(F32)
    width = kv_heads * HD
    context = keys_values.shape[0]
    for g in range(kv_heads):
        q = q_scr[g * group : (g + 1) * group, :]
        keys = keys_values[:, g * HD : (g + 1) * HD]
        values = keys_values[:, width + g * HD : width + (g + 1) * HD]
        scores = (
            lax.dot_general(
                q.astype(BF16), keys, (((1,), (1,)), ((), ())), preferred_element_type=F32
            )
            * HD ** (-0.5)
        )
        if length is not None:
            valid = lax.broadcasted_iota(jnp.int32, (group, context), 1) < length
            scores = jnp.where(valid, scores, -1e30)
        top_cache = jnp.max(scores, axis=-1, keepdims=True)
        weights = jnp.exp(scores - top_cache)
        if length is not None:
            weights = jnp.where(valid, weights, 0.0)
        total = jnp.sum(weights, axis=-1, keepdims=True)
        mixed = jnp.dot(weights.astype(BF16), values, preferred_element_type=F32)
        own_key = fresh_row[:, g * HD : (g + 1) * HD].astype(F32)
        own_value = fresh_row[:, width + g * HD : width + (g + 1) * HD].astype(F32)
        own = jnp.sum(q * own_key, axis=-1, keepdims=True) * HD ** (-0.5)
        top = jnp.maximum(top_cache, own)
        cache_factor = jnp.exp(top_cache - top)
        own_factor = jnp.exp(own - top)
        done = (cache_factor * mixed + own_factor * own_value) / (
            cache_factor * total + own_factor
        )
        for j in range(group):
            put(g * group + j, done[j : j + 1, :])


def entry_kernel(
    n_dp, q_hbm, fresh_hbm, res_hbm, routes_hbm, gates_hbm,
    row_ref, q_ref, fresh_ref, res_ref, ext_ref, routes, gates, sems,
):
    copies = [
        pltpu.make_async_copy(source, to, sems.at[i])
        for i, (source, to) in enumerate(
            [
                (routes_hbm, routes), (gates_hbm, gates), (q_hbm, q_ref),
                (fresh_hbm, fresh_ref), (res_hbm, res_ref),
            ]
        )
    ]
    for copy in copies:
        copy.start()
    copies[0].wait()
    copies[1].wait()
    top, tokens = routes.shape
    lane = lax.broadcasted_iota(jnp.int32, (1, ext_ref.shape[1]), 1)
    turn = jnp.where(lane >= n_dp, 1, 0) + jnp.where(lane >= 2 * n_dp, 1, 0)
    name = lane - n_dp * turn
    for t in range(tokens):
        share = jnp.zeros(lane.shape, F32)
        for k in range(top):
            share = jnp.where(name == routes[k, t], gates[k, t], share)
        high = share.astype(BF16).astype(F32)
        middle = (share - high).astype(BF16).astype(F32)
        low = share - high - middle
        share = jnp.where(turn == 0, high, jnp.where(turn == 1, middle, low))
        ext_ref[t : t + 1, :] = jnp.where(lane < 3 * n_dp, share, 0.0)
    for copy in copies[2:]:
        copy.wait()
    model, width = q_ref.shape[1], fresh_ref.shape[1]
    row_ref[:, :model] = q_ref[0:1, :]
    row_ref[:, model : model + width] = fresh_ref[0:1, :]
    row_ref[:, model + width : 2 * model + width] = res_ref[0:1, :]
    row_ref[:, 2 * model + width :] = ext_ref[0:1, :].astype(BF16)


def local_kernel(
    kv_heads, len_hbm, moves_hbm, q_ref, fresh_ref, cache_hbm, w_hbm,
    att_ref, kv0_ref, rel_ref, w_ref, kv, q_scr, lengths, moves, sems,
):
    parts, tokens, part = att_ref.shape
    copies = [
        pltpu.make_async_copy(
            cache_hbm.at[t], kv0_ref if t == 0 else kv.at[t - 1], sems.at[t]
        )
        for t in range(tokens)
    ]
    lens = pltpu.make_async_copy(len_hbm, lengths, sems.at[tokens])
    goals = pltpu.make_async_copy(moves_hbm, moves, sems.at[tokens + 1])
    weight = pltpu.make_async_copy(w_hbm, w_ref, sems.at[tokens + 2])
    lens.start()
    goals.start()
    for t in list(range(1, tokens)) + [0]:
        copies[t].start()
    weight.start()
    lens.wait()
    per = part // HD
    for t in range(1, tokens):
        copies[t].wait()

        def put(head, row, t=t):
            att_ref[head // per, t : t + 1, (head % per) * HD : (head % per + 1) * HD] = row

        attend(
            q_ref[t : t + 1, :], fresh_ref[t : t + 1, :], kv[t - 1], lengths[t],
            q_scr.at[t], put, kv_heads,
        )
    for s in range(parts):
        att_ref[s, 0:1, :] = jnp.zeros((1, part), F32)
    goals.wait()
    dp = lax.axis_index("dp")
    rel_ref[...] = jnp.full(rel_ref.shape, moves[lax.axis_index("expert"), dp] ^ dp, jnp.int32)
    copies[0].wait()
    weight.wait()


def moved_kernel(n_dp, n_ex, kv_heads, width, *refs):
    rel_ref = refs[0]
    rows = refs[1 : 1 + n_dp]
    att_ref, kv0_ref, res_ref, ext_ref = refs[1 + n_dp : 5 + n_dp]
    outs = refs[5 + n_dp : 5 + n_dp + n_ex]
    base_ref, ext_out, row_scr, q_scr, full = refs[5 + n_dp + n_ex :]
    ex = lax.axis_index("expert")
    rel = rel_ref[0:1, 0:1]
    row = rows[0][...].astype(F32)
    for r in range(1, n_dp):
        row = jnp.where(rel == r, rows[r][...].astype(F32), row)
    row_scr[...] = row
    model = res_ref.shape[1]
    full[...] = att_ref[...]
    part = full.shape[2]
    per = part // HD

    def put(head, value):
        full[head // per, 0:1, (head % per) * HD : (head % per + 1) * HD] = value

    attend(
        row_scr[:, :model], row_scr[:, model : model + width], kv0_ref[...],
        None, q_scr, put, kv_heads,
    )
    for s in range(n_ex):
        outs[s][...] = full[s ^ ex].astype(BF16)
    first = lax.broadcasted_iota(jnp.int32, (res_ref.shape[0], 1), 0) == 0
    base_ref[...] = jnp.where(first, row_scr[:, model + width : 2 * model + width], res_ref[...].astype(F32))
    ext_out[...] = jnp.where(first, row_scr[:, 2 * model + width :], ext_ref[...])


def project_kernel(n_ex, *refs):
    blocks, w_ref, down_hbm = refs[:n_ex], refs[n_ex], refs[n_ex + 1]
    outs, down_ref, lhs, sem = refs[n_ex + 2 : 2 * n_ex + 2], *refs[2 * n_ex + 2 :]
    down = pltpu.make_async_copy(down_hbm, down_ref, sem)
    down.start()
    tokens = blocks[0].shape[0]
    for s in range(n_ex):
        lhs[s * tokens : (s + 1) * tokens, :] = blocks[s][...].astype(F32)
    left = lhs[...].astype(BF16)
    model = w_ref.shape[1]
    chunk = min(1024, model)
    for at in range(0, model, chunk):
        out = jnp.dot(left, w_ref[:, at : at + chunk], preferred_element_type=F32)
        for s in range(n_ex):
            outs[s][:, at : at + chunk] = out[s * tokens : (s + 1) * tokens, :].astype(outs[s].dtype)
    down.wait()


def norm_kernel(n_ex, n_dp, *refs):
    parts, base_ref, ext_ref, gain_ref = refs[:n_ex], *refs[n_ex : n_ex + 3]
    hid_ref, pay_ref = refs[n_ex + 3 :]
    hidden = base_ref[...]
    for s in range(n_ex):
        hidden = hidden + parts[s][...].astype(F32)
    hid_ref[...] = hidden
    model = hidden.shape[1]
    mean = jnp.mean(hidden * hidden, axis=-1, keepdims=True) + NORM_EPS
    normed = hidden * lax.rsqrt(mean) * gain_ref[...]
    pay_ref[:, :model] = normed.astype(BF16)
    ext = ext_ref[...]
    root = jnp.sqrt(mean)
    high = root.astype(BF16).astype(F32)
    middle = (root - high).astype(BF16).astype(F32)
    low = root - high - middle
    lane = lax.broadcasted_iota(jnp.int32, ext.shape, 1)
    at = 3 * n_dp
    ext = jnp.where(lane == at, high, ext)
    ext = jnp.where(lane == at + 1, middle, ext)
    ext = jnp.where(lane == at + 2, low, ext)
    pay_ref[:, model:] = ext.astype(BF16)


def expert_kernel(n_dp, n_ex, tokens, *refs):
    moves_ref = refs[0]
    pieces = refs[1 : 1 + n_dp]
    gate_ref, up_ref, down_ref, gain_ref, hid_ref = refs[1 + n_dp : 6 + n_dp]
    outs = refs[6 + n_dp : 6 + 2 * n_dp]
    real_ref, lhs, act_scr, new_scr = refs[6 + 2 * n_dp :]
    dp = lax.axis_index("dp")
    ex = lax.axis_index("expert")
    model = gain_ref.shape[1]
    rows = n_ex * tokens
    coef = []
    source = 0
    for d in range(n_dp):
        source = jnp.where(moves_ref[ex, d] == dp, d, source)
    rel = source ^ dp
    carried = jnp.zeros((1, pieces[0].shape[1]), F32)
    for r in range(n_dp):
        lhs[r * rows : (r + 1) * rows, :] = pieces[r][:, :model]
        ext = pieces[r][:, model:].astype(F32)
        lane = lax.broadcasted_iota(jnp.int32, ext.shape, 1)
        mine = (lane == dp) | (lane == dp + n_dp) | (lane == dp + 2 * n_dp)
        coef.append(jnp.sum(jnp.where(mine, ext, 0.0), axis=-1, keepdims=True))
        carried = jnp.where(rel == r, pieces[r][0:tokens, :].astype(F32)[0:1, :], carried)
    tail = carried[:, model:]
    lane = lax.broadcasted_iota(jnp.int32, tail.shape, 1)
    root = jnp.sum(
        jnp.where((lane >= 3 * n_dp) & (lane < 3 * n_dp + 3), tail, 0.0), axis=-1, keepdims=True
    )
    first = lax.broadcasted_iota(jnp.int32, (tokens, 1), 0) == 0
    real_ref[...] = jnp.where(first, carried[:, :model] * root / gain_ref[...], hid_ref[...])
    x = lhs[...]
    gate = jnp.dot(x, gate_ref[0], preferred_element_type=F32)
    up = jnp.dot(x, up_ref[0], preferred_element_type=F32)
    act = gate / (1.0 + jnp.exp(-gate)) * up
    for r in range(n_dp):
        act_scr[r * rows : (r + 1) * rows, :] = coef[r] * act[r * rows : (r + 1) * rows, :]
    new_scr[...] = act_scr[...]
    for r in range(n_dp):
        for s in range(n_ex):
            to = ((moves_ref[ex ^ s, dp ^ r] ^ dp) * n_ex + s) * tokens
            at = (r * n_ex + s) * tokens
            new_scr[pl.ds(to, 1), :] = act_scr[at : at + 1, :]
    left = new_scr[...].astype(BF16)
    chunk = min(1024, model)
    for at in range(0, model, chunk):
        out = jnp.dot(left, down_ref[0, :, at : at + chunk], preferred_element_type=F32)
        for r in range(n_dp):
            outs[r][:, at : at + chunk] = out[r * rows : (r + 1) * rows, :].astype(outs[r].dtype)


def per_device(
    query, fresh_kv, cache, lengths, moves, residual, out_weight, norm_gain,
    w_gate, w_up, w_down, routes, gates,
):
    n_dp = lax.axis_size("dp")
    n_ex = lax.axis_size("expert")
    tokens, model = query.shape
    width = fresh_kv.shape[1] // 2
    kv_heads = width // HD
    part = out_weight.shape[0]
    context = cache.shape[1]
    shape = jax.ShapeDtypeStruct

    ext_width = -(-(3 * n_dp + 3) // LANES) * LANES
    top_count = routes.shape[1]
    hbm = spec(pltpu.HBM)
    row, q_in, fresh_in, res_in, ext = call(
        functools.partial(entry_kernel, n_dp),
        [
            shape((1, 2 * model + 2 * width + ext_width), BF16),
            shape(query.shape, BF16),
            shape(fresh_kv.shape, BF16),
            shape(residual.shape, BF16),
            shape((tokens, ext_width), F32),
        ],
        [hbm] * 5,
        scratch=[
            pltpu.SMEM((top_count, tokens), jnp.int32),
            pltpu.SMEM((top_count, tokens), F32),
            pltpu.SemaphoreType.DMA((5,)),
        ],
        limit=4 << 20,
        moved=tokens * model * 4,
    )(query, fresh_kv, residual, routes.T, gates.T)
    rows = xor_exchange([row] * n_dp, "dp", n_dp)

    att, kv0, rel, out_w = call(
        functools.partial(local_kernel, kv_heads),
        [
            shape((n_ex, tokens, part), F32),
            shape(cache.shape[1:], BF16),
            shape((8, LANES), jnp.int32),
            shape(out_weight.shape, BF16),
        ],
        [hbm, hbm, spec(), spec(), hbm, hbm],
        scratch=[
            pltpu.VMEM((tokens - 1,) + cache.shape[1:], BF16),
            pltpu.VMEM((tokens, model // HD, HD), F32),
            pltpu.SMEM(lengths.shape, jnp.int32),
            pltpu.SMEM(moves.shape, jnp.int32),
            pltpu.SemaphoreType.DMA((tokens + 3,)),
        ],
        limit=(8 << 20) + out_weight.size * 2,
        flops=4 * tokens * model * context,
        moved=cache.size * 2 + out_weight.size * 2,
    )(lengths, moves, q_in, fresh_in, cache, out_weight)

    moved = call(
        functools.partial(moved_kernel, n_dp, n_ex, kv_heads, 2 * width),
        [shape((tokens, part), BF16)] * n_ex
        + [shape((tokens, model), F32), shape((tokens, ext_width), F32)],
        [spec()] * (n_dp + 5),
        scratch=[
            pltpu.VMEM(row.shape, F32),
            pltpu.VMEM((model // HD, HD), F32),
            pltpu.VMEM((n_ex, tokens, part), F32),
        ],
        limit=6 << 20,
        flops=4 * model * context,
        moved=cache.size // tokens * 2,
    )(rel, *rows, att, kv0, res_in, ext)
    blocks = xor_exchange(moved[:n_ex], "expert", n_ex)
    base, ext_all = moved[n_ex:]

    *partials, down_w = call(
        functools.partial(project_kernel, n_ex),
        [shape((tokens, model), F32)]
        + [shape((tokens, model), BF16)] * (n_ex - 1)
        + [shape(w_down.shape, BF16)],
        [spec()] * (n_ex + 1) + [hbm],
        scratch=[pltpu.VMEM((n_ex * tokens, part), F32), pltpu.SemaphoreType.DMA(())],
        limit=(4 << 20) + (out_weight.size + w_down.size) * 2,
        flops=2 * n_ex * tokens * part * model,
        moved=(out_weight.size + w_down.size) * 2,
    )(*blocks, out_w, w_down)
    partials = xor_exchange(partials, "expert", n_ex)

    hidden, payload = call(
        functools.partial(norm_kernel, n_ex, n_dp),
        [shape((tokens, model), F32), shape((tokens, model + ext_width), BF16)],
        [spec()] * (n_ex + 3),
        limit=4 << 20,
        flops=10 * tokens * model,
        moved=tokens * model * 16,
    )(*partials, base, ext_all, norm_gain[None])
    gathered = xor_exchange([payload] * n_ex, "expert", n_ex)
    pieces = {0: jnp.concatenate(gathered, axis=0)}
    bits = [1 << b for b in range(n_dp.bit_length() - 1)]
    for bit in reversed(bits):
        for r in list(pieces):
            pieces[r | bit] = lax.ppermute(
                pieces[r], "dp", [(j, j ^ bit) for j in range(n_dp)]
            )

    group_rows = n_ex * tokens
    all_rows = n_dp * group_rows
    hidden_units = w_down.shape[1]
    weights_bytes = (w_gate.size + w_up.size + w_down.size) * 2
    done = call(
        functools.partial(expert_kernel, n_dp, n_ex, tokens),
        [shape((group_rows, model), BF16)] * n_dp + [shape((tokens, model), F32)],
        [spec(pltpu.SMEM)] + [spec()] * (n_dp + 5),
        scratch=[
            pltpu.VMEM((all_rows, model), BF16),
            pltpu.VMEM((all_rows, hidden_units), F32),
            pltpu.VMEM((all_rows, hidden_units), F32),
        ],
        limit=weights_bytes + (6 << 20) + all_rows * model * 8,
        flops=6 * all_rows * model * hidden_units,
        moved=weights_bytes,
    )(moves, *[pieces[r] for r in range(n_dp)], w_gate, w_up, down_w, norm_gain[None], hidden)
    sums = {r: done[r] for r in range(n_dp)}
    real = done[n_dp]
    for bit in bits:
        for r in sorted((r for r in sums if r & bit), reverse=True):
            got = lax.ppermute(sums.pop(r), "dp", [(j, j ^ bit) for j in range(n_dp)])
            total = sums[r ^ bit].astype(F32) + got.astype(F32)
            sums[r ^ bit] = total.astype(BF16) if r ^ bit else total
    mixed = sums[0].reshape(n_ex, tokens, model)
    back = xor_exchange(
        [mixed[0]] + [mixed[s].astype(BF16) for s in range(1, n_ex)], "expert", n_ex
    )
    total = real
    for s in range(n_ex):
        total = total + back[s].astype(F32)
    return total.astype(BF16)


def solution(mesh):
    placed = (
        P(("groups", "dp", "expert"), None),
        P(("groups", "dp", "expert"), None),
        P(("groups", "dp", "expert"), None, None),
        P(("groups", "dp", "expert")),
        P("groups", None),
        P(("groups", "dp", "expert"), None),
        P("expert", None),
        P(),
        P("dp", None, "expert"),
        P("dp", None, "expert"),
        P("dp", "expert", None),
        P(("groups", "dp", "expert"), None),
        P(("groups", "dp", "expert"), None),
    )

    return jax.shard_map(
        per_device,
        mesh=mesh,
        in_specs=placed,
        out_specs=P(("groups", "dp", "expert"), None),
        check_vma=False,
    )
```

```python
import functools

import jax
import jax.numpy as jnp
from jax import lax
from jax.experimental import pallas as pl
from jax.experimental.pallas import tpu as pltpu
from jax.sharding import PartitionSpec as P


HD = 128
LANES = 128
NORM_EPS = 1e-06
F32 = jnp.float32
BF16 = jnp.bfloat16


def xor_exchange(blocks, axis, count):
    moved = list(blocks)
    for step in range(count - 1, 0, -1):
        moved[step] = lax.ppermute(blocks[step], axis, [(j, j ^ step) for j in range(count)])
    return moved


def spec(space=pltpu.VMEM):
    return pl.BlockSpec(memory_space=space)


def call(kernel, outs, ins, scratch=(), limit=None, flops=0, moved=0):
    many = isinstance(outs, (list, tuple))
    return pl.pallas_call(
        kernel,
        out_shape=outs,
        in_specs=ins,
        out_specs=[spec()] * len(outs) if many else spec(),
        scratch_shapes=list(scratch),
        compiler_params=pltpu.CompilerParams(vmem_limit_bytes=limit),
        cost_estimate=pl.CostEstimate(flops=flops, bytes_accessed=moved, transcendentals=0),
    )


def attend(q_row, fresh_row, keys_values, length, q_scr, put, kv_heads):
    heads = q_row.shape[1] // HD
    group = heads // kv_heads
    for h in range(heads):
        q_scr[h : h + 1, :] = q_row[:, h * HD : (h + 1) * HD].astype(F32)
    width = kv_heads * HD
    context = keys_values.shape[0]
    for g in range(kv_heads):
        q = q_scr[g * group : (g + 1) * group, :]
        keys = keys_values[:, g * HD : (g + 1) * HD]
        values = keys_values[:, width + g * HD : width + (g + 1) * HD]
        scores = (
            lax.dot_general(
                q.astype(BF16), keys, (((1,), (1,)), ((), ())), preferred_element_type=F32
            )
            * HD ** (-0.5)
        )
        if length is not None:
            valid = lax.broadcasted_iota(jnp.int32, (group, context), 1) < length
            scores = jnp.where(valid, scores, -1e30)
        top_cache = jnp.max(scores, axis=-1, keepdims=True)
        weights = jnp.exp(scores - top_cache)
        if length is not None:
            weights = jnp.where(valid, weights, 0.0)
        total = jnp.sum(weights, axis=-1, keepdims=True)
        mixed = jnp.dot(weights.astype(BF16), values, preferred_element_type=F32)
        own_key = fresh_row[:, g * HD : (g + 1) * HD].astype(F32)
        own_value = fresh_row[:, width + g * HD : width + (g + 1) * HD].astype(F32)
        own = jnp.sum(q * own_key, axis=-1, keepdims=True) * HD ** (-0.5)
        top = jnp.maximum(top_cache, own)
        cache_factor = jnp.exp(top_cache - top)
        own_factor = jnp.exp(own - top)
        done = (cache_factor * mixed + own_factor * own_value) / (
            cache_factor * total + own_factor
        )
        for j in range(group):
            put(g * group + j, done[j : j + 1, :])


def entry_kernel(
    n_dp, q_hbm, fresh_hbm, res_hbm, routes_hbm, gates_hbm, len_hbm, moves_hbm,
    row_ref, q_ref, fresh_ref, res_ref, ext_ref, info_ref, routes, gates, lengths, moves, sems,
):
    copies = [
        pltpu.make_async_copy(source, to, sems.at[i])
        for i, (source, to) in enumerate(
            [
                (routes_hbm, routes), (gates_hbm, gates), (q_hbm, q_ref),
                (fresh_hbm, fresh_ref), (res_hbm, res_ref), (len_hbm, lengths), (moves_hbm, moves),
            ]
        )
    ]
    for copy in copies:
        copy.start()
    copies[0].wait()
    copies[1].wait()
    top, tokens = routes.shape
    lane = lax.broadcasted_iota(jnp.int32, (1, ext_ref.shape[1]), 1)
    turn = jnp.where(lane >= n_dp, 1, 0) + jnp.where(lane >= 2 * n_dp, 1, 0)
    name = lane - n_dp * turn
    for t in range(tokens):
        share = jnp.zeros(lane.shape, F32)
        for k in range(top):
            share = jnp.where(name == routes[k, t], gates[k, t], share)
        high = share.astype(BF16).astype(F32)
        middle = (share - high).astype(BF16).astype(F32)
        low = share - high - middle
        share = jnp.where(turn == 0, high, jnp.where(turn == 1, middle, low))
        ext_ref[t : t + 1, :] = jnp.where(lane < 3 * n_dp, share, 0.0)
    for copy in copies[2:]:
        copy.wait()
    for t in range(tokens):
        info_ref[t : t + 1, :] = jnp.full((1, LANES), lengths[t], jnp.int32)
    dp = lax.axis_index("dp")
    rel = moves[lax.axis_index("expert"), dp] ^ dp
    info_ref[tokens : tokens + 1, :] = jnp.full((1, LANES), rel, jnp.int32)
    model, width = q_ref.shape[1], fresh_ref.shape[1]
    row_ref[:, :model] = q_ref[0:1, :]
    row_ref[:, model : model + width] = fresh_ref[0:1, :]
    row_ref[:, model + width : 2 * model + width] = res_ref[0:1, :]
    row_ref[:, 2 * model + width :] = ext_ref[0:1, :].astype(BF16)


def fetch(source, to, sems, rows_from=0, pieces=4):
    rows = to.shape[0]
    step = rows // pieces
    return [
        pltpu.make_async_copy(
            source.at[pl.ds(rows_from + i * step, step)], to.at[pl.ds(i * step, step)], sems.at[i]
        )
        for i in range(pieces)
    ]


def local_kernel(
    kv_heads, info_ref, q_ref, fresh_ref, cache_hbm, w_hbm,
    att_ref, kv0_ref, w_ref, kv, q_scr, sems, w_sems,
):
    parts, tokens, part = att_ref.shape
    per = part // HD
    copies = [
        pltpu.make_async_copy(cache_hbm.at[t], kv.at[t - 1] if t else kv0_ref, sems.at[t])
        for t in range(tokens)
    ]
    weight = fetch(w_hbm, w_ref, w_sems)
    for copy in copies[1:] + copies[:1] + weight:
        copy.start()
    for t in range(1, tokens):
        copies[t].wait()

        def put(head, row, t=t):
            att_ref[head // per, t : t + 1, (head % per) * HD : (head % per + 1) * HD] = row

        attend(
            q_ref[t : t + 1, :], fresh_ref[t : t + 1, :], kv.at[t - 1],
            info_ref[t : t + 1, 0:1], q_scr.at[t], put, kv_heads,
        )
    for s in range(parts):
        att_ref[s, 0:1, :] = jnp.zeros((1, part), F32)
    for copy in copies[:1] + weight:
        copy.wait()


def fetch_kernel(rows_from, source, to, sems):
    copies = fetch(source, to, sems, rows_from)
    for copy in copies:
        copy.start()
    for copy in copies:
        copy.wait()


def fetched(source, rows, rows_from):
    return call(
        functools.partial(fetch_kernel, rows_from),
        jax.ShapeDtypeStruct((rows,) + source.shape[1:], source.dtype),
        [spec(pltpu.HBM)],
        scratch=[pltpu.SemaphoreType.DMA((4,))],
        limit=1 << 20,
        moved=source.size // source.shape[0] * rows * 4,
    )(in_hbm(source))


def in_hbm(array):
    return pltpu.with_memory_space_constraint(array, pltpu.HBM)


def moved_kernel(n_dp, n_ex, kv_heads, width, *refs):
    info_ref = refs[0]
    rows = refs[1 : 1 + n_dp]
    att_ref, kv0_ref, res_ref, ext_ref = refs[1 + n_dp : 5 + n_dp]
    outs = refs[5 + n_dp : 5 + n_dp + n_ex]
    base_ref, ext_out, row_scr, q_scr, full = refs[5 + n_dp + n_ex :]
    ex = lax.axis_index("expert")
    tokens = res_ref.shape[0]
    rel = info_ref[tokens : tokens + 1, 0:1]
    row = rows[0][...].astype(F32)
    for r in range(1, n_dp):
        row = jnp.where(rel == r, rows[r][...].astype(F32), row)
    row_scr[...] = row
    model = res_ref.shape[1]
    full[...] = att_ref[...]
    part = full.shape[2]
    per = part // HD

    def put(head, value):
        full[head // per, 0:1, (head % per) * HD : (head % per + 1) * HD] = value

    attend(
        row_scr[:, :model], row_scr[:, model : model + width], kv0_ref,
        None, q_scr, put, kv_heads,
    )
    for s in range(n_ex):
        outs[s][...] = full[s ^ ex].astype(BF16)
    first = lax.broadcasted_iota(jnp.int32, (res_ref.shape[0], 1), 0) == 0
    base_ref[...] = jnp.where(first, row_scr[:, model + width : 2 * model + width], res_ref[...].astype(F32))
    ext_out[...] = jnp.where(first, row_scr[:, 2 * model + width :], ext_ref[...])


def project_kernel(n_ex, *refs):
    blocks, w_refs, outs, lhs = refs[:n_ex], refs[n_ex : n_ex + 2], refs[n_ex + 2 : -1], refs[-1]
    tokens = blocks[0].shape[0]
    for s in range(n_ex):
        lhs[s * tokens : (s + 1) * tokens, :] = blocks[s][...].astype(F32)
    left = lhs[...].astype(BF16)
    early, model = w_refs[0].shape
    chunk = min(1024, model)
    for at in range(0, model, chunk):
        out = jnp.dot(
            left[:, :early], w_refs[0][:, at : at + chunk], preferred_element_type=F32
        ) + jnp.dot(left[:, early:], w_refs[1][:, at : at + chunk], preferred_element_type=F32)
        for s in range(n_ex):
            outs[s][:, at : at + chunk] = out[s * tokens : (s + 1) * tokens, :].astype(outs[s].dtype)


def norm_kernel(n_ex, n_dp, *refs):
    parts, base_ref, ext_ref, gain_ref = refs[:n_ex], *refs[n_ex : n_ex + 3]
    hid_ref, pay_ref = refs[n_ex + 3 :]
    hidden = base_ref[...]
    for s in range(n_ex):
        hidden = hidden + parts[s][...].astype(F32)
    hid_ref[...] = hidden
    model = hidden.shape[1]
    mean = jnp.mean(hidden * hidden, axis=-1, keepdims=True) + NORM_EPS
    normed = hidden * lax.rsqrt(mean) * gain_ref[...]
    pay_ref[:, :model] = normed.astype(BF16)
    ext = ext_ref[...]
    root = jnp.sqrt(mean)
    high = root.astype(BF16).astype(F32)
    middle = (root - high).astype(BF16).astype(F32)
    low = root - high - middle
    lane = lax.broadcasted_iota(jnp.int32, ext.shape, 1)
    at = 3 * n_dp
    ext = jnp.where(lane == at, high, ext)
    ext = jnp.where(lane == at + 1, middle, ext)
    ext = jnp.where(lane == at + 2, low, ext)
    pay_ref[:, model:] = ext.astype(BF16)


def expert_kernel(n_dp, n_ex, tokens, *refs):
    moves_ref = refs[0]
    pieces = refs[1 : 1 + n_dp]
    gate_ref, up_ref, down_ref, gain_ref, hid_ref = refs[1 + n_dp : 6 + n_dp]
    outs = refs[6 + n_dp : 6 + 2 * n_dp]
    real_ref, lhs, act_scr, new_scr = refs[6 + 2 * n_dp :]
    dp = lax.axis_index("dp")
    ex = lax.axis_index("expert")
    model = gain_ref.shape[1]
    rows = n_ex * tokens
    coef = []
    source = 0
    for d in range(n_dp):
        source = jnp.where(moves_ref[ex, d] == dp, d, source)
    rel = source ^ dp
    carried = jnp.zeros((1, pieces[0].shape[1]), F32)
    for r in range(n_dp):
        lhs[r * rows : (r + 1) * rows, :] = pieces[r][:, :model]
        ext = pieces[r][:, model:].astype(F32)
        lane = lax.broadcasted_iota(jnp.int32, ext.shape, 1)
        mine = (lane == dp) | (lane == dp + n_dp) | (lane == dp + 2 * n_dp)
        coef.append(jnp.sum(jnp.where(mine, ext, 0.0), axis=-1, keepdims=True))
        carried = jnp.where(rel == r, pieces[r][0:tokens, :].astype(F32)[0:1, :], carried)
    tail = carried[:, model:]
    lane = lax.broadcasted_iota(jnp.int32, tail.shape, 1)
    root = jnp.sum(
        jnp.where((lane >= 3 * n_dp) & (lane < 3 * n_dp + 3), tail, 0.0), axis=-1, keepdims=True
    )
    first = lax.broadcasted_iota(jnp.int32, (tokens, 1), 0) == 0
    real_ref[...] = jnp.where(first, carried[:, :model] * root / gain_ref[...], hid_ref[...])
    x = lhs[...]
    gate = jnp.dot(x, gate_ref[0], preferred_element_type=F32)
    up = jnp.dot(x, up_ref[0], preferred_element_type=F32)
    act = gate / (1.0 + jnp.exp(-gate)) * up
    for r in range(n_dp):
        act_scr[r * rows : (r + 1) * rows, :] = coef[r] * act[r * rows : (r + 1) * rows, :]
    new_scr[...] = act_scr[...]
    for r in range(n_dp):
        for s in range(n_ex):
            to = ((moves_ref[ex ^ s, dp ^ r] ^ dp) * n_ex + s) * tokens
            at = (r * n_ex + s) * tokens
            new_scr[pl.ds(to, 1), :] = act_scr[at : at + 1, :]
    left = new_scr[...].astype(BF16)
    chunk = min(1024, model)
    for at in range(0, model, chunk):
        out = jnp.dot(left, down_ref[:, at : at + chunk], preferred_element_type=F32)
        for r in range(n_dp):
            outs[r][:, at : at + chunk] = out[r * rows : (r + 1) * rows, :].astype(outs[r].dtype)


def per_device(
    query, fresh_kv, cache, lengths, moves, residual, out_weight, norm_gain,
    w_gate, w_up, w_down, routes, gates,
):
    n_dp = lax.axis_size("dp")
    n_ex = lax.axis_size("expert")
    tokens, model = query.shape
    width = fresh_kv.shape[1] // 2
    kv_heads = width // HD
    part = out_weight.shape[0]
    context = cache.shape[1]
    shape = jax.ShapeDtypeStruct

    ext_width = -(-(3 * n_dp + 3) // LANES) * LANES
    top_count = routes.shape[1]
    small = (query, fresh_kv, residual, routes.T, gates.T, lengths, moves)
    row, q_in, fresh_in, res_in, ext, info = call(
        functools.partial(entry_kernel, n_dp),
        [
            shape((1, 2 * model + 2 * width + ext_width), BF16),
            shape(query.shape, BF16),
            shape(fresh_kv.shape, BF16),
            shape(residual.shape, BF16),
            shape((tokens, ext_width), F32),
            shape((2 * tokens, LANES), jnp.int32),
        ],
        [spec(pltpu.HBM)] * len(small),
        scratch=[
            pltpu.SMEM((top_count, tokens), jnp.int32),
            pltpu.SMEM((top_count, tokens), F32),
            pltpu.SMEM(lengths.shape, jnp.int32),
            pltpu.SMEM(moves.shape, jnp.int32),
            pltpu.SemaphoreType.DMA((len(small),)),
        ],
        limit=4 << 20,
        moved=tokens * model * 4,
    )(*map(in_hbm, small))
    rows = xor_exchange([row] * n_dp, "dp", n_dp)

    early = part // 2
    att, kv0, out_early = call(
        functools.partial(local_kernel, kv_heads),
        [
            shape((n_ex, tokens, part), F32),
            shape(cache.shape[1:], BF16),
            shape((early, model), BF16),
        ],
        [spec()] * 3 + [spec(pltpu.HBM)] * 2,
        scratch=[
            pltpu.VMEM((tokens - 1,) + cache.shape[1:], BF16),
            pltpu.VMEM((tokens, model // HD, HD), F32),
            pltpu.SemaphoreType.DMA((tokens,)),
            pltpu.SemaphoreType.DMA((4,)),
        ],
        limit=6 << 20,
        flops=4 * tokens * model * context,
        moved=cache.size * 2 + early * model * 2,
    )(info, q_in, fresh_in, in_hbm(cache), in_hbm(out_weight))

    moved = call(
        functools.partial(moved_kernel, n_dp, n_ex, kv_heads, 2 * width),
        [shape((tokens, part), BF16)] * n_ex
        + [shape((tokens, model), F32), shape((tokens, ext_width), F32)],
        [spec()] * (n_dp + 5),
        scratch=[
            pltpu.VMEM(row.shape, F32),
            pltpu.VMEM((model // HD, HD), F32),
            pltpu.VMEM((n_ex, tokens, part), F32),
        ],
        limit=6 << 20,
        flops=4 * model * context,
        moved=cache.size // tokens * 2,
    )(info, *rows, att, kv0, res_in, ext)
    blocks = xor_exchange(moved[:n_ex], "expert", n_ex)
    base, ext_all = moved[n_ex:]

    out_late = fetched(out_weight, part - early, early)
    partials = call(
        functools.partial(project_kernel, n_ex),
        [shape((tokens, model), F32)] + [shape((tokens, model), BF16)] * (n_ex - 1),
        [spec()] * (n_ex + 2),
        scratch=[pltpu.VMEM((n_ex * tokens, part), F32)],
        limit=4 << 20,
        flops=2 * n_ex * tokens * part * model,
        moved=out_weight.size * 2,
    )(*blocks, out_early, out_late)
    partials = xor_exchange(partials, "expert", n_ex)

    down = fetched(w_down[0], w_down.shape[1], 0)

    hidden, payload = call(
        functools.partial(norm_kernel, n_ex, n_dp),
        [shape((tokens, model), F32), shape((tokens, model + ext_width), BF16)],
        [spec()] * (n_ex + 3),
        limit=4 << 20,
        flops=10 * tokens * model,
        moved=tokens * model * 16,
    )(*partials, base, ext_all, norm_gain[None])
    gathered = xor_exchange([payload] * n_ex, "expert", n_ex)
    pieces = {0: jnp.concatenate(gathered, axis=0)}
    bits = [1 << b for b in range(n_dp.bit_length() - 1)]
    for bit in reversed(bits):
        for r in list(pieces):
            pieces[r | bit] = lax.ppermute(
                pieces[r], "dp", [(j, j ^ bit) for j in range(n_dp)]
            )

    group_rows = n_ex * tokens
    all_rows = n_dp * group_rows
    hidden_units = w_down.shape[1]
    weights_bytes = (w_gate.size + w_up.size + w_down.size) * 2
    done = call(
        functools.partial(expert_kernel, n_dp, n_ex, tokens),
        [shape((group_rows, model), BF16)] * n_dp + [shape((tokens, model), F32)],
        [spec(pltpu.SMEM)] + [spec()] * (n_dp + 5),
        scratch=[
            pltpu.VMEM((all_rows, model), BF16),
            pltpu.VMEM((all_rows, hidden_units), F32),
            pltpu.VMEM((all_rows, hidden_units), F32),
        ],
        limit=(8 << 20) + all_rows * model * 8,
        flops=6 * all_rows * model * hidden_units,
        moved=weights_bytes,
    )(moves, *[pieces[r] for r in range(n_dp)], w_gate, w_up, down, norm_gain[None], hidden)
    sums = {r: done[r] for r in range(n_dp)}
    real = done[n_dp]
    for bit in bits:
        for r in sorted((r for r in sums if r & bit), reverse=True):
            got = lax.ppermute(sums.pop(r), "dp", [(j, j ^ bit) for j in range(n_dp)])
            total = sums[r ^ bit].astype(F32) + got.astype(F32)
            sums[r ^ bit] = total.astype(BF16) if r ^ bit else total
    mixed = sums[0].reshape(n_ex, tokens, model)
    back = xor_exchange(
        [mixed[0]] + [mixed[s].astype(BF16) for s in range(1, n_ex)], "expert", n_ex
    )
    total = real
    for s in range(n_ex):
        total = total + back[s].astype(F32)
    return total.astype(BF16)


def solution(mesh):
    placed = (
        P(("groups", "dp", "expert"), None),
        P(("groups", "dp", "expert"), None),
        P(("groups", "dp", "expert"), None, None),
        P(("groups", "dp", "expert")),
        P("groups", None),
        P(("groups", "dp", "expert"), None),
        P("expert", None),
        P(),
        P("dp", None, "expert"),
        P("dp", None, "expert"),
        P("dp", "expert", None),
        P(("groups", "dp", "expert"), None),
        P(("groups", "dp", "expert"), None),
    )

    return jax.shard_map(
        per_device,
        mesh=mesh,
        in_specs=placed,
        out_specs=P(("groups", "dp", "expert"), None),
        check_vma=False,
    )
```

```python
import functools

import jax
import jax.numpy as jnp
from jax import lax
from jax.experimental import pallas as pl
from jax.experimental.pallas import tpu as pltpu
from jax.sharding import PartitionSpec as P


HD = 128
LANES = 128
NORM_EPS = 1e-06
F32 = jnp.float32
BF16 = jnp.bfloat16


def xor_exchange(blocks, axis, count):
    moved = list(blocks)
    for step in range(count - 1, 0, -1):
        moved[step] = lax.ppermute(blocks[step], axis, [(j, j ^ step) for j in range(count)])
    return moved


def dp_turns(n_dp):
    return [(1 << b) | 1 for b in range(n_dp.bit_length() - 1)]


def crossed_exchange(blocks, n_dp, n_ex):
    moved = list(blocks)
    for step in range(n_ex - 1, 0, -1):
        pairs = [
            (d * n_ex + e, (d ^ 1) * n_ex + (e ^ step)) for d in range(n_dp) for e in range(n_ex)
        ]
        moved[step] = lax.ppermute(blocks[step], ("dp", "expert"), pairs)
    return moved


def spec(space=pltpu.VMEM):
    return pl.BlockSpec(memory_space=space)


def call(kernel, outs, ins, scratch=(), limit=None, flops=0, moved=0):
    many = isinstance(outs, (list, tuple))
    return pl.pallas_call(
        kernel,
        out_shape=outs,
        in_specs=ins,
        out_specs=[spec()] * len(outs) if many else spec(),
        scratch_shapes=list(scratch),
        compiler_params=pltpu.CompilerParams(vmem_limit_bytes=limit),
        cost_estimate=pl.CostEstimate(flops=flops, bytes_accessed=moved, transcendentals=0),
    )


def attend(q_row, fresh_row, keys_values, length, q_scr, put, kv_heads):
    heads = q_row.shape[1] // HD
    group = heads // kv_heads
    for h in range(heads):
        q_scr[h : h + 1, :] = q_row[:, h * HD : (h + 1) * HD].astype(F32)
    width = kv_heads * HD
    context = keys_values.shape[0]
    for g in range(kv_heads):
        q = q_scr[g * group : (g + 1) * group, :]
        keys = keys_values[:, g * HD : (g + 1) * HD]
        values = keys_values[:, width + g * HD : width + (g + 1) * HD]
        scores = (
            lax.dot_general(
                q.astype(BF16), keys, (((1,), (1,)), ((), ())), preferred_element_type=F32
            )
            * HD ** (-0.5)
        )
        if length is not None:
            valid = lax.broadcasted_iota(jnp.int32, (group, context), 1) < length
            scores = jnp.where(valid, scores, -1e30)
        top_cache = jnp.max(scores, axis=-1, keepdims=True)
        weights = jnp.exp(scores - top_cache)
        if length is not None:
            weights = jnp.where(valid, weights, 0.0)
        total = jnp.sum(weights, axis=-1, keepdims=True)
        mixed = jnp.dot(weights.astype(BF16), values, preferred_element_type=F32)
        own_key = fresh_row[:, g * HD : (g + 1) * HD].astype(F32)
        own_value = fresh_row[:, width + g * HD : width + (g + 1) * HD].astype(F32)
        own = jnp.sum(q * own_key, axis=-1, keepdims=True) * HD ** (-0.5)
        top = jnp.maximum(top_cache, own)
        cache_factor = jnp.exp(top_cache - top)
        own_factor = jnp.exp(own - top)
        done = (cache_factor * mixed + own_factor * own_value) / (
            cache_factor * total + own_factor
        )
        for j in range(group):
            put(g * group + j, done[j : j + 1, :])


def entry_kernel(
    n_dp, q_hbm, fresh_hbm, res_hbm, routes_hbm, gates_hbm, len_hbm, moves_hbm,
    row_ref, q_ref, fresh_ref, res_ref, ext_ref, info_ref, routes, gates, lengths, moves, sems,
):
    copies = [
        pltpu.make_async_copy(source, to, sems.at[i])
        for i, (source, to) in enumerate(
            [
                (routes_hbm, routes), (gates_hbm, gates), (q_hbm, q_ref),
                (fresh_hbm, fresh_ref), (res_hbm, res_ref), (len_hbm, lengths), (moves_hbm, moves),
            ]
        )
    ]
    for copy in copies:
        copy.start()
    copies[0].wait()
    copies[1].wait()
    top, tokens = routes.shape
    lane = lax.broadcasted_iota(jnp.int32, (1, ext_ref.shape[1]), 1)
    turn = jnp.where(lane >= n_dp, 1, 0) + jnp.where(lane >= 2 * n_dp, 1, 0)
    name = lane - n_dp * turn
    for t in range(tokens):
        share = jnp.zeros(lane.shape, F32)
        for k in range(top):
            share = jnp.where(name == routes[k, t], gates[k, t], share)
        high = share.astype(BF16).astype(F32)
        middle = (share - high).astype(BF16).astype(F32)
        low = share - high - middle
        share = jnp.where(turn == 0, high, jnp.where(turn == 1, middle, low))
        ext_ref[t : t + 1, :] = jnp.where(lane < 3 * n_dp, share, 0.0)
    for copy in copies[2:]:
        copy.wait()
    for t in range(tokens):
        info_ref[t : t + 1, :] = jnp.full((1, LANES), lengths[t], jnp.int32)
    dp = lax.axis_index("dp")
    rel = moves[lax.axis_index("expert"), dp] ^ dp
    info_ref[tokens : tokens + 1, :] = jnp.full((1, LANES), rel, jnp.int32)
    model, width = q_ref.shape[1], fresh_ref.shape[1]
    row_ref[:, :model] = q_ref[0:1, :]
    row_ref[:, model : model + width] = fresh_ref[0:1, :]
    row_ref[:, model + width : 2 * model + width] = res_ref[0:1, :]
    row_ref[:, 2 * model + width :] = ext_ref[0:1, :].astype(BF16)


def fetch(source, to, sems, rows_from=0, pieces=4):
    rows = to.shape[0]
    step = rows // pieces
    return [
        pltpu.make_async_copy(
            source.at[pl.ds(rows_from + i * step, step)], to.at[pl.ds(i * step, step)], sems.at[i]
        )
        for i in range(pieces)
    ]


def local_kernel(
    kv_heads, info_ref, q_ref, fresh_ref, cache_hbm, w_hbm,
    att_ref, kv0_ref, w_ref, kv, q_scr, sems, w_sems,
):
    parts, tokens, part = att_ref.shape
    per = part // HD
    copies = [
        pltpu.make_async_copy(cache_hbm.at[t], kv.at[t - 1] if t else kv0_ref, sems.at[t])
        for t in range(tokens)
    ]
    weight = fetch(w_hbm, w_ref, w_sems)
    for copy in copies[1:] + copies[:1] + weight:
        copy.start()
    for t in range(1, tokens):
        copies[t].wait()

        def put(head, row, t=t):
            att_ref[head // per, t : t + 1, (head % per) * HD : (head % per + 1) * HD] = row

        attend(
            q_ref[t : t + 1, :], fresh_ref[t : t + 1, :], kv.at[t - 1],
            info_ref[t : t + 1, 0:1], q_scr.at[t], put, kv_heads,
        )
    for s in range(parts):
        att_ref[s, 0:1, :] = jnp.zeros((1, part), F32)
    for copy in copies[:1] + weight:
        copy.wait()


def fetch_kernel(rows_from, source, to, sems):
    copies = fetch(source, to, sems, rows_from)
    for copy in copies:
        copy.start()
    for copy in copies:
        copy.wait()


def fetched(source, rows, rows_from):
    return call(
        functools.partial(fetch_kernel, rows_from),
        jax.ShapeDtypeStruct((rows,) + source.shape[1:], source.dtype),
        [spec(pltpu.HBM)],
        scratch=[pltpu.SemaphoreType.DMA((4,))],
        limit=1 << 20,
        moved=source.size // source.shape[0] * rows * 4,
    )(in_hbm(source))


def in_hbm(array):
    return pltpu.with_memory_space_constraint(array, pltpu.HBM)


def moved_kernel(n_dp, n_ex, kv_heads, width, *refs):
    info_ref = refs[0]
    rows = refs[1 : 1 + n_dp]
    att_ref, kv0_ref, res_ref, ext_ref = refs[1 + n_dp : 5 + n_dp]
    outs = refs[5 + n_dp : 5 + n_dp + n_ex]
    base_ref, ext_out, row_scr, q_scr, full = refs[5 + n_dp + n_ex :]
    ex = lax.axis_index("expert")
    tokens = res_ref.shape[0]
    rel = info_ref[tokens : tokens + 1, 0:1]
    row = rows[0][...].astype(F32)
    for r in range(1, n_dp):
        row = jnp.where(rel == r, rows[r][...].astype(F32), row)
    row_scr[...] = row
    model = res_ref.shape[1]
    full[...] = att_ref[...]
    part = full.shape[2]
    per = part // HD

    def put(head, value):
        full[head // per, 0:1, (head % per) * HD : (head % per + 1) * HD] = value

    attend(
        row_scr[:, :model], row_scr[:, model : model + width], kv0_ref,
        None, q_scr, put, kv_heads,
    )
    for s in range(n_ex):
        outs[s][...] = full[s ^ ex].astype(BF16)
    first = lax.broadcasted_iota(jnp.int32, (res_ref.shape[0], 1), 0) == 0
    base_ref[...] = jnp.where(first, row_scr[:, model + width : 2 * model + width], res_ref[...].astype(F32))
    ext_out[...] = jnp.where(first, row_scr[:, 2 * model + width :], ext_ref[...])


def project_kernel(n_ex, *refs):
    blocks, w_refs, outs, lhs = refs[:n_ex], refs[n_ex : n_ex + 2], refs[n_ex + 2 : -1], refs[-1]
    tokens = blocks[0].shape[0]
    for s in range(n_ex):
        lhs[s * tokens : (s + 1) * tokens, :] = blocks[s][...].astype(F32)
    left = lhs[...].astype(BF16)
    early, model = w_refs[0].shape
    chunk = min(1024, model)
    for at in range(0, model, chunk):
        out = jnp.dot(
            left[:, :early], w_refs[0][:, at : at + chunk], preferred_element_type=F32
        ) + jnp.dot(left[:, early:], w_refs[1][:, at : at + chunk], preferred_element_type=F32)
        for s in range(n_ex):
            outs[s][:, at : at + chunk] = out[s * tokens : (s + 1) * tokens, :].astype(outs[s].dtype)


def norm_kernel(n_ex, n_dp, *refs):
    parts, base_ref, ext_ref, gain_ref = refs[:n_ex], *refs[n_ex : n_ex + 3]
    hid_ref, pay_ref = refs[n_ex + 3 :]
    hidden = base_ref[...]
    for s in range(n_ex):
        hidden = hidden + parts[s][...].astype(F32)
    hid_ref[...] = hidden
    model = hidden.shape[1]
    mean = jnp.mean(hidden * hidden, axis=-1, keepdims=True) + NORM_EPS
    normed = hidden * lax.rsqrt(mean) * gain_ref[...]
    pay_ref[:, :model] = normed.astype(BF16)
    ext = ext_ref[...]
    root = jnp.sqrt(mean)
    high = root.astype(BF16).astype(F32)
    middle = (root - high).astype(BF16).astype(F32)
    low = root - high - middle
    lane = lax.broadcasted_iota(jnp.int32, ext.shape, 1)
    at = 3 * n_dp
    ext = jnp.where(lane == at, high, ext)
    ext = jnp.where(lane == at + 1, middle, ext)
    ext = jnp.where(lane == at + 2, low, ext)
    pay_ref[:, model:] = ext.astype(BF16)


def expert_kernel(n_dp, n_ex, tokens, *refs):
    moves_ref = refs[0]
    pieces = refs[1 : 1 + n_dp]
    gate_ref, up_ref, down_ref, gain_ref, hid_ref = refs[1 + n_dp : 6 + n_dp]
    outs = refs[6 + n_dp : 6 + 2 * n_dp]
    real_ref, lhs, act_scr, new_scr = refs[6 + 2 * n_dp :]
    dp = lax.axis_index("dp")
    ex = lax.axis_index("expert")
    model = gain_ref.shape[1]
    rows = n_ex * tokens
    coef = []
    source = 0
    for d in range(n_dp):
        source = jnp.where(moves_ref[ex, d] == dp, d, source)
    rel = source ^ dp
    carried = jnp.zeros((1, pieces[0].shape[1]), F32)
    for r in range(n_dp):
        lhs[r * rows : (r + 1) * rows, :] = pieces[r][:, :model]
        ext = pieces[r][:, model:].astype(F32)
        lane = lax.broadcasted_iota(jnp.int32, ext.shape, 1)
        mine = (lane == dp) | (lane == dp + n_dp) | (lane == dp + 2 * n_dp)
        coef.append(jnp.sum(jnp.where(mine, ext, 0.0), axis=-1, keepdims=True))
        carried = jnp.where(rel == r, pieces[r][0:tokens, :].astype(F32)[0:1, :], carried)
    tail = carried[:, model:]
    lane = lax.broadcasted_iota(jnp.int32, tail.shape, 1)
    root = jnp.sum(
        jnp.where((lane >= 3 * n_dp) & (lane < 3 * n_dp + 3), tail, 0.0), axis=-1, keepdims=True
    )
    first = lax.broadcasted_iota(jnp.int32, (tokens, 1), 0) == 0
    real_ref[...] = jnp.where(first, carried[:, :model] * root / gain_ref[...], hid_ref[...])
    x = lhs[...]
    gate = jnp.dot(x, gate_ref[0], preferred_element_type=F32)
    up = jnp.dot(x, up_ref[0], preferred_element_type=F32)
    act = gate / (1.0 + jnp.exp(-gate)) * up
    for r in range(n_dp):
        act_scr[r * rows : (r + 1) * rows, :] = coef[r] * act[r * rows : (r + 1) * rows, :]
    new_scr[...] = act_scr[...]
    for r in range(n_dp):
        for s in range(n_ex):
            side = 1 if s else 0
            to = ((moves_ref[ex ^ s, dp ^ r ^ side] ^ dp ^ side) * n_ex + s) * tokens
            at = (r * n_ex + s) * tokens
            new_scr[pl.ds(to, 1), :] = act_scr[at : at + 1, :]
    left = new_scr[...].astype(BF16)
    chunk = min(1024, model)
    for at in range(0, model, chunk):
        out = jnp.dot(left, down_ref[:, at : at + chunk], preferred_element_type=F32)
        for r in range(n_dp):
            outs[r][:, at : at + chunk] = out[r * rows : (r + 1) * rows, :].astype(outs[r].dtype)


def per_device(
    query, fresh_kv, cache, lengths, moves, residual, out_weight, norm_gain,
    w_gate, w_up, w_down, routes, gates,
):
    n_dp = lax.axis_size("dp")
    n_ex = lax.axis_size("expert")
    tokens, model = query.shape
    width = fresh_kv.shape[1] // 2
    kv_heads = width // HD
    part = out_weight.shape[0]
    context = cache.shape[1]
    shape = jax.ShapeDtypeStruct

    ext_width = -(-(3 * n_dp + 3) // LANES) * LANES
    top_count = routes.shape[1]
    small = (query, fresh_kv, residual, routes.T, gates.T, lengths, moves)
    row, q_in, fresh_in, res_in, ext, info = call(
        functools.partial(entry_kernel, n_dp),
        [
            shape((1, 2 * model + 2 * width + ext_width), BF16),
            shape(query.shape, BF16),
            shape(fresh_kv.shape, BF16),
            shape(residual.shape, BF16),
            shape((tokens, ext_width), F32),
            shape((2 * tokens, LANES), jnp.int32),
        ],
        [spec(pltpu.HBM)] * len(small),
        scratch=[
            pltpu.SMEM((top_count, tokens), jnp.int32),
            pltpu.SMEM((top_count, tokens), F32),
            pltpu.SMEM(lengths.shape, jnp.int32),
            pltpu.SMEM(moves.shape, jnp.int32),
            pltpu.SemaphoreType.DMA((len(small),)),
        ],
        limit=4 << 20,
        moved=tokens * model * 4,
    )(*map(in_hbm, small))
    rows = xor_exchange([row] * n_dp, "dp", n_dp)

    early = part // 2
    att, kv0, out_early = call(
        functools.partial(local_kernel, kv_heads),
        [
            shape((n_ex, tokens, part), F32),
            shape(cache.shape[1:], BF16),
            shape((early, model), BF16),
        ],
        [spec()] * 3 + [spec(pltpu.HBM)] * 2,
        scratch=[
            pltpu.VMEM((tokens - 1,) + cache.shape[1:], BF16),
            pltpu.VMEM((tokens, model // HD, HD), F32),
            pltpu.SemaphoreType.DMA((tokens,)),
            pltpu.SemaphoreType.DMA((4,)),
        ],
        limit=6 << 20,
        flops=4 * tokens * model * context,
        moved=cache.size * 2 + early * model * 2,
    )(info, q_in, fresh_in, in_hbm(cache), in_hbm(out_weight))

    moved = call(
        functools.partial(moved_kernel, n_dp, n_ex, kv_heads, 2 * width),
        [shape((tokens, part), BF16)] * n_ex
        + [shape((tokens, model), F32), shape((tokens, ext_width), F32)],
        [spec()] * (n_dp + 5),
        scratch=[
            pltpu.VMEM(row.shape, F32),
            pltpu.VMEM((model // HD, HD), F32),
            pltpu.VMEM((n_ex, tokens, part), F32),
        ],
        limit=6 << 20,
        flops=4 * model * context,
        moved=cache.size // tokens * 2,
    )(info, *rows, att, kv0, res_in, ext)
    blocks = crossed_exchange(moved[:n_ex], n_dp, n_ex)
    base, ext_all = moved[n_ex:]

    out_late = fetched(out_weight, part - early, early)
    partials = call(
        functools.partial(project_kernel, n_ex),
        [shape((tokens, model), F32)] + [shape((tokens, model), BF16)] * (n_ex - 1),
        [spec()] * (n_ex + 2),
        scratch=[pltpu.VMEM((n_ex * tokens, part), F32)],
        limit=4 << 20,
        flops=2 * n_ex * tokens * part * model,
        moved=out_weight.size * 2,
    )(*blocks, out_early, out_late)
    partials = crossed_exchange(partials, n_dp, n_ex)

    down = fetched(w_down[0], w_down.shape[1], 0)

    hidden, payload = call(
        functools.partial(norm_kernel, n_ex, n_dp),
        [shape((tokens, model), F32), shape((tokens, model + ext_width), BF16)],
        [spec()] * (n_ex + 3),
        limit=4 << 20,
        flops=10 * tokens * model,
        moved=tokens * model * 16,
    )(*partials, base, ext_all, norm_gain[None])
    gathered = crossed_exchange([payload] * n_ex, n_dp, n_ex)
    pieces = {0: jnp.concatenate(gathered, axis=0)}
    turns = dp_turns(n_dp)
    for turn in reversed(turns):
        for r in list(pieces):
            pieces[r ^ turn] = lax.ppermute(pieces[r], "dp", [(j, j ^ turn) for j in range(n_dp)])

    group_rows = n_ex * tokens
    all_rows = n_dp * group_rows
    hidden_units = w_down.shape[1]
    weights_bytes = (w_gate.size + w_up.size + w_down.size) * 2
    done = call(
        functools.partial(expert_kernel, n_dp, n_ex, tokens),
        [shape((group_rows, model), BF16)] * n_dp + [shape((tokens, model), F32)],
        [spec(pltpu.SMEM)] + [spec()] * (n_dp + 5),
        scratch=[
            pltpu.VMEM((all_rows, model), BF16),
            pltpu.VMEM((all_rows, hidden_units), F32),
            pltpu.VMEM((all_rows, hidden_units), F32),
        ],
        limit=(8 << 20) + all_rows * model * 8,
        flops=6 * all_rows * model * hidden_units,
        moved=weights_bytes,
    )(moves, *[pieces[r] for r in range(n_dp)], w_gate, w_up, down, norm_gain[None], hidden)
    sums = {r: done[r] for r in range(n_dp)}
    reach = {0: 0}
    for i, turn in enumerate(turns):
        reach |= {r ^ turn: mark | 1 << i for r, mark in reach.items()}
    real = done[n_dp]
    for i, turn in enumerate(turns):
        bit = 1 << i
        far = {r: r ^ turn for r in sums if reach[r] & bit}
        for r in sorted(far, key=lambda r: -reach[r]):
            got = lax.ppermute(sums.pop(r), "dp", [(j, j ^ turn) for j in range(n_dp)])
            total = sums[far[r]].astype(F32) + got.astype(F32)
            sums[far[r]] = total.astype(BF16) if far[r] else total
    mixed = sums[0].reshape(n_ex, tokens, model)
    back = crossed_exchange(
        [mixed[0]] + [mixed[s].astype(BF16) for s in range(1, n_ex)], n_dp, n_ex
    )
    total = real
    for s in range(n_ex):
        total = total + back[s].astype(F32)
    return total.astype(BF16)


def solution(mesh):
    placed = (
        P(("groups", "dp", "expert"), None),
        P(("groups", "dp", "expert"), None),
        P(("groups", "dp", "expert"), None, None),
        P(("groups", "dp", "expert")),
        P("groups", None),
        P(("groups", "dp", "expert"), None),
        P("expert", None),
        P(),
        P("dp", None, "expert"),
        P("dp", None, "expert"),
        P("dp", "expert", None),
        P(("groups", "dp", "expert"), None),
        P(("groups", "dp", "expert"), None),
    )

    return jax.shard_map(
        per_device,
        mesh=mesh,
        in_specs=placed,
        out_specs=P(("groups", "dp", "expert"), None),
        check_vma=False,
    )
```

```python
import functools

import jax
import jax.numpy as jnp
from jax import lax
from jax.experimental import pallas as pl
from jax.experimental.pallas import tpu as pltpu
from jax.sharding import PartitionSpec as P


HD = 128
LANES = 128
NORM_EPS = 1e-06
F32 = jnp.float32
BF16 = jnp.bfloat16


def xor_exchange(blocks, axis, count):
    moved = list(blocks)
    for step in range(count - 1, 0, -1):
        moved[step] = lax.ppermute(blocks[step], axis, [(j, j ^ step) for j in range(count)])
    return moved


def dp_turns(n_dp):
    return [(1 << b) | 1 for b in range(n_dp.bit_length() - 1)]


def crossed_exchange(blocks, n_dp, n_ex):
    moved = list(blocks)
    for step in range(n_ex - 1, 0, -1):
        pairs = [
            (d * n_ex + e, (d ^ 1) * n_ex + (e ^ step)) for d in range(n_dp) for e in range(n_ex)
        ]
        moved[step] = lax.ppermute(blocks[step], ("dp", "expert"), pairs)
    return moved


def spec(space=pltpu.VMEM):
    return pl.BlockSpec(memory_space=space)


def call(kernel, outs, ins, scratch=(), limit=None, flops=0, moved=0):
    many = isinstance(outs, (list, tuple))
    return pl.pallas_call(
        kernel,
        out_shape=outs,
        in_specs=ins,
        out_specs=[spec()] * len(outs) if many else spec(),
        scratch_shapes=list(scratch),
        compiler_params=pltpu.CompilerParams(vmem_limit_bytes=limit),
        cost_estimate=pl.CostEstimate(flops=flops, bytes_accessed=moved, transcendentals=0),
    )


def attend(q_row, fresh_row, keys_values, length, q_scr, put, kv_heads):
    heads = q_row.shape[1] // HD
    group = heads // kv_heads
    for h in range(heads):
        q_scr[h : h + 1, :] = q_row[:, h * HD : (h + 1) * HD].astype(F32)
    width = kv_heads * HD
    context = keys_values.shape[0]
    for g in range(kv_heads):
        q = q_scr[g * group : (g + 1) * group, :]
        keys = keys_values[:, g * HD : (g + 1) * HD]
        values = keys_values[:, width + g * HD : width + (g + 1) * HD]
        scores = (
            lax.dot_general(
                q.astype(BF16), keys, (((1,), (1,)), ((), ())), preferred_element_type=F32
            )
            * HD ** (-0.5)
        )
        if length is not None:
            valid = lax.broadcasted_iota(jnp.int32, (group, context), 1) < length
            scores = jnp.where(valid, scores, -1e30)
        top_cache = jnp.max(scores, axis=-1, keepdims=True)
        weights = jnp.exp(scores - top_cache)
        if length is not None:
            weights = jnp.where(valid, weights, 0.0)
        total = jnp.sum(weights, axis=-1, keepdims=True)
        mixed = jnp.dot(weights.astype(BF16), values, preferred_element_type=F32)
        own_key = fresh_row[:, g * HD : (g + 1) * HD].astype(F32)
        own_value = fresh_row[:, width + g * HD : width + (g + 1) * HD].astype(F32)
        own = jnp.sum(q * own_key, axis=-1, keepdims=True) * HD ** (-0.5)
        top = jnp.maximum(top_cache, own)
        cache_factor = jnp.exp(top_cache - top)
        own_factor = jnp.exp(own - top)
        done = (cache_factor * mixed + own_factor * own_value) / (
            cache_factor * total + own_factor
        )
        for j in range(group):
            put(g * group + j, done[j : j + 1, :])


def entry_kernel(
    n_dp, q_hbm, fresh_hbm, res_hbm, routes_hbm, gates_hbm, len_hbm, moves_hbm,
    row_ref, q_ref, fresh_ref, res_ref, ext_ref, info_ref, routes, gates, lengths, moves, sems,
):
    copies = [
        pltpu.make_async_copy(source, to, sems.at[i])
        for i, (source, to) in enumerate(
            [
                (routes_hbm, routes), (gates_hbm, gates), (q_hbm, q_ref),
                (fresh_hbm, fresh_ref), (res_hbm, res_ref), (len_hbm, lengths), (moves_hbm, moves),
            ]
        )
    ]
    for copy in copies:
        copy.start()
    copies[0].wait()
    copies[1].wait()
    top, tokens = routes.shape
    lane = lax.broadcasted_iota(jnp.int32, (1, ext_ref.shape[1]), 1)
    turn = jnp.where(lane >= n_dp, 1, 0) + jnp.where(lane >= 2 * n_dp, 1, 0)
    name = lane - n_dp * turn
    for t in range(tokens):
        share = jnp.zeros(lane.shape, F32)
        for k in range(top):
            share = jnp.where(name == routes[k, t], gates[k, t], share)
        high = share.astype(BF16).astype(F32)
        middle = (share - high).astype(BF16).astype(F32)
        low = share - high - middle
        share = jnp.where(turn == 0, high, jnp.where(turn == 1, middle, low))
        ext_ref[t : t + 1, :] = jnp.where(lane < 3 * n_dp, share, 0.0)
    for copy in copies[2:]:
        copy.wait()
    for t in range(tokens):
        info_ref[t : t + 1, :] = jnp.full((1, LANES), lengths[t], jnp.int32)
    dp = lax.axis_index("dp")
    rel = moves[lax.axis_index("expert"), dp] ^ dp
    info_ref[tokens : tokens + 1, :] = jnp.full((1, LANES), rel, jnp.int32)
    model, width = q_ref.shape[1], fresh_ref.shape[1]
    row_ref[:, :model] = q_ref[0:1, :]
    row_ref[:, model : model + width] = fresh_ref[0:1, :]
    row_ref[:, model + width : 2 * model + width] = res_ref[0:1, :]
    row_ref[:, 2 * model + width :] = ext_ref[0:1, :].astype(BF16)


def fetch(source, to, sems, rows_from=0, pieces=4):
    rows = to.shape[0]
    step = rows // pieces
    return [
        pltpu.make_async_copy(
            source.at[pl.ds(rows_from + i * step, step)], to.at[pl.ds(i * step, step)], sems.at[i]
        )
        for i in range(pieces)
    ]


def local_kernel(
    n_dp, kv_heads, info_ref, q_ref, fresh_ref, moves_hbm, cache_hbm, w_hbm,
    att_ref, kv0_ref, w_ref, to_ref, kv, q_scr, moves, moves_sem, sems, w_sems,
):
    parts, tokens, part = att_ref.shape
    goals = pltpu.make_async_copy(moves_hbm, moves, moves_sem)
    goals.start()
    per = part // HD
    copies = [
        pltpu.make_async_copy(cache_hbm.at[t], kv.at[t - 1] if t else kv0_ref, sems.at[t])
        for t in range(tokens)
    ]
    weight = fetch(w_hbm, w_ref, w_sems)
    for copy in copies[1:] + copies[:1] + weight:
        copy.start()
    for t in range(1, tokens):
        copies[t].wait()

        def put(head, row, t=t):
            att_ref[head // per, t : t + 1, (head % per) * HD : (head % per + 1) * HD] = row

        attend(
            q_ref[t : t + 1, :], fresh_ref[t : t + 1, :], kv.at[t - 1],
            info_ref[t : t + 1, 0:1], q_scr.at[t], put, kv_heads,
        )
    for s in range(parts):
        att_ref[s, 0:1, :] = jnp.zeros((1, part), F32)
    goals.wait()
    dp = lax.axis_index("dp")
    ex = lax.axis_index("expert")
    for r in range(n_dp):
        for s in range(parts):
            side = 1 if s else 0
            to = ((moves[ex ^ s, dp ^ r ^ side] ^ dp ^ side) * parts + s) * tokens
            at = r * parts + s
            to_ref[at : at + 1, :] = jnp.full((1, LANES), to, jnp.int32)
    source = 0
    for d in range(n_dp):
        source = jnp.where(moves[ex, d] == dp, d, source)
    to_ref[n_dp * parts : n_dp * parts + 1, :] = jnp.full((1, LANES), source ^ dp, jnp.int32)
    for copy in copies[:1] + weight:
        copy.wait()


def fetch_kernel(rows_from, source, to, sems):
    copies = fetch(source, to, sems, rows_from)
    for copy in copies:
        copy.start()
    for copy in copies:
        copy.wait()


def fetched(source, rows, rows_from):
    return call(
        functools.partial(fetch_kernel, rows_from),
        jax.ShapeDtypeStruct((rows,) + source.shape[1:], source.dtype),
        [spec(pltpu.HBM)],
        scratch=[pltpu.SemaphoreType.DMA((4,))],
        limit=1 << 20,
        moved=source.size // source.shape[0] * rows * 4,
    )(in_hbm(source))


def in_hbm(array):
    return pltpu.with_memory_space_constraint(array, pltpu.HBM)


def moved_kernel(n_dp, n_ex, kv_heads, width, *refs):
    info_ref = refs[0]
    rows = refs[1 : 1 + n_dp]
    att_ref, kv0_ref, res_ref, ext_ref = refs[1 + n_dp : 5 + n_dp]
    outs = refs[5 + n_dp : 5 + n_dp + n_ex]
    base_ref, ext_out, row_scr, q_scr, full = refs[5 + n_dp + n_ex :]
    ex = lax.axis_index("expert")
    tokens = res_ref.shape[0]
    rel = info_ref[tokens : tokens + 1, 0:1]
    row = rows[0][...].astype(F32)
    for r in range(1, n_dp):
        row = jnp.where(rel == r, rows[r][...].astype(F32), row)
    row_scr[...] = row
    model = res_ref.shape[1]
    full[...] = att_ref[...]
    part = full.shape[2]
    per = part // HD

    def put(head, value):
        full[head // per, 0:1, (head % per) * HD : (head % per + 1) * HD] = value

    attend(
        row_scr[:, :model], row_scr[:, model : model + width], kv0_ref,
        None, q_scr, put, kv_heads,
    )
    for s in range(n_ex):
        outs[s][...] = full[s ^ ex].astype(BF16)
    first = lax.broadcasted_iota(jnp.int32, (res_ref.shape[0], 1), 0) == 0
    base_ref[...] = jnp.where(first, row_scr[:, model + width : 2 * model + width], res_ref[...].astype(F32))
    ext_out[...] = jnp.where(first, row_scr[:, 2 * model + width :], ext_ref[...])


def project_kernel(n_ex, *refs):
    blocks, w_refs, outs, lhs = refs[:n_ex], refs[n_ex : n_ex + 2], refs[n_ex + 2 : -1], refs[-1]
    tokens = blocks[0].shape[0]
    for s in range(n_ex):
        lhs[s * tokens : (s + 1) * tokens, :] = blocks[s][...].astype(F32)
    left = lhs[...].astype(BF16)
    early, model = w_refs[0].shape
    chunk = min(1024, model)
    for at in range(0, model, chunk):
        out = jnp.dot(
            left[:, :early], w_refs[0][:, at : at + chunk], preferred_element_type=F32
        ) + jnp.dot(left[:, early:], w_refs[1][:, at : at + chunk], preferred_element_type=F32)
        for s in range(n_ex):
            outs[s][:, at : at + chunk] = out[s * tokens : (s + 1) * tokens, :].astype(outs[s].dtype)


def norm_kernel(n_ex, n_dp, *refs):
    parts, base_ref, ext_ref, gain_ref = refs[:n_ex], *refs[n_ex : n_ex + 3]
    hid_ref, pay_ref = refs[n_ex + 3 :]
    hidden = base_ref[...]
    for s in range(n_ex):
        hidden = hidden + parts[s][...].astype(F32)
    hid_ref[...] = hidden
    model = hidden.shape[1]
    mean = jnp.mean(hidden * hidden, axis=-1, keepdims=True) + NORM_EPS
    normed = hidden * lax.rsqrt(mean) * gain_ref[...]
    pay_ref[:, :model] = normed.astype(BF16)
    ext = ext_ref[...]
    root = jnp.sqrt(mean)
    high = root.astype(BF16).astype(F32)
    middle = (root - high).astype(BF16).astype(F32)
    low = root - high - middle
    lane = lax.broadcasted_iota(jnp.int32, ext.shape, 1)
    at = 3 * n_dp
    ext = jnp.where(lane == at, high, ext)
    ext = jnp.where(lane == at + 1, middle, ext)
    ext = jnp.where(lane == at + 2, low, ext)
    pay_ref[:, model:] = ext.astype(BF16)


def expert_kernel(n_dp, n_ex, tokens, *refs):
    to_ref = refs[0]
    pieces = refs[1 : 1 + n_dp]
    gate_ref, up_ref, down_ref, gain_ref, hid_ref = refs[1 + n_dp : 6 + n_dp]
    outs = refs[6 + n_dp : 6 + 2 * n_dp]
    real_ref, lhs, act_scr, new_scr = refs[6 + 2 * n_dp :]
    dp = lax.axis_index("dp")
    model = gain_ref.shape[1]
    rows = n_ex * tokens
    coef = []
    rel = to_ref[n_dp * n_ex : n_dp * n_ex + 1, 0:1]
    carried = jnp.zeros((1, pieces[0].shape[1]), F32)
    for r in range(n_dp):
        lhs[r * rows : (r + 1) * rows, :] = pieces[r][:, :model]
        ext = pieces[r][:, model:].astype(F32)
        lane = lax.broadcasted_iota(jnp.int32, ext.shape, 1)
        mine = (lane == dp) | (lane == dp + n_dp) | (lane == dp + 2 * n_dp)
        coef.append(jnp.sum(jnp.where(mine, ext, 0.0), axis=-1, keepdims=True))
        carried = jnp.where(rel == r, pieces[r][0:tokens, :].astype(F32)[0:1, :], carried)
    tail = carried[:, model:]
    lane = lax.broadcasted_iota(jnp.int32, tail.shape, 1)
    root = jnp.sum(
        jnp.where((lane >= 3 * n_dp) & (lane < 3 * n_dp + 3), tail, 0.0), axis=-1, keepdims=True
    )
    first = lax.broadcasted_iota(jnp.int32, (tokens, 1), 0) == 0
    real_ref[...] = jnp.where(first, carried[:, :model] * root / gain_ref[...], hid_ref[...])
    x = lhs[...]
    gate = jnp.dot(x, gate_ref[0], preferred_element_type=F32)
    up = jnp.dot(x, up_ref[0], preferred_element_type=F32)
    act = gate / (1.0 + jnp.exp(-gate)) * up
    for r in range(n_dp):
        act_scr[r * rows : (r + 1) * rows, :] = coef[r] * act[r * rows : (r + 1) * rows, :]
    new_scr[...] = act_scr[...]
    for r in range(n_dp):
        for s in range(n_ex):
            to = to_ref[r * n_ex + s : r * n_ex + s + 1, 0:1][0, 0]
            at = (r * n_ex + s) * tokens
            new_scr[pl.ds(to, 1), :] = act_scr[at : at + 1, :]
    left = new_scr[...].astype(BF16)
    chunk = min(1024, model)
    for at in range(0, model, chunk):
        out = jnp.dot(left, down_ref[:, at : at + chunk], preferred_element_type=F32)
        for r in range(n_dp):
            for s in range(n_ex):
                first_row = (r * n_ex + s) * tokens
                outs[r][s, :, at : at + chunk] = out[first_row : first_row + tokens, :].astype(BF16)


def per_device(
    query, fresh_kv, cache, lengths, moves, residual, out_weight, norm_gain,
    w_gate, w_up, w_down, routes, gates,
):
    n_dp = lax.axis_size("dp")
    n_ex = lax.axis_size("expert")
    tokens, model = query.shape
    width = fresh_kv.shape[1] // 2
    kv_heads = width // HD
    part = out_weight.shape[0]
    context = cache.shape[1]
    shape = jax.ShapeDtypeStruct

    ext_width = -(-(3 * n_dp + 3) // LANES) * LANES
    top_count = routes.shape[1]
    small = (query, fresh_kv, residual, routes.T, gates.T, lengths, moves)
    row, q_in, fresh_in, res_in, ext, info = call(
        functools.partial(entry_kernel, n_dp),
        [
            shape((1, 2 * model + 2 * width + ext_width), BF16),
            shape(query.shape, BF16),
            shape(fresh_kv.shape, BF16),
            shape(residual.shape, BF16),
            shape((tokens, ext_width), F32),
            shape((2 * tokens, LANES), jnp.int32),
        ],
        [spec(pltpu.HBM)] * len(small),
        scratch=[
            pltpu.SMEM((top_count, tokens), jnp.int32),
            pltpu.SMEM((top_count, tokens), F32),
            pltpu.SMEM(lengths.shape, jnp.int32),
            pltpu.SMEM(moves.shape, jnp.int32),
            pltpu.SemaphoreType.DMA((len(small),)),
        ],
        limit=4 << 20,
        moved=tokens * model * 4,
    )(*map(in_hbm, small))
    rows = xor_exchange([row] * n_dp, "dp", n_dp)

    early = part // 4
    att, kv0, out_early, targets = call(
        functools.partial(local_kernel, n_dp, kv_heads),
        [
            shape((n_ex, tokens, part), F32),
            shape(cache.shape[1:], BF16),
            shape((early, model), BF16),
            shape((n_dp * n_ex + 8, LANES), jnp.int32),
        ],
        [spec()] * 3 + [spec(pltpu.HBM)] * 3,
        scratch=[
            pltpu.VMEM((tokens - 1,) + cache.shape[1:], BF16),
            pltpu.VMEM((tokens, model // HD, HD), F32),
            pltpu.SMEM(moves.shape, jnp.int32),
            pltpu.SemaphoreType.DMA(()),
            pltpu.SemaphoreType.DMA((tokens,)),
            pltpu.SemaphoreType.DMA((4,)),
        ],
        limit=6 << 20,
        flops=4 * tokens * model * context,
        moved=cache.size * 2 + early * model * 2,
    )(info, q_in, fresh_in, in_hbm(moves), in_hbm(cache), in_hbm(out_weight))

    moved = call(
        functools.partial(moved_kernel, n_dp, n_ex, kv_heads, 2 * width),
        [shape((tokens, part), BF16)] * n_ex
        + [shape((tokens, model), F32), shape((tokens, ext_width), F32)],
        [spec()] * (n_dp + 5),
        scratch=[
            pltpu.VMEM(row.shape, F32),
            pltpu.VMEM((model // HD, HD), F32),
            pltpu.VMEM((n_ex, tokens, part), F32),
        ],
        limit=6 << 20,
        flops=4 * model * context,
        moved=cache.size // tokens * 2,
    )(info, *rows, att, kv0, res_in, ext)
    blocks = crossed_exchange(moved[:n_ex], n_dp, n_ex)
    base, ext_all = moved[n_ex:]

    out_late = fetched(out_weight, part - early, early)
    partials = call(
        functools.partial(project_kernel, n_ex),
        [shape((tokens, model), F32)] + [shape((tokens, model), BF16)] * (n_ex - 1),
        [spec()] * (n_ex + 2),
        scratch=[pltpu.VMEM((n_ex * tokens, part), F32)],
        limit=4 << 20,
        flops=2 * n_ex * tokens * part * model,
        moved=out_weight.size * 2,
    )(*blocks, out_early, out_late)
    partials = crossed_exchange(partials, n_dp, n_ex)

    down = fetched(w_down[0], w_down.shape[1], 0)

    hidden, payload = call(
        functools.partial(norm_kernel, n_ex, n_dp),
        [shape((tokens, model), F32), shape((tokens, model + ext_width), BF16)],
        [spec()] * (n_ex + 3),
        limit=4 << 20,
        flops=10 * tokens * model,
        moved=tokens * model * 16,
    )(*partials, base, ext_all, norm_gain[None])
    gathered = crossed_exchange([payload] * n_ex, n_dp, n_ex)
    turns = dp_turns(n_dp)

    def over_dp(array, turn):
        return lax.ppermute(array, "dp", [(j, j ^ turn) for j in range(n_dp)])

    top = turns[-1]
    near = over_dp(payload, top)
    rest = over_dp(jnp.stack(gathered[1:]), top)
    pieces = {
        0: jnp.concatenate(gathered, axis=0),
        top: jnp.concatenate([near] + [rest[s] for s in range(n_ex - 1)], axis=0),
    }
    for turn in reversed(turns[:-1]):
        for r in list(pieces):
            pieces[r ^ turn] = over_dp(pieces[r], turn)

    group_rows = n_ex * tokens
    all_rows = n_dp * group_rows
    hidden_units = w_down.shape[1]
    weights_bytes = (w_gate.size + w_up.size + w_down.size) * 2
    done = call(
        functools.partial(expert_kernel, n_dp, n_ex, tokens),
        [shape((n_ex, tokens, model), BF16)] * n_dp + [shape((tokens, model), F32)],
        [spec()] * (n_dp + 6),
        scratch=[
            pltpu.VMEM((all_rows, model), BF16),
            pltpu.VMEM((all_rows, hidden_units), F32),
            pltpu.VMEM((all_rows, hidden_units), F32),
        ],
        limit=(8 << 20) + all_rows * model * 8,
        flops=6 * all_rows * model * hidden_units,
        moved=weights_bytes,
    )(targets, *[pieces[r] for r in range(n_dp)], w_gate, w_up, down, norm_gain[None], hidden)
    terms = {r: [done[r]] for r in range(n_dp)}
    reach = {0: 0}
    for i, turn in enumerate(turns):
        reach |= {r ^ turn: mark | 1 << i for r, mark in reach.items()}
    real = done[n_dp]

    def added(arrays):
        return functools.reduce(jnp.add, [array.astype(F32) for array in arrays])

    for i, turn in enumerate(turns[:-1]):
        far = {r: r ^ turn for r in terms if reach[r] >> i & 1}
        for r in sorted(far, key=lambda r: -reach[r]):
            whole = terms.pop(r)
            whole = whole[0] if len(whole) == 1 else added(whole).astype(BF16)
            terms[far[r]].append(over_dp(whole, turn))
    rest = over_dp(added([t[1:] for t in terms[top]]).astype(BF16), top)
    near = over_dp(added([t[0] for t in terms[top]]).astype(BF16), top)
    mixed = added([t[1:] for t in terms[0]] + [rest]).astype(BF16)
    staying = added([t[0] for t in terms[0]] + [near])
    back = crossed_exchange([staying] + [mixed[s] for s in range(n_ex - 1)], n_dp, n_ex)
    total = real
    for s in range(n_ex):
        total = total + back[s].astype(F32)
    return total.astype(BF16)


def solution(mesh):
    placed = (
        P(("groups", "dp", "expert"), None),
        P(("groups", "dp", "expert"), None),
        P(("groups", "dp", "expert"), None, None),
        P(("groups", "dp", "expert")),
        P("groups", None),
        P(("groups", "dp", "expert"), None),
        P("expert", None),
        P(),
        P("dp", None, "expert"),
        P("dp", None, "expert"),
        P("dp", "expert", None),
        P(("groups", "dp", "expert"), None),
        P(("groups", "dp", "expert"), None),
    )

    return jax.shard_map(
        per_device,
        mesh=mesh,
        in_specs=placed,
        out_specs=P(("groups", "dp", "expert"), None),
        check_vma=False,
    )
```

```python
import functools

import jax
import jax.numpy as jnp
from jax import lax
from jax.experimental import pallas as pl
from jax.experimental.pallas import tpu as pltpu
from jax.sharding import PartitionSpec as P


HD = 128
LANES = 128
NORM_EPS = 1e-06
F32 = jnp.float32
BF16 = jnp.bfloat16


def xor_exchange(blocks, axis, count):
    moved = list(blocks)
    for step in range(count - 1, 0, -1):
        moved[step] = lax.ppermute(blocks[step], axis, [(j, j ^ step) for j in range(count)])
    return moved


def dp_turns(n_dp):
    return [(1 << b) | 1 for b in range(n_dp.bit_length() - 1)]


def crossed_exchange(blocks, n_dp, n_ex):
    moved = list(blocks)
    for step in range(n_ex - 1, 0, -1):
        pairs = [
            (d * n_ex + e, (d ^ 1) * n_ex + (e ^ step)) for d in range(n_dp) for e in range(n_ex)
        ]
        moved[step] = lax.ppermute(blocks[step], ("dp", "expert"), pairs)
    return moved


def spec(space=pltpu.VMEM):
    return pl.BlockSpec(memory_space=space)


def call(kernel, outs, ins, scratch=(), limit=None, flops=0, moved=0):
    many = isinstance(outs, (list, tuple))
    return pl.pallas_call(
        kernel,
        out_shape=outs,
        in_specs=ins,
        out_specs=[spec()] * len(outs) if many else spec(),
        scratch_shapes=list(scratch),
        compiler_params=pltpu.CompilerParams(vmem_limit_bytes=limit),
        cost_estimate=pl.CostEstimate(flops=flops, bytes_accessed=moved, transcendentals=0),
    )


def attend(jobs, kv_heads):
    chains = []
    for q_row, _, q_scr, _, _, _ in jobs:
        heads = q_row.shape[1] // HD
        for h in range(heads):
            q_scr[h : h + 1, :] = q_row[:, h * HD : (h + 1) * HD].astype(F32)
    for job in jobs:
        q_row, fresh_row, q_scr, _, _, _ = job
        group = q_row.shape[1] // HD // kv_heads
        for g in range(kv_heads):
            q = q_scr[g * group : (g + 1) * group, :]
            own_key = fresh_row[:, g * HD : (g + 1) * HD].astype(F32)
            own = jnp.sum(q * own_key, axis=-1, keepdims=True) * HD ** (-0.5)
            chains.append([job, g, group, q.astype(BF16), own])
    return chains


def attend_cache(chains, kv_heads):
    width = kv_heads * HD
    all_scores = []
    for (_, _, _, cache, _, _), g, _, q, _ in chains:
        keys = cache[:, g * HD : (g + 1) * HD]
        all_scores.append(
            lax.dot_general(q, keys, (((1,), (1,)), ((), ())), preferred_element_type=F32)
            * HD ** (-0.5)
        )
    parts = []
    for scores, ((_, _, _, _, length, _), _, _, _, own) in zip(all_scores, chains):
        if length is not None:
            valid = lax.broadcasted_iota(jnp.int32, scores.shape, 1) < length
            scores = jnp.where(valid, scores, -1e30)
        top_cache = jnp.max(scores, axis=-1, keepdims=True)
        weights = jnp.exp(scores - top_cache)
        if length is not None:
            weights = jnp.where(valid, weights, 0.0)
        total = jnp.sum(weights, axis=-1, keepdims=True)
        top = jnp.maximum(top_cache, own)
        parts.append((weights.astype(BF16), total, jnp.exp(top_cache - top), jnp.exp(own - top)))
    mixes = []
    for (weights, _, _, _), ((_, _, _, cache, _, _), g, _, _, _) in zip(parts, chains):
        values = cache[:, width + g * HD : width + (g + 1) * HD]
        mixes.append(jnp.dot(weights, values, preferred_element_type=F32))
    for mixed, (_, total, cache_factor, own_factor), (job, g, group, _, _) in zip(
        mixes, parts, chains
    ):
        _, fresh_row, _, _, _, put = job
        own_value = fresh_row[:, width + g * HD : width + (g + 1) * HD].astype(F32)
        done = (cache_factor * mixed + own_factor * own_value) / (
            cache_factor * total + own_factor
        )
        for j in range(group):
            put(g * group + j, done[j : j + 1, :])


def entry_kernel(
    n_dp, q_hbm, fresh_hbm, res_hbm, routes_hbm, gates_hbm, len_hbm, moves_hbm,
    row_ref, q_ref, fresh_ref, res_ref, ext_ref, info_ref, routes, gates, lengths, moves, sems,
):
    copies = [
        pltpu.make_async_copy(source, to, sems.at[i])
        for i, (source, to) in enumerate(
            [
                (routes_hbm, routes), (gates_hbm, gates), (q_hbm, q_ref),
                (fresh_hbm, fresh_ref), (res_hbm, res_ref), (len_hbm, lengths), (moves_hbm, moves),
            ]
        )
    ]
    for copy in copies:
        copy.start()
    copies[0].wait()
    copies[1].wait()
    top, tokens = routes.shape
    lane = lax.broadcasted_iota(jnp.int32, (1, ext_ref.shape[1]), 1)
    turn = jnp.where(lane >= n_dp, 1, 0) + jnp.where(lane >= 2 * n_dp, 1, 0)
    name = lane - n_dp * turn
    for t in range(tokens):
        share = jnp.zeros(lane.shape, F32)
        for k in range(top):
            share = jnp.where(name == routes[k, t], gates[k, t], share)
        high = share.astype(BF16).astype(F32)
        middle = (share - high).astype(BF16).astype(F32)
        low = share - high - middle
        share = jnp.where(turn == 0, high, jnp.where(turn == 1, middle, low))
        ext_ref[t : t + 1, :] = jnp.where(lane < 3 * n_dp, share, 0.0)
    for copy in copies[2:]:
        copy.wait()
    for t in range(tokens):
        info_ref[t : t + 1, :] = jnp.full((1, LANES), lengths[t], jnp.int32)
    dp = lax.axis_index("dp")
    rel = moves[lax.axis_index("expert"), dp] ^ dp
    info_ref[tokens : tokens + 1, :] = jnp.full((1, LANES), rel, jnp.int32)
    model, width = q_ref.shape[1], fresh_ref.shape[1]
    row_ref[:, :model] = q_ref[0:1, :]
    row_ref[:, model : model + width] = fresh_ref[0:1, :]
    row_ref[:, model + width : 2 * model + width] = res_ref[0:1, :]
    row_ref[:, 2 * model + width :] = ext_ref[0:1, :].astype(BF16)


def fetch(source, to, sems, rows_from=0, pieces=4):
    rows = to.shape[0]
    step = rows // pieces
    return [
        pltpu.make_async_copy(
            source.at[pl.ds(rows_from + i * step, step)], to.at[pl.ds(i * step, step)], sems.at[i]
        )
        for i in range(pieces)
    ]


def local_kernel(
    n_dp, kv_heads, info_ref, q_ref, fresh_ref, moves_hbm, cache_hbm, w_hbm,
    att_ref, kv0_ref, w_ref, to_ref, kv, q_scr, moves, moves_sem, sems, w_sems,
):
    parts, tokens, part = att_ref.shape
    goals = pltpu.make_async_copy(moves_hbm, moves, moves_sem)
    goals.start()
    per = part // HD
    copies = [
        pltpu.make_async_copy(cache_hbm.at[t], kv.at[t - 1] if t else kv0_ref, sems.at[t])
        for t in range(tokens)
    ]
    weight = fetch(w_hbm, w_ref, w_sems)
    for copy in copies[1:] + copies[:1] + weight:
        copy.start()
    jobs = []
    for t in range(1, tokens):

        def put(head, row, t=t):
            att_ref[head // per, t : t + 1, (head % per) * HD : (head % per + 1) * HD] = row

        jobs.append(
            (
                q_ref[t : t + 1, :], fresh_ref[t : t + 1, :], q_scr.at[t], kv.at[t - 1],
                info_ref[t : t + 1, 0:1], put,
            )
        )
    chains = attend(jobs, kv_heads)
    for copy in copies[1:]:
        copy.wait()
    attend_cache(chains, kv_heads)
    for s in range(parts):
        att_ref[s, 0:1, :] = jnp.zeros((1, part), F32)
    goals.wait()
    dp = lax.axis_index("dp")
    ex = lax.axis_index("expert")
    for r in range(n_dp):
        for s in range(parts):
            side = 1 if s else 0
            to = ((moves[ex ^ s, dp ^ r ^ side] ^ dp ^ side) * parts + s) * tokens
            at = r * parts + s
            to_ref[at : at + 1, :] = jnp.full((1, LANES), to, jnp.int32)
    source = 0
    for d in range(n_dp):
        source = jnp.where(moves[ex, d] == dp, d, source)
    to_ref[n_dp * parts : n_dp * parts + 1, :] = jnp.full((1, LANES), source ^ dp, jnp.int32)
    for copy in copies[:1] + weight:
        copy.wait()


def fetch_kernel(rows_from, source, to, sems):
    copies = fetch(source, to, sems, rows_from)
    for copy in copies:
        copy.start()
    for copy in copies:
        copy.wait()


def fetched(source, rows, rows_from):
    return call(
        functools.partial(fetch_kernel, rows_from),
        jax.ShapeDtypeStruct((rows,) + source.shape[1:], source.dtype),
        [spec(pltpu.HBM)],
        scratch=[pltpu.SemaphoreType.DMA((4,))],
        limit=1 << 20,
        moved=source.size // source.shape[0] * rows * 4,
    )(in_hbm(source))


def in_hbm(array):
    return pltpu.with_memory_space_constraint(array, pltpu.HBM)


def moved_kernel(n_dp, n_ex, kv_heads, width, *refs):
    info_ref = refs[0]
    rows = refs[1 : 1 + n_dp]
    att_ref, kv0_ref, res_ref, ext_ref = refs[1 + n_dp : 5 + n_dp]
    outs = refs[5 + n_dp : 5 + n_dp + n_ex]
    base_ref, ext_out, row_scr, q_scr, full = refs[5 + n_dp + n_ex :]
    ex = lax.axis_index("expert")
    tokens = res_ref.shape[0]
    rel = info_ref[tokens : tokens + 1, 0:1]
    row = rows[0][...].astype(F32)
    for r in range(1, n_dp):
        row = jnp.where(rel == r, rows[r][...].astype(F32), row)
    row_scr[...] = row
    model = res_ref.shape[1]
    full[...] = att_ref[...]
    part = full.shape[2]
    per = part // HD

    def put(head, value):
        full[head // per, 0:1, (head % per) * HD : (head % per + 1) * HD] = value

    job = (row_scr[:, :model], row_scr[:, model : model + width], q_scr, kv0_ref, None, put)
    attend_cache(attend([job], kv_heads), kv_heads)
    for s in range(n_ex):
        outs[s][...] = full[s ^ ex].astype(BF16)
    first = lax.broadcasted_iota(jnp.int32, (res_ref.shape[0], 1), 0) == 0
    base_ref[...] = jnp.where(first, row_scr[:, model + width : 2 * model + width], res_ref[...].astype(F32))
    ext_out[...] = jnp.where(first, row_scr[:, 2 * model + width :], ext_ref[...])


def project_kernel(n_ex, *refs):
    blocks, w_refs, outs, lhs = refs[:n_ex], refs[n_ex : n_ex + 2], refs[n_ex + 2 : -1], refs[-1]
    tokens = blocks[0].shape[0]
    for s in range(n_ex):
        lhs[s * tokens : (s + 1) * tokens, :] = blocks[s][...].astype(F32)
    left = lhs[...].astype(BF16)
    early, model = w_refs[0].shape
    chunk = min(1024, model)
    for at in range(0, model, chunk):
        out = jnp.dot(
            left[:, :early], w_refs[0][:, at : at + chunk], preferred_element_type=F32
        ) + jnp.dot(left[:, early:], w_refs[1][:, at : at + chunk], preferred_element_type=F32)
        for s in range(n_ex):
            outs[s][:, at : at + chunk] = out[s * tokens : (s + 1) * tokens, :].astype(outs[s].dtype)


def norm_kernel(n_ex, n_dp, *refs):
    parts, base_ref, ext_ref, gain_ref = refs[:n_ex], *refs[n_ex : n_ex + 3]
    hid_ref, pay_ref = refs[n_ex + 3 :]
    hidden = base_ref[...]
    for s in range(n_ex):
        hidden = hidden + parts[s][...].astype(F32)
    hid_ref[...] = hidden
    model = hidden.shape[1]
    mean = jnp.mean(hidden * hidden, axis=-1, keepdims=True) + NORM_EPS
    normed = hidden * lax.rsqrt(mean) * gain_ref[...]
    pay_ref[:, :model] = normed.astype(BF16)
    ext = ext_ref[...]
    root = jnp.sqrt(mean)
    high = root.astype(BF16).astype(F32)
    middle = (root - high).astype(BF16).astype(F32)
    low = root - high - middle
    lane = lax.broadcasted_iota(jnp.int32, ext.shape, 1)
    at = 3 * n_dp
    ext = jnp.where(lane == at, high, ext)
    ext = jnp.where(lane == at + 1, middle, ext)
    ext = jnp.where(lane == at + 2, low, ext)
    pay_ref[:, model:] = ext.astype(BF16)


def expert_kernel(n_dp, n_ex, tokens, *refs):
    to_ref = refs[0]
    pieces = refs[1 : 1 + n_dp]
    gate_ref, up_ref, down_ref, gain_ref, hid_ref = refs[1 + n_dp : 6 + n_dp]
    outs = refs[6 + n_dp : 6 + 2 * n_dp]
    real_ref, lhs, act_scr, new_scr = refs[6 + 2 * n_dp :]
    dp = lax.axis_index("dp")
    model = gain_ref.shape[1]
    rows = n_ex * tokens
    coef = []
    rel = to_ref[n_dp * n_ex : n_dp * n_ex + 1, 0:1]
    carried = jnp.zeros((1, pieces[0].shape[1]), F32)
    for r in range(n_dp):
        lhs[r * rows : (r + 1) * rows, :] = pieces[r][:, :model]
        ext = pieces[r][:, model:].astype(F32)
        lane = lax.broadcasted_iota(jnp.int32, ext.shape, 1)
        mine = (lane == dp) | (lane == dp + n_dp) | (lane == dp + 2 * n_dp)
        coef.append(jnp.sum(jnp.where(mine, ext, 0.0), axis=-1, keepdims=True))
        carried = jnp.where(rel == r, pieces[r][0:tokens, :].astype(F32)[0:1, :], carried)
    tail = carried[:, model:]
    lane = lax.broadcasted_iota(jnp.int32, tail.shape, 1)
    root = jnp.sum(
        jnp.where((lane >= 3 * n_dp) & (lane < 3 * n_dp + 3), tail, 0.0), axis=-1, keepdims=True
    )
    first = lax.broadcasted_iota(jnp.int32, (tokens, 1), 0) == 0
    real_ref[...] = jnp.where(first, carried[:, :model] * root / gain_ref[...], hid_ref[...])
    x = lhs[...]
    gate = jnp.dot(x, gate_ref[0], preferred_element_type=F32)
    up = jnp.dot(x, up_ref[0], preferred_element_type=F32)
    act = gate / (1.0 + jnp.exp(-gate)) * up
    for r in range(n_dp):
        act_scr[r * rows : (r + 1) * rows, :] = coef[r] * act[r * rows : (r + 1) * rows, :]
    new_scr[...] = act_scr[...]
    for r in range(n_dp):
        for s in range(n_ex):
            to = to_ref[r * n_ex + s : r * n_ex + s + 1, 0:1][0, 0]
            at = (r * n_ex + s) * tokens
            new_scr[pl.ds(to, 1), :] = act_scr[at : at + 1, :]
    left = new_scr[...].astype(BF16)
    chunk = min(1024, model)
    for at in range(0, model, chunk):
        out = jnp.dot(left, down_ref[:, at : at + chunk], preferred_element_type=F32)
        for r in range(n_dp):
            for s in range(n_ex):
                first_row = (r * n_ex + s) * tokens
                outs[r][s, :, at : at + chunk] = out[first_row : first_row + tokens, :].astype(BF16)


def per_device(
    query, fresh_kv, cache, lengths, moves, residual, out_weight, norm_gain,
    w_gate, w_up, w_down, routes, gates,
):
    n_dp = lax.axis_size("dp")
    n_ex = lax.axis_size("expert")
    tokens, model = query.shape
    width = fresh_kv.shape[1] // 2
    kv_heads = width // HD
    part = out_weight.shape[0]
    context = cache.shape[1]
    shape = jax.ShapeDtypeStruct

    ext_width = -(-(3 * n_dp + 3) // LANES) * LANES
    top_count = routes.shape[1]
    small = (query, fresh_kv, residual, routes.T, gates.T, lengths, moves)
    row, q_in, fresh_in, res_in, ext, info = call(
        functools.partial(entry_kernel, n_dp),
        [
            shape((1, 2 * model + 2 * width + ext_width), BF16),
            shape(query.shape, BF16),
            shape(fresh_kv.shape, BF16),
            shape(residual.shape, BF16),
            shape((tokens, ext_width), F32),
            shape((2 * tokens, LANES), jnp.int32),
        ],
        [spec(pltpu.HBM)] * len(small),
        scratch=[
            pltpu.SMEM((top_count, tokens), jnp.int32),
            pltpu.SMEM((top_count, tokens), F32),
            pltpu.SMEM(lengths.shape, jnp.int32),
            pltpu.SMEM(moves.shape, jnp.int32),
            pltpu.SemaphoreType.DMA((len(small),)),
        ],
        limit=4 << 20,
        moved=tokens * model * 4,
    )(*map(in_hbm, small))
    rows = xor_exchange([row] * n_dp, "dp", n_dp)

    early = part // 2
    att, kv0, out_early, targets = call(
        functools.partial(local_kernel, n_dp, kv_heads),
        [
            shape((n_ex, tokens, part), F32),
            shape(cache.shape[1:], BF16),
            shape((early, model), BF16),
            shape((n_dp * n_ex + 8, LANES), jnp.int32),
        ],
        [spec()] * 3 + [spec(pltpu.HBM)] * 3,
        scratch=[
            pltpu.VMEM((tokens - 1,) + cache.shape[1:], BF16),
            pltpu.VMEM((tokens, model // HD, HD), F32),
            pltpu.SMEM(moves.shape, jnp.int32),
            pltpu.SemaphoreType.DMA(()),
            pltpu.SemaphoreType.DMA((tokens,)),
            pltpu.SemaphoreType.DMA((4,)),
        ],
        limit=6 << 20,
        flops=4 * tokens * model * context,
        moved=cache.size * 2 + early * model * 2,
    )(info, q_in, fresh_in, in_hbm(moves), in_hbm(cache), in_hbm(out_weight))

    moved = call(
        functools.partial(moved_kernel, n_dp, n_ex, kv_heads, 2 * width),
        [shape((tokens, part), BF16)] * n_ex
        + [shape((tokens, model), F32), shape((tokens, ext_width), F32)],
        [spec()] * (n_dp + 5),
        scratch=[
            pltpu.VMEM(row.shape, F32),
            pltpu.VMEM((model // HD, HD), F32),
            pltpu.VMEM((n_ex, tokens, part), F32),
        ],
        limit=6 << 20,
        flops=4 * model * context,
        moved=cache.size // tokens * 2,
    )(info, *rows, att, kv0, res_in, ext)
    blocks = crossed_exchange(moved[:n_ex], n_dp, n_ex)
    base, ext_all = moved[n_ex:]

    out_late = fetched(out_weight, part - early, early)
    partials = call(
        functools.partial(project_kernel, n_ex),
        [shape((tokens, model), F32)] + [shape((tokens, model), BF16)] * (n_ex - 1),
        [spec()] * (n_ex + 2),
        scratch=[pltpu.VMEM((n_ex * tokens, part), F32)],
        limit=4 << 20,
        flops=2 * n_ex * tokens * part * model,
        moved=out_weight.size * 2,
    )(*blocks, out_early, out_late)
    partials = crossed_exchange(partials, n_dp, n_ex)

    down = fetched(w_down[0], w_down.shape[1], 0)

    hidden, payload = call(
        functools.partial(norm_kernel, n_ex, n_dp),
        [shape((tokens, model), F32), shape((tokens, model + ext_width), BF16)],
        [spec()] * (n_ex + 3),
        limit=4 << 20,
        flops=10 * tokens * model,
        moved=tokens * model * 16,
    )(*partials, base, ext_all, norm_gain[None])
    gathered = crossed_exchange([payload] * n_ex, n_dp, n_ex)
    turns = dp_turns(n_dp)

    def over_dp(array, turn):
        return lax.ppermute(array, "dp", [(j, j ^ turn) for j in range(n_dp)])

    top = turns[-1]
    near = over_dp(payload, top)
    rest = over_dp(jnp.stack(gathered[1:]), top)
    pieces = {
        0: jnp.concatenate(gathered, axis=0),
        top: jnp.concatenate([near] + [rest[s] for s in range(n_ex - 1)], axis=0),
    }
    for turn in reversed(turns[:-1]):
        for r in list(pieces):
            pieces[r ^ turn] = over_dp(pieces[r], turn)

    group_rows = n_ex * tokens
    all_rows = n_dp * group_rows
    hidden_units = w_down.shape[1]
    weights_bytes = (w_gate.size + w_up.size + w_down.size) * 2
    done = call(
        functools.partial(expert_kernel, n_dp, n_ex, tokens),
        [shape((n_ex, tokens, model), BF16)] * n_dp + [shape((tokens, model), F32)],
        [spec()] * (n_dp + 6),
        scratch=[
            pltpu.VMEM((all_rows, model), BF16),
            pltpu.VMEM((all_rows, hidden_units), F32),
            pltpu.VMEM((all_rows, hidden_units), F32),
        ],
        limit=(8 << 20) + all_rows * model * 8,
        flops=6 * all_rows * model * hidden_units,
        moved=weights_bytes,
    )(targets, *[pieces[r] for r in range(n_dp)], w_gate, w_up, down, norm_gain[None], hidden)
    terms = {r: [done[r]] for r in range(n_dp)}
    reach = {0: 0}
    for i, turn in enumerate(turns):
        reach |= {r ^ turn: mark | 1 << i for r, mark in reach.items()}
    real = done[n_dp]

    def added(arrays):
        return functools.reduce(jnp.add, [array.astype(F32) for array in arrays])

    for i, turn in enumerate(turns[:-1]):
        far = {r: r ^ turn for r in terms if reach[r] >> i & 1}
        for r in sorted(far, key=lambda r: -reach[r]):
            whole = terms.pop(r)
            whole = whole[0] if len(whole) == 1 else added(whole).astype(BF16)
            terms[far[r]].append(over_dp(whole, turn))
    rest = over_dp(added([t[1:] for t in terms[top]]).astype(BF16), top)
    near = over_dp(added([t[0] for t in terms[top]]).astype(BF16), top)
    mixed = added([t[1:] for t in terms[0]] + [rest]).astype(BF16)
    staying = added([t[0] for t in terms[0]] + [near])
    back = crossed_exchange([staying] + [mixed[s] for s in range(n_ex - 1)], n_dp, n_ex)
    total = real
    for s in range(n_ex):
        total = total + back[s].astype(F32)
    return total.astype(BF16)


def solution(mesh):
    placed = (
        P(("groups", "dp", "expert"), None),
        P(("groups", "dp", "expert"), None),
        P(("groups", "dp", "expert"), None, None),
        P(("groups", "dp", "expert")),
        P("groups", None),
        P(("groups", "dp", "expert"), None),
        P("expert", None),
        P(),
        P("dp", None, "expert"),
        P("dp", None, "expert"),
        P("dp", "expert", None),
        P(("groups", "dp", "expert"), None),
        P(("groups", "dp", "expert"), None),
    )

    return jax.shard_map(
        per_device,
        mesh=mesh,
        in_specs=placed,
        out_specs=P(("groups", "dp", "expert"), None),
        check_vma=False,
    )
```

```python
import functools

import jax
import jax.numpy as jnp
from jax import lax
from jax.experimental import pallas as pl
from jax.experimental.pallas import tpu as pltpu
from jax.sharding import PartitionSpec as P


HD = 128
LANES = 128
NORM_EPS = 1e-06
F32 = jnp.float32
BF16 = jnp.bfloat16


def xor_exchange(blocks, axis, count):
    moved = list(blocks)
    for step in range(count - 1, 0, -1):
        moved[step] = lax.ppermute(blocks[step], axis, [(j, j ^ step) for j in range(count)])
    return moved


def dp_turns(n_dp):
    return [(1 << b) | 1 for b in range(n_dp.bit_length() - 1)]


def crossed_exchange(blocks, n_dp, n_ex):
    moved = list(blocks)
    for step in range(n_ex - 1, 0, -1):
        pairs = [
            (d * n_ex + e, (d ^ 1) * n_ex + (e ^ step)) for d in range(n_dp) for e in range(n_ex)
        ]
        moved[step] = lax.ppermute(blocks[step], ("dp", "expert"), pairs)
    return moved


def spec(space=pltpu.VMEM):
    return pl.BlockSpec(memory_space=space)


def call(kernel, outs, ins, scratch=(), limit=None, flops=0, moved=0):
    many = isinstance(outs, (list, tuple))
    return pl.pallas_call(
        kernel,
        out_shape=outs,
        in_specs=ins,
        out_specs=[spec()] * len(outs) if many else spec(),
        scratch_shapes=list(scratch),
        compiler_params=pltpu.CompilerParams(vmem_limit_bytes=limit),
        cost_estimate=pl.CostEstimate(flops=flops, bytes_accessed=moved, transcendentals=0),
    )


def attend(jobs, kv_heads):
    chains = []
    for q_row, _, q_scr, _, _, _ in jobs:
        heads = q_row.shape[1] // HD
        for h in range(heads):
            q_scr[h : h + 1, :] = q_row[:, h * HD : (h + 1) * HD].astype(F32)
    for job in jobs:
        q_row, fresh_row, q_scr, _, _, _ = job
        group = q_row.shape[1] // HD // kv_heads
        for g in range(kv_heads):
            q = q_scr[g * group : (g + 1) * group, :]
            own_key = fresh_row[:, g * HD : (g + 1) * HD].astype(F32)
            own = jnp.sum(q * own_key, axis=-1, keepdims=True) * HD ** (-0.5)
            chains.append([job, g, group, q.astype(BF16), own])
    return chains


def attend_cache(chains, kv_heads):
    width = kv_heads * HD
    all_scores = []
    for (_, _, _, cache, _, _), g, _, q, _ in chains:
        keys = cache[:, g * HD : (g + 1) * HD]
        all_scores.append(
            lax.dot_general(q, keys, (((1,), (1,)), ((), ())), preferred_element_type=F32)
            * HD ** (-0.5)
        )
    parts = []
    for scores, ((_, _, _, _, length, _), _, _, _, own) in zip(all_scores, chains):
        if length is not None:
            valid = lax.broadcasted_iota(jnp.int32, scores.shape, 1) < length
            scores = jnp.where(valid, scores, -1e30)
        top_cache = jnp.max(scores, axis=-1, keepdims=True)
        weights = jnp.exp(scores - top_cache)
        if length is not None:
            weights = jnp.where(valid, weights, 0.0)
        total = jnp.sum(weights, axis=-1, keepdims=True)
        top = jnp.maximum(top_cache, own)
        parts.append((weights.astype(BF16), total, jnp.exp(top_cache - top), jnp.exp(own - top)))
    mixes = []
    for (weights, _, _, _), ((_, _, _, cache, _, _), g, _, _, _) in zip(parts, chains):
        values = cache[:, width + g * HD : width + (g + 1) * HD]
        mixes.append(jnp.dot(weights, values, preferred_element_type=F32))
    for mixed, (_, total, cache_factor, own_factor), (job, g, group, _, _) in zip(
        mixes, parts, chains
    ):
        _, fresh_row, _, _, _, put = job
        own_value = fresh_row[:, width + g * HD : width + (g + 1) * HD].astype(F32)
        done = (cache_factor * mixed + own_factor * own_value) / (
            cache_factor * total + own_factor
        )
        for j in range(group):
            put(g * group + j, done[j : j + 1, :])


def entry_kernel(
    n_dp, q_hbm, fresh_hbm, res_hbm, routes_hbm, gates_hbm, len_hbm, moves_hbm,
    row_ref, q_ref, fresh_ref, res_ref, ext_ref, info_ref, routes, gates, lengths, moves, sems,
):
    copies = [
        pltpu.make_async_copy(source, to, sems.at[i])
        for i, (source, to) in enumerate(
            [
                (routes_hbm, routes), (gates_hbm, gates), (q_hbm, q_ref),
                (fresh_hbm, fresh_ref), (res_hbm, res_ref), (len_hbm, lengths), (moves_hbm, moves),
            ]
        )
    ]
    for copy in copies:
        copy.start()
    copies[0].wait()
    copies[1].wait()
    top, tokens = routes.shape
    lane = lax.broadcasted_iota(jnp.int32, (1, ext_ref.shape[1]), 1)
    turn = jnp.where(lane >= n_dp, 1, 0) + jnp.where(lane >= 2 * n_dp, 1, 0)
    name = lane - n_dp * turn
    for t in range(tokens):
        share = jnp.zeros(lane.shape, F32)
        for k in range(top):
            share = jnp.where(name == routes[k, t], gates[k, t], share)
        high = share.astype(BF16).astype(F32)
        middle = (share - high).astype(BF16).astype(F32)
        low = share - high - middle
        share = jnp.where(turn == 0, high, jnp.where(turn == 1, middle, low))
        ext_ref[t : t + 1, :] = jnp.where(lane < 3 * n_dp, share, 0.0)
    for copy in copies[2:]:
        copy.wait()
    for t in range(tokens):
        info_ref[t : t + 1, :] = jnp.full((1, LANES), lengths[t], jnp.int32)
    dp = lax.axis_index("dp")
    rel = moves[lax.axis_index("expert"), dp] ^ dp
    info_ref[tokens : tokens + 1, :] = jnp.full((1, LANES), rel, jnp.int32)
    model, width = q_ref.shape[1], fresh_ref.shape[1]
    row_ref[:, :model] = q_ref[0:1, :]
    row_ref[:, model : model + width] = fresh_ref[0:1, :]
    row_ref[:, model + width : 2 * model + width] = res_ref[0:1, :]
    row_ref[:, 2 * model + width :] = ext_ref[0:1, :].astype(BF16)


def fetch(source, to, sems, column=0, pieces=4):
    rows, columns = to.shape
    step = rows // pieces
    return [
        pltpu.make_async_copy(
            source.at[pl.ds(i * step, step), pl.ds(column, columns)],
            to.at[pl.ds(i * step, step)],
            sems.at[i],
        )
        for i in range(pieces)
    ]


def local_kernel(
    n_dp, kv_heads, info_ref, q_ref, fresh_ref, moves_hbm, cache_hbm, w_hbm,
    att_ref, kv0_ref, w_ref, to_ref, kv, q_scr, moves, moves_sem, sems, w_sems,
):
    parts, tokens, part = att_ref.shape
    goals = pltpu.make_async_copy(moves_hbm, moves, moves_sem)
    goals.start()
    per = part // HD
    copies = [
        pltpu.make_async_copy(cache_hbm.at[t], kv.at[t - 1] if t else kv0_ref, sems.at[t])
        for t in range(tokens)
    ]
    weight = fetch(w_hbm, w_ref, w_sems)
    for copy in copies[1:] + copies[:1] + weight:
        copy.start()
    jobs = []
    for t in range(1, tokens):

        def put(head, row, t=t):
            att_ref[head // per, t : t + 1, (head % per) * HD : (head % per + 1) * HD] = row

        jobs.append(
            (
                q_ref[t : t + 1, :], fresh_ref[t : t + 1, :], q_scr.at[t], kv.at[t - 1],
                info_ref[t : t + 1, 0:1], put,
            )
        )
    chains = attend(jobs, kv_heads)
    for copy in copies[1:]:
        copy.wait()
    attend_cache(chains, kv_heads)
    for s in range(parts):
        att_ref[s, 0:1, :] = jnp.zeros((1, part), F32)
    goals.wait()
    dp = lax.axis_index("dp")
    ex = lax.axis_index("expert")
    for r in range(n_dp):
        for s in range(parts):
            side = 1 if s else 0
            to = ((moves[ex ^ s, dp ^ r ^ side] ^ dp ^ side) * parts + s) * tokens
            at = r * parts + s
            to_ref[at : at + 1, :] = jnp.full((1, LANES), to, jnp.int32)
    source = 0
    for d in range(n_dp):
        source = jnp.where(moves[ex, d] == dp, d, source)
    to_ref[n_dp * parts : n_dp * parts + 1, :] = jnp.full((1, LANES), source ^ dp, jnp.int32)
    for copy in copies[:1] + weight:
        copy.wait()


def fetch_kernel(column, source, to, sems):
    copies = fetch(source, to, sems, column)
    for copy in copies:
        copy.start()
    for copy in copies:
        copy.wait()


def fetched(source, column, columns):
    return call(
        functools.partial(fetch_kernel, column),
        jax.ShapeDtypeStruct((source.shape[0], columns), source.dtype),
        [spec(pltpu.HBM)],
        scratch=[pltpu.SemaphoreType.DMA((4,))],
        limit=1 << 20,
        moved=source.shape[0] * columns * 4,
    )(in_hbm(source))


def in_hbm(array):
    return pltpu.with_memory_space_constraint(array, pltpu.HBM)


def moved_kernel(n_dp, n_ex, kv_heads, width, *refs):
    info_ref = refs[0]
    rows = refs[1 : 1 + n_dp]
    att_ref, kv0_ref, res_ref, ext_ref = refs[1 + n_dp : 5 + n_dp]
    outs = refs[5 + n_dp : 5 + n_dp + n_ex]
    base_ref, ext_out, row_scr, q_scr, full = refs[5 + n_dp + n_ex :]
    ex = lax.axis_index("expert")
    tokens = res_ref.shape[0]
    rel = info_ref[tokens : tokens + 1, 0:1]
    row = rows[0][...].astype(F32)
    for r in range(1, n_dp):
        row = jnp.where(rel == r, rows[r][...].astype(F32), row)
    row_scr[...] = row
    model = res_ref.shape[1]
    full[...] = att_ref[...]
    part = full.shape[2]
    per = part // HD

    def put(head, value):
        full[head // per, 0:1, (head % per) * HD : (head % per + 1) * HD] = value

    job = (row_scr[:, :model], row_scr[:, model : model + width], q_scr, kv0_ref, None, put)
    attend_cache(attend([job], kv_heads), kv_heads)
    for s in range(n_ex):
        outs[s][...] = full[s ^ ex].astype(BF16)
    first = lax.broadcasted_iota(jnp.int32, (res_ref.shape[0], 1), 0) == 0
    base_ref[...] = jnp.where(first, row_scr[:, model + width : 2 * model + width], res_ref[...].astype(F32))
    ext_out[...] = jnp.where(first, row_scr[:, 2 * model + width :], ext_ref[...])


def project_kernel(n_ex, *refs):
    blocks, w_refs, w_hbm = refs[:n_ex], refs[n_ex : n_ex + 2], refs[n_ex + 2]
    outs, lhs, w_last, sems = refs[n_ex + 3 : -3], *refs[-3:]
    tokens = blocks[0].shape[0]
    edges = [0, w_refs[0].shape[1], w_refs[0].shape[1] + w_refs[1].shape[1]]
    last = fetch(w_hbm, w_last, sems, edges[2])
    for copy in last:
        copy.start()
    for s in range(n_ex):
        lhs[s * tokens : (s + 1) * tokens, :] = blocks[s][...].astype(F32)
    left = lhs[...].astype(BF16)
    for w_ref, edge in zip((*w_refs, w_last), edges):
        if w_ref is w_last:
            for copy in last:
                copy.wait()
        columns = w_ref.shape[1]
        chunk = min(1024, columns)
        for at in range(0, columns, chunk):
            out = jnp.dot(left, w_ref[:, at : at + chunk], preferred_element_type=F32)
            for s in range(n_ex):
                outs[s][:, edge + at : edge + at + chunk] = out[
                    s * tokens : (s + 1) * tokens, :
                ].astype(outs[s].dtype)


def norm_kernel(n_ex, n_dp, *refs):
    parts, base_ref, ext_ref, gain_ref = refs[:n_ex], *refs[n_ex : n_ex + 3]
    hid_ref, pay_ref = refs[n_ex + 3 :]
    hidden = base_ref[...]
    for s in range(n_ex):
        hidden = hidden + parts[s][...].astype(F32)
    hid_ref[...] = hidden
    model = hidden.shape[1]
    mean = jnp.mean(hidden * hidden, axis=-1, keepdims=True) + NORM_EPS
    normed = hidden * lax.rsqrt(mean) * gain_ref[...]
    pay_ref[:, :model] = normed.astype(BF16)
    ext = ext_ref[...]
    root = jnp.sqrt(mean)
    high = root.astype(BF16).astype(F32)
    middle = (root - high).astype(BF16).astype(F32)
    low = root - high - middle
    lane = lax.broadcasted_iota(jnp.int32, ext.shape, 1)
    at = 3 * n_dp
    ext = jnp.where(lane == at, high, ext)
    ext = jnp.where(lane == at + 1, middle, ext)
    ext = jnp.where(lane == at + 2, low, ext)
    pay_ref[:, model:] = ext.astype(BF16)


def expert_kernel(n_dp, n_ex, tokens, *refs):
    to_ref = refs[0]
    pieces = refs[1 : 1 + n_dp]
    gate_ref, up_ref, down_ref, gain_ref, hid_ref = refs[1 + n_dp : 6 + n_dp]
    outs = refs[6 + n_dp : 6 + 2 * n_dp]
    real_ref, lhs, act_scr, new_scr = refs[6 + 2 * n_dp :]
    dp = lax.axis_index("dp")
    model = gain_ref.shape[1]
    rows = n_ex * tokens
    coef = []
    rel = to_ref[n_dp * n_ex : n_dp * n_ex + 1, 0:1]
    carried = jnp.zeros((1, pieces[0].shape[1]), F32)
    for r in range(n_dp):
        lhs[r * rows : (r + 1) * rows, :] = pieces[r][:, :model]
        ext = pieces[r][:, model:].astype(F32)
        lane = lax.broadcasted_iota(jnp.int32, ext.shape, 1)
        mine = (lane == dp) | (lane == dp + n_dp) | (lane == dp + 2 * n_dp)
        coef.append(jnp.sum(jnp.where(mine, ext, 0.0), axis=-1, keepdims=True))
        carried = jnp.where(rel == r, pieces[r][0:tokens, :].astype(F32)[0:1, :], carried)
    tail = carried[:, model:]
    lane = lax.broadcasted_iota(jnp.int32, tail.shape, 1)
    root = jnp.sum(
        jnp.where((lane >= 3 * n_dp) & (lane < 3 * n_dp + 3), tail, 0.0), axis=-1, keepdims=True
    )
    first = lax.broadcasted_iota(jnp.int32, (tokens, 1), 0) == 0
    real_ref[...] = jnp.where(first, carried[:, :model] * root / gain_ref[...], hid_ref[...])
    x = lhs[...]
    gate = jnp.dot(x, gate_ref[0], preferred_element_type=F32)
    up = jnp.dot(x, up_ref[0], preferred_element_type=F32)
    act = gate / (1.0 + jnp.exp(-gate)) * up
    for r in range(n_dp):
        act_scr[r * rows : (r + 1) * rows, :] = coef[r] * act[r * rows : (r + 1) * rows, :]
    new_scr[...] = act_scr[...]
    for r in range(n_dp):
        for s in range(n_ex):
            to = to_ref[r * n_ex + s : r * n_ex + s + 1, 0:1][0, 0]
            at = (r * n_ex + s) * tokens
            new_scr[pl.ds(to, 1), :] = act_scr[at : at + 1, :]
    left = new_scr[...].astype(BF16)
    chunk = min(1024, model)
    for at in range(0, model, chunk):
        out = jnp.dot(left, down_ref[:, at : at + chunk], preferred_element_type=F32)
        for r in range(n_dp):
            for s in range(n_ex):
                first_row = (r * n_ex + s) * tokens
                outs[r][s, :, at : at + chunk] = out[first_row : first_row + tokens, :].astype(BF16)


def per_device(
    query, fresh_kv, cache, lengths, moves, residual, out_weight, norm_gain,
    w_gate, w_up, w_down, routes, gates,
):
    n_dp = lax.axis_size("dp")
    n_ex = lax.axis_size("expert")
    tokens, model = query.shape
    width = fresh_kv.shape[1] // 2
    kv_heads = width // HD
    part = out_weight.shape[0]
    context = cache.shape[1]
    shape = jax.ShapeDtypeStruct

    ext_width = -(-(3 * n_dp + 3) // LANES) * LANES
    top_count = routes.shape[1]
    small = (query, fresh_kv, residual, routes.T, gates.T, lengths, moves)
    row, q_in, fresh_in, res_in, ext, info = call(
        functools.partial(entry_kernel, n_dp),
        [
            shape((1, 2 * model + 2 * width + ext_width), BF16),
            shape(query.shape, BF16),
            shape(fresh_kv.shape, BF16),
            shape(residual.shape, BF16),
            shape((tokens, ext_width), F32),
            shape((2 * tokens, LANES), jnp.int32),
        ],
        [spec(pltpu.HBM)] * len(small),
        scratch=[
            pltpu.SMEM((top_count, tokens), jnp.int32),
            pltpu.SMEM((top_count, tokens), F32),
            pltpu.SMEM(lengths.shape, jnp.int32),
            pltpu.SMEM(moves.shape, jnp.int32),
            pltpu.SemaphoreType.DMA((len(small),)),
        ],
        limit=4 << 20,
        moved=tokens * model * 4,
    )(*map(in_hbm, small))
    rows = xor_exchange([row] * n_dp, "dp", n_dp)

    early = model // 4
    att, kv0, out_early, targets = call(
        functools.partial(local_kernel, n_dp, kv_heads),
        [
            shape((n_ex, tokens, part), F32),
            shape(cache.shape[1:], BF16),
            shape((part, early), BF16),
            shape((n_dp * n_ex + 8, LANES), jnp.int32),
        ],
        [spec()] * 3 + [spec(pltpu.HBM)] * 3,
        scratch=[
            pltpu.VMEM((tokens - 1,) + cache.shape[1:], BF16),
            pltpu.VMEM((tokens, model // HD, HD), F32),
            pltpu.SMEM(moves.shape, jnp.int32),
            pltpu.SemaphoreType.DMA(()),
            pltpu.SemaphoreType.DMA((tokens,)),
            pltpu.SemaphoreType.DMA((4,)),
        ],
        limit=6 << 20,
        flops=4 * tokens * model * context,
        moved=cache.size * 2 + part * early * 2,
    )(info, q_in, fresh_in, in_hbm(moves), in_hbm(cache), in_hbm(out_weight))

    moved = call(
        functools.partial(moved_kernel, n_dp, n_ex, kv_heads, 2 * width),
        [shape((tokens, part), BF16)] * n_ex
        + [shape((tokens, model), F32), shape((tokens, ext_width), F32)],
        [spec()] * (n_dp + 5),
        scratch=[
            pltpu.VMEM(row.shape, F32),
            pltpu.VMEM((model // HD, HD), F32),
            pltpu.VMEM((n_ex, tokens, part), F32),
        ],
        limit=6 << 20,
        flops=4 * model * context,
        moved=cache.size // tokens * 2,
    )(info, *rows, att, kv0, res_in, ext)
    blocks = crossed_exchange(moved[:n_ex], n_dp, n_ex)
    base, ext_all = moved[n_ex:]

    late = model // 2
    out_late = fetched(out_weight, early, late)
    partials = call(
        functools.partial(project_kernel, n_ex),
        [shape((tokens, model), F32)] + [shape((tokens, model), BF16)] * (n_ex - 1),
        [spec()] * (n_ex + 2) + [spec(pltpu.HBM)],
        scratch=[
            pltpu.VMEM((n_ex * tokens, part), F32),
            pltpu.VMEM((part, model - early - late), BF16),
            pltpu.SemaphoreType.DMA((4,)),
        ],
        limit=8 << 20,
        flops=2 * n_ex * tokens * part * model,
        moved=out_weight.size * 2,
    )(*blocks, out_early, out_late, in_hbm(out_weight))
    partials = crossed_exchange(partials, n_dp, n_ex)

    down = fetched(w_down[0], 0, model)

    hidden, payload = call(
        functools.partial(norm_kernel, n_ex, n_dp),
        [shape((tokens, model), F32), shape((tokens, model + ext_width), BF16)],
        [spec()] * (n_ex + 3),
        limit=4 << 20,
        flops=10 * tokens * model,
        moved=tokens * model * 16,
    )(*partials, base, ext_all, norm_gain[None])
    gathered = crossed_exchange([payload] * n_ex, n_dp, n_ex)
    turns = dp_turns(n_dp)

    def over_dp(array, turn):
        return lax.ppermute(array, "dp", [(j, j ^ turn) for j in range(n_dp)])

    top = turns[-1]
    near = over_dp(payload, top)
    rest = over_dp(jnp.stack(gathered[1:]), top)
    pieces = {
        0: jnp.concatenate(gathered, axis=0),
        top: jnp.concatenate([near] + [rest[s] for s in range(n_ex - 1)], axis=0),
    }
    for turn in reversed(turns[:-1]):
        for r in list(pieces):
            pieces[r ^ turn] = over_dp(pieces[r], turn)

    group_rows = n_ex * tokens
    all_rows = n_dp * group_rows
    hidden_units = w_down.shape[1]
    weights_bytes = (w_gate.size + w_up.size + w_down.size) * 2
    done = call(
        functools.partial(expert_kernel, n_dp, n_ex, tokens),
        [shape((n_ex, tokens, model), BF16)] * n_dp + [shape((tokens, model), F32)],
        [spec()] * (n_dp + 6),
        scratch=[
            pltpu.VMEM((all_rows, model), BF16),
            pltpu.VMEM((all_rows, hidden_units), F32),
            pltpu.VMEM((all_rows, hidden_units), F32),
        ],
        limit=(8 << 20) + all_rows * model * 8,
        flops=6 * all_rows * model * hidden_units,
        moved=weights_bytes,
    )(targets, *[pieces[r] for r in range(n_dp)], w_gate, w_up, down, norm_gain[None], hidden)
    terms = {r: [done[r]] for r in range(n_dp)}
    reach = {0: 0}
    for i, turn in enumerate(turns):
        reach |= {r ^ turn: mark | 1 << i for r, mark in reach.items()}
    real = done[n_dp]

    def added(arrays):
        return functools.reduce(jnp.add, [array.astype(F32) for array in arrays])

    for i, turn in enumerate(turns[:-1]):
        far = {r: r ^ turn for r in terms if reach[r] >> i & 1}
        for r in sorted(far, key=lambda r: -reach[r]):
            whole = terms.pop(r)
            whole = whole[0] if len(whole) == 1 else added(whole).astype(BF16)
            terms[far[r]].append(over_dp(whole, turn))
    rest = over_dp(added([t[1:] for t in terms[top]]).astype(BF16), top)
    near = over_dp(added([t[0] for t in terms[top]]).astype(BF16), top)
    mixed = added([t[1:] for t in terms[0]] + [rest]).astype(BF16)
    staying = added([t[0] for t in terms[0]] + [near])
    back = crossed_exchange([staying] + [mixed[s] for s in range(n_ex - 1)], n_dp, n_ex)
    total = real
    for s in range(n_ex):
        total = total + back[s].astype(F32)
    return total.astype(BF16)


def solution(mesh):
    placed = (
        P(("groups", "dp", "expert"), None),
        P(("groups", "dp", "expert"), None),
        P(("groups", "dp", "expert"), None, None),
        P(("groups", "dp", "expert")),
        P("groups", None),
        P(("groups", "dp", "expert"), None),
        P("expert", None),
        P(),
        P("dp", None, "expert"),
        P("dp", None, "expert"),
        P("dp", "expert", None),
        P(("groups", "dp", "expert"), None),
        P(("groups", "dp", "expert"), None),
    )

    return jax.shard_map(
        per_device,
        mesh=mesh,
        in_specs=placed,
        out_specs=P(("groups", "dp", "expert"), None),
        check_vma=False,
    )
```

```python
import functools

import jax
import jax.numpy as jnp
from jax import lax
from jax.experimental import pallas as pl
from jax.experimental.pallas import tpu as pltpu
from jax.sharding import PartitionSpec as P


HD = 128
LANES = 128
NORM_EPS = 1e-06
F32 = jnp.float32
BF16 = jnp.bfloat16
COVER = 10**10


def xor_exchange(blocks, axis, count):
    moved = list(blocks)
    for step in range(count - 1, 0, -1):
        moved[step] = lax.ppermute(blocks[step], axis, [(j, j ^ step) for j in range(count)])
    return moved


def dp_turns(n_dp):
    return [(1 << b) | 1 for b in range(n_dp.bit_length() - 1)]


def crossed_exchange(blocks, n_dp, n_ex):
    moved = list(blocks)
    for step in range(n_ex - 1, 0, -1):
        pairs = [
            (d * n_ex + e, (d ^ 1) * n_ex + (e ^ step)) for d in range(n_dp) for e in range(n_ex)
        ]
        moved[step] = lax.ppermute(blocks[step], ("dp", "expert"), pairs)
    return moved


def spec(space=pltpu.VMEM):
    return pl.BlockSpec(memory_space=space)


def call(kernel, outs, ins, scratch=(), limit=None, flops=0, moved=0):
    many = isinstance(outs, (list, tuple))
    return pl.pallas_call(
        kernel,
        out_shape=outs,
        in_specs=ins,
        out_specs=[spec()] * len(outs) if many else spec(),
        scratch_shapes=list(scratch),
        compiler_params=pltpu.CompilerParams(vmem_limit_bytes=limit),
        cost_estimate=pl.CostEstimate(flops=flops, bytes_accessed=moved, transcendentals=0),
    )


def attend(jobs, kv_heads):
    chains = []
    for q_row, _, q_scr, _, _, _ in jobs:
        heads = q_row.shape[1] // HD
        for h in range(heads):
            q_scr[h : h + 1, :] = q_row[:, h * HD : (h + 1) * HD].astype(F32)
    for job in jobs:
        q_row, fresh_row, q_scr, _, _, _ = job
        group = q_row.shape[1] // HD // kv_heads
        for g in range(kv_heads):
            q = q_scr[g * group : (g + 1) * group, :]
            own_key = fresh_row[:, g * HD : (g + 1) * HD].astype(F32)
            own = jnp.sum(q * own_key, axis=-1, keepdims=True) * HD ** (-0.5)
            chains.append([job, g, group, q.astype(BF16), own])
    return chains


def attend_cache(chains, kv_heads):
    width = kv_heads * HD
    all_scores = []
    for (_, _, _, cache, _, _), g, _, q, _ in chains:
        keys = cache[:, g * HD : (g + 1) * HD]
        all_scores.append(
            lax.dot_general(q, keys, (((1,), (1,)), ((), ())), preferred_element_type=F32)
            * HD ** (-0.5)
        )
    parts = []
    for scores, ((_, _, _, _, length, _), _, _, _, own) in zip(all_scores, chains):
        if length is not None:
            valid = lax.broadcasted_iota(jnp.int32, scores.shape, 1) < length
            scores = jnp.where(valid, scores, -1e30)
        top_cache = jnp.max(scores, axis=-1, keepdims=True)
        weights = jnp.exp(scores - top_cache)
        if length is not None:
            weights = jnp.where(valid, weights, 0.0)
        total = jnp.sum(weights, axis=-1, keepdims=True)
        top = jnp.maximum(top_cache, own)
        parts.append((weights.astype(BF16), total, jnp.exp(top_cache - top), jnp.exp(own - top)))
    mixes = []
    for (weights, _, _, _), ((_, _, _, cache, _, _), g, _, _, _) in zip(parts, chains):
        values = cache[:, width + g * HD : width + (g + 1) * HD]
        mixes.append(jnp.dot(weights, values, preferred_element_type=F32))
    for mixed, (_, total, cache_factor, own_factor), (job, g, group, _, _) in zip(
        mixes, parts, chains
    ):
        _, fresh_row, _, _, _, put = job
        own_value = fresh_row[:, width + g * HD : width + (g + 1) * HD].astype(F32)
        done = (cache_factor * mixed + own_factor * own_value) / (
            cache_factor * total + own_factor
        )
        for j in range(group):
            put(g * group + j, done[j : j + 1, :])


def entry_kernel(
    n_dp, q_hbm, fresh_hbm, res_hbm, routes_hbm, gates_hbm, len_hbm, moves_hbm,
    row_ref, q_ref, fresh_ref, res_ref, ext_ref, info_ref, routes, gates, lengths, moves, sems,
):
    copies = [
        pltpu.make_async_copy(source, to, sems.at[i])
        for i, (source, to) in enumerate(
            [
                (routes_hbm, routes), (gates_hbm, gates), (q_hbm, q_ref),
                (fresh_hbm, fresh_ref), (res_hbm, res_ref), (len_hbm, lengths), (moves_hbm, moves),
            ]
        )
    ]
    for copy in copies:
        copy.start()
    copies[0].wait()
    copies[1].wait()
    top, tokens = routes.shape
    lane = lax.broadcasted_iota(jnp.int32, (1, ext_ref.shape[1]), 1)
    turn = jnp.where(lane >= n_dp, 1, 0) + jnp.where(lane >= 2 * n_dp, 1, 0)
    name = lane - n_dp * turn
    for t in range(tokens):
        share = jnp.zeros(lane.shape, F32)
        for k in range(top):
            share = jnp.where(name == routes[k, t], gates[k, t], share)
        high = share.astype(BF16).astype(F32)
        middle = (share - high).astype(BF16).astype(F32)
        low = share - high - middle
        share = jnp.where(turn == 0, high, jnp.where(turn == 1, middle, low))
        ext_ref[t : t + 1, :] = jnp.where(lane < 3 * n_dp, share, 0.0)
    for copy in copies[2:]:
        copy.wait()
    for t in range(tokens):
        info_ref[t : t + 1, :] = jnp.full((1, LANES), lengths[t], jnp.int32)
    dp = lax.axis_index("dp")
    rel = moves[lax.axis_index("expert"), dp] ^ dp
    info_ref[tokens : tokens + 1, :] = jnp.full((1, LANES), rel, jnp.int32)
    model, width = q_ref.shape[1], fresh_ref.shape[1]
    row_ref[:, :model] = q_ref[0:1, :]
    row_ref[:, model : model + width] = fresh_ref[0:1, :]
    row_ref[:, model + width : 2 * model + width] = res_ref[0:1, :]
    row_ref[:, 2 * model + width :] = ext_ref[0:1, :].astype(BF16)


def local_kernel(
    n_dp, kv_heads, info_ref, q_ref, fresh_ref, moves_hbm, cache_ref,
    att_ref, to_ref, q_scr, moves, moves_sem,
):
    parts, tokens, part = att_ref.shape
    goals = pltpu.make_async_copy(moves_hbm, moves, moves_sem)
    goals.start()
    per = part // HD
    jobs = []
    for t in range(1, tokens):

        def put(head, row, t=t):
            att_ref[head // per, t : t + 1, (head % per) * HD : (head % per + 1) * HD] = row

        jobs.append(
            (
                q_ref[t : t + 1, :], fresh_ref[t : t + 1, :], q_scr.at[t], cache_ref.at[t],
                info_ref[t : t + 1, 0:1], put,
            )
        )
    attend_cache(attend(jobs, kv_heads), kv_heads)
    for s in range(parts):
        att_ref[s, 0:1, :] = jnp.zeros((1, part), F32)
    goals.wait()
    dp = lax.axis_index("dp")
    ex = lax.axis_index("expert")
    for r in range(n_dp):
        for s in range(parts):
            side = 1 if s else 0
            to = ((moves[ex ^ s, dp ^ r ^ side] ^ dp ^ side) * parts + s) * tokens
            at = r * parts + s
            to_ref[at : at + 1, :] = jnp.full((1, LANES), to, jnp.int32)
    source = 0
    for d in range(n_dp):
        source = jnp.where(moves[ex, d] == dp, d, source)
    to_ref[n_dp * parts : n_dp * parts + 1, :] = jnp.full((1, LANES), source ^ dp, jnp.int32)


def in_hbm(array):
    return pltpu.with_memory_space_constraint(array, pltpu.HBM)


def moved_kernel(n_dp, n_ex, kv_heads, width, *refs):
    info_ref = refs[0]
    rows = refs[1 : 1 + n_dp]
    att_ref, cache_ref, res_ref, ext_ref = refs[1 + n_dp : 5 + n_dp]
    outs = refs[5 + n_dp : 5 + n_dp + n_ex]
    base_ref, ext_out, row_scr, q_scr, full = refs[5 + n_dp + n_ex :]
    ex = lax.axis_index("expert")
    tokens = res_ref.shape[0]
    rel = info_ref[tokens : tokens + 1, 0:1]
    row = rows[0][...].astype(F32)
    for r in range(1, n_dp):
        row = jnp.where(rel == r, rows[r][...].astype(F32), row)
    row_scr[...] = row
    model = res_ref.shape[1]
    full[...] = att_ref[...]
    part = full.shape[2]
    per = part // HD

    def put(head, value):
        full[head // per, 0:1, (head % per) * HD : (head % per + 1) * HD] = value

    job = (row_scr[:, :model], row_scr[:, model : model + width], q_scr, cache_ref.at[0], None, put)
    attend_cache(attend([job], kv_heads), kv_heads)
    for s in range(n_ex):
        outs[s][...] = full[s ^ ex].astype(BF16)
    first = lax.broadcasted_iota(jnp.int32, (res_ref.shape[0], 1), 0) == 0
    base_ref[...] = jnp.where(first, row_scr[:, model + width : 2 * model + width], res_ref[...].astype(F32))
    ext_out[...] = jnp.where(first, row_scr[:, 2 * model + width :], ext_ref[...])


def project_kernel(n_ex, *refs):
    blocks, w_ref, outs, lhs = refs[:n_ex], refs[n_ex], refs[n_ex + 1 : -1], refs[-1]
    tokens = blocks[0].shape[0]
    for s in range(n_ex):
        lhs[s * tokens : (s + 1) * tokens, :] = blocks[s][...].astype(F32)
    left = lhs[...].astype(BF16)
    model = w_ref.shape[1]
    chunk = min(1024, model)
    for at in range(0, model, chunk):
        out = jnp.dot(left, w_ref[:, at : at + chunk], preferred_element_type=F32)
        for s in range(n_ex):
            outs[s][:, at : at + chunk] = out[s * tokens : (s + 1) * tokens, :].astype(outs[s].dtype)


def norm_kernel(n_ex, n_dp, *refs):
    parts, base_ref, ext_ref, gain_ref = refs[:n_ex], *refs[n_ex : n_ex + 3]
    hid_ref, pay_ref = refs[n_ex + 3 :]
    hidden = base_ref[...]
    for s in range(n_ex):
        hidden = hidden + parts[s][...].astype(F32)
    hid_ref[...] = hidden
    model = hidden.shape[1]
    mean = jnp.mean(hidden * hidden, axis=-1, keepdims=True) + NORM_EPS
    normed = hidden * lax.rsqrt(mean) * gain_ref[...]
    pay_ref[:, :model] = normed.astype(BF16)
    ext = ext_ref[...]
    root = jnp.sqrt(mean)
    high = root.astype(BF16).astype(F32)
    middle = (root - high).astype(BF16).astype(F32)
    low = root - high - middle
    lane = lax.broadcasted_iota(jnp.int32, ext.shape, 1)
    at = 3 * n_dp
    ext = jnp.where(lane == at, high, ext)
    ext = jnp.where(lane == at + 1, middle, ext)
    ext = jnp.where(lane == at + 2, low, ext)
    pay_ref[:, model:] = ext.astype(BF16)


def expert_kernel(n_dp, n_ex, tokens, *refs):
    to_ref = refs[0]
    pieces = refs[1 : 1 + n_dp]
    gate_ref, up_ref, down_ref, gain_ref, hid_ref = refs[1 + n_dp : 6 + n_dp]
    outs = refs[6 + n_dp : 6 + 2 * n_dp]
    real_ref, lhs, act_scr, new_scr = refs[6 + 2 * n_dp :]
    dp = lax.axis_index("dp")
    model = gain_ref.shape[1]
    rows = n_ex * tokens
    coef = []
    rel = to_ref[n_dp * n_ex : n_dp * n_ex + 1, 0:1]
    carried = jnp.zeros((1, pieces[0].shape[1]), F32)
    for r in range(n_dp):
        lhs[r * rows : (r + 1) * rows, :] = pieces[r][:, :model]
        ext = pieces[r][:, model:].astype(F32)
        lane = lax.broadcasted_iota(jnp.int32, ext.shape, 1)
        mine = (lane == dp) | (lane == dp + n_dp) | (lane == dp + 2 * n_dp)
        coef.append(jnp.sum(jnp.where(mine, ext, 0.0), axis=-1, keepdims=True))
        carried = jnp.where(rel == r, pieces[r][0:tokens, :].astype(F32)[0:1, :], carried)
    tail = carried[:, model:]
    lane = lax.broadcasted_iota(jnp.int32, tail.shape, 1)
    root = jnp.sum(
        jnp.where((lane >= 3 * n_dp) & (lane < 3 * n_dp + 3), tail, 0.0), axis=-1, keepdims=True
    )
    first = lax.broadcasted_iota(jnp.int32, (tokens, 1), 0) == 0
    real_ref[...] = jnp.where(first, carried[:, :model] * root / gain_ref[...], hid_ref[...])
    x = lhs[...]
    gate = jnp.dot(x, gate_ref[0], preferred_element_type=F32)
    up = jnp.dot(x, up_ref[0], preferred_element_type=F32)
    act = gate / (1.0 + jnp.exp(-gate)) * up
    for r in range(n_dp):
        act_scr[r * rows : (r + 1) * rows, :] = coef[r] * act[r * rows : (r + 1) * rows, :]
    new_scr[...] = act_scr[...]
    for r in range(n_dp):
        for s in range(n_ex):
            to = to_ref[r * n_ex + s : r * n_ex + s + 1, 0:1][0, 0]
            at = (r * n_ex + s) * tokens
            new_scr[pl.ds(to, 1), :] = act_scr[at : at + 1, :]
    left = new_scr[...].astype(BF16)
    chunk = min(1024, model)
    for at in range(0, model, chunk):
        out = jnp.dot(left, down_ref[0, :, at : at + chunk], preferred_element_type=F32)
        for r in range(n_dp):
            for s in range(n_ex):
                first_row = (r * n_ex + s) * tokens
                outs[r][s, :, at : at + chunk] = out[first_row : first_row + tokens, :].astype(BF16)


def per_device(
    query, fresh_kv, cache, lengths, moves, residual, out_weight, norm_gain,
    w_gate, w_up, w_down, routes, gates,
):
    n_dp = lax.axis_size("dp")
    n_ex = lax.axis_size("expert")
    tokens, model = query.shape
    width = fresh_kv.shape[1] // 2
    kv_heads = width // HD
    part = out_weight.shape[0]
    context = cache.shape[1]
    shape = jax.ShapeDtypeStruct

    ext_width = -(-(3 * n_dp + 3) // LANES) * LANES
    top_count = routes.shape[1]
    small = (query, fresh_kv, residual, routes.T, gates.T, lengths, moves)
    row, q_in, fresh_in, res_in, ext, info = call(
        functools.partial(entry_kernel, n_dp),
        [
            shape((1, 2 * model + 2 * width + ext_width), BF16),
            shape(query.shape, BF16),
            shape(fresh_kv.shape, BF16),
            shape(residual.shape, BF16),
            shape((tokens, ext_width), F32),
            shape((2 * tokens, LANES), jnp.int32),
        ],
        [spec(pltpu.HBM)] * len(small),
        scratch=[
            pltpu.SMEM((top_count, tokens), jnp.int32),
            pltpu.SMEM((top_count, tokens), F32),
            pltpu.SMEM(lengths.shape, jnp.int32),
            pltpu.SMEM(moves.shape, jnp.int32),
            pltpu.SemaphoreType.DMA((len(small),)),
        ],
        limit=4 << 20,
        flops=COVER,
        moved=tokens * model * 4,
    )(*map(in_hbm, small))
    rows = xor_exchange([row] * n_dp, "dp", n_dp)

    att, targets = call(
        functools.partial(local_kernel, n_dp, kv_heads),
        [
            shape((n_ex, tokens, part), F32),
            shape((n_dp * n_ex + 8, LANES), jnp.int32),
        ],
        [spec()] * 3 + [spec(pltpu.HBM), spec()],
        scratch=[
            pltpu.VMEM((tokens, model // HD, HD), F32),
            pltpu.SMEM(moves.shape, jnp.int32),
            pltpu.SemaphoreType.DMA(()),
        ],
        limit=4 << 20,
        flops=4 * tokens * model * context,
        moved=cache.size * 2,
    )(info, q_in, fresh_in, in_hbm(moves), cache)

    moved = call(
        functools.partial(moved_kernel, n_dp, n_ex, kv_heads, 2 * width),
        [shape((tokens, part), BF16)] * n_ex
        + [shape((tokens, model), F32), shape((tokens, ext_width), F32)],
        [spec()] * (n_dp + 5),
        scratch=[
            pltpu.VMEM(row.shape, F32),
            pltpu.VMEM((model // HD, HD), F32),
            pltpu.VMEM((n_ex, tokens, part), F32),
        ],
        limit=6 << 20,
        flops=COVER,
        moved=cache.size // tokens * 2,
    )(info, *rows, att, cache, res_in, ext)
    blocks = crossed_exchange(moved[:n_ex], n_dp, n_ex)
    base, ext_all = moved[n_ex:]

    partials = call(
        functools.partial(project_kernel, n_ex),
        [shape((tokens, model), F32)] + [shape((tokens, model), BF16)] * (n_ex - 1),
        [spec()] * (n_ex + 1),
        scratch=[pltpu.VMEM((n_ex * tokens, part), F32)],
        limit=4 << 20,
        flops=2 * n_ex * tokens * part * model,
        moved=out_weight.size * 2,
    )(*blocks, out_weight)
    partials = crossed_exchange(partials, n_dp, n_ex)

    hidden, payload = call(
        functools.partial(norm_kernel, n_ex, n_dp),
        [shape((tokens, model), F32), shape((tokens, model + ext_width), BF16)],
        [spec()] * (n_ex + 3),
        limit=4 << 20,
        flops=COVER,
        moved=tokens * model * 16,
    )(*partials, base, ext_all, norm_gain[None])
    gathered = crossed_exchange([payload] * n_ex, n_dp, n_ex)
    turns = dp_turns(n_dp)

    def over_dp(array, turn):
        return lax.ppermute(array, "dp", [(j, j ^ turn) for j in range(n_dp)])

    top = turns[-1]
    near = over_dp(payload, top)
    rest = over_dp(jnp.stack(gathered[1:]), top)
    pieces = {
        0: jnp.concatenate(gathered, axis=0),
        top: jnp.concatenate([near] + [rest[s] for s in range(n_ex - 1)], axis=0),
    }
    for turn in reversed(turns[:-1]):
        for r in list(pieces):
            pieces[r ^ turn] = over_dp(pieces[r], turn)

    group_rows = n_ex * tokens
    all_rows = n_dp * group_rows
    hidden_units = w_down.shape[1]
    weights_bytes = (w_gate.size + w_up.size + w_down.size) * 2
    done = call(
        functools.partial(expert_kernel, n_dp, n_ex, tokens),
        [shape((n_ex, tokens, model), BF16)] * n_dp + [shape((tokens, model), F32)],
        [spec()] * (n_dp + 6),
        scratch=[
            pltpu.VMEM((all_rows, model), BF16),
            pltpu.VMEM((all_rows, hidden_units), F32),
            pltpu.VMEM((all_rows, hidden_units), F32),
        ],
        limit=(8 << 20) + all_rows * model * 8,
        flops=6 * all_rows * model * hidden_units,
        moved=weights_bytes,
    )(targets, *[pieces[r] for r in range(n_dp)], w_gate, w_up, w_down, norm_gain[None], hidden)
    terms = {r: [done[r]] for r in range(n_dp)}
    reach = {0: 0}
    for i, turn in enumerate(turns):
        reach |= {r ^ turn: mark | 1 << i for r, mark in reach.items()}
    real = done[n_dp]

    def added(arrays):
        return functools.reduce(jnp.add, [array.astype(F32) for array in arrays])

    for i, turn in enumerate(turns[:-1]):
        far = {r: r ^ turn for r in terms if reach[r] >> i & 1}
        for r in sorted(far, key=lambda r: -reach[r]):
            whole = terms.pop(r)
            whole = whole[0] if len(whole) == 1 else added(whole).astype(BF16)
            terms[far[r]].append(over_dp(whole, turn))
    rest = over_dp(added([t[1:] for t in terms[top]]).astype(BF16), top)
    near = over_dp(added([t[0] for t in terms[top]]).astype(BF16), top)
    mixed = added([t[1:] for t in terms[0]] + [rest]).astype(BF16)
    staying = added([t[0] for t in terms[0]] + [near])
    back = crossed_exchange([staying] + [mixed[s] for s in range(n_ex - 1)], n_dp, n_ex)
    total = real
    for s in range(n_ex):
        total = total + back[s].astype(F32)
    return total.astype(BF16)


def solution(mesh):
    placed = (
        P(("groups", "dp", "expert"), None),
        P(("groups", "dp", "expert"), None),
        P(("groups", "dp", "expert"), None, None),
        P(("groups", "dp", "expert")),
        P("groups", None),
        P(("groups", "dp", "expert"), None),
        P("expert", None),
        P(),
        P("dp", None, "expert"),
        P("dp", None, "expert"),
        P("dp", "expert", None),
        P(("groups", "dp", "expert"), None),
        P(("groups", "dp", "expert"), None),
    )

    return jax.shard_map(
        per_device,
        mesh=mesh,
        in_specs=placed,
        out_specs=P(("groups", "dp", "expert"), None),
        check_vma=False,
    )
```

```python
import functools

import jax
import jax.numpy as jnp
from jax import lax
from jax.experimental import pallas as pl
from jax.experimental.pallas import tpu as pltpu
from jax.sharding import PartitionSpec as P


HD = 128
LANES = 128
NORM_EPS = 1e-06
F32 = jnp.float32
BF16 = jnp.bfloat16
COVER = 10**10


def dp_turns(n_dp):
    return [(1 << b) | 1 for b in range(n_dp.bit_length() - 1)]


def crossed_exchange(blocks, n_dp, n_ex):
    moved = list(blocks)
    for step in range(n_ex - 1, 0, -1):
        pairs = [
            (d * n_ex + e, (d ^ 1) * n_ex + (e ^ step)) for d in range(n_dp) for e in range(n_ex)
        ]
        moved[step] = lax.ppermute(blocks[step], ("dp", "expert"), pairs)
    return moved


def spec(space=pltpu.VMEM):
    return pl.BlockSpec(memory_space=space)


def call(kernel, outs, ins, scratch=(), limit=None, flops=0, moved=0):
    many = isinstance(outs, (list, tuple))
    return pl.pallas_call(
        kernel,
        out_shape=outs,
        in_specs=ins,
        out_specs=[spec()] * len(outs) if many else spec(),
        scratch_shapes=list(scratch),
        compiler_params=pltpu.CompilerParams(vmem_limit_bytes=limit),
        cost_estimate=pl.CostEstimate(flops=flops, bytes_accessed=moved, transcendentals=0),
    )


def attend(jobs, kv_heads):
    chains = []
    for q_row, _, q_scr, _, _, _ in jobs:
        heads = q_row.shape[1] // HD
        for h in range(heads):
            q_scr[h : h + 1, :] = q_row[:, h * HD : (h + 1) * HD].astype(F32)
    for job in jobs:
        q_row, fresh_row, q_scr, _, _, _ = job
        group = q_row.shape[1] // HD // kv_heads
        for g in range(kv_heads):
            q = q_scr[g * group : (g + 1) * group, :]
            own_key = fresh_row[:, g * HD : (g + 1) * HD].astype(F32)
            own = jnp.sum(q * own_key, axis=-1, keepdims=True) * HD ** (-0.5)
            chains.append([job, g, group, q.astype(BF16), own])
    return chains


def attend_cache(chains, kv_heads):
    width = kv_heads * HD
    all_scores = []
    for (_, _, _, cache, _, _), g, _, q, _ in chains:
        keys = cache[:, g * HD : (g + 1) * HD]
        all_scores.append(
            lax.dot_general(q, keys, (((1,), (1,)), ((), ())), preferred_element_type=F32)
            * HD ** (-0.5)
        )
    parts = []
    for scores, ((_, _, _, _, length, _), _, _, _, own) in zip(all_scores, chains):
        if length is not None:
            valid = lax.broadcasted_iota(jnp.int32, scores.shape, 1) < length
            scores = jnp.where(valid, scores, -1e30)
        top_cache = jnp.max(scores, axis=-1, keepdims=True)
        weights = jnp.exp(scores - top_cache)
        if length is not None:
            weights = jnp.where(valid, weights, 0.0)
        total = jnp.sum(weights, axis=-1, keepdims=True)
        top = jnp.maximum(top_cache, own)
        parts.append((weights.astype(BF16), total, jnp.exp(top_cache - top), jnp.exp(own - top)))
    mixes = []
    for (weights, _, _, _), ((_, _, _, cache, _, _), g, _, _, _) in zip(parts, chains):
        values = cache[:, width + g * HD : width + (g + 1) * HD]
        mixes.append(jnp.dot(weights, values, preferred_element_type=F32))
    for mixed, (_, total, cache_factor, own_factor), (job, g, group, _, _) in zip(
        mixes, parts, chains
    ):
        _, fresh_row, _, _, _, put = job
        own_value = fresh_row[:, width + g * HD : width + (g + 1) * HD].astype(F32)
        done = (cache_factor * mixed + own_factor * own_value) / (
            cache_factor * total + own_factor
        )
        for j in range(group):
            put(g * group + j, done[j : j + 1, :])


def entry_kernel(
    n_dp, q_hbm, fresh_hbm, res_hbm, routes_hbm, gates_hbm, len_hbm, moves_hbm,
    row_ref, q_ref, fresh_ref, res_ref, ext_ref, info_ref, routes, gates, lengths, moves, sems,
):
    copies = [
        pltpu.make_async_copy(source, to, sems.at[i])
        for i, (source, to) in enumerate(
            [
                (routes_hbm, routes), (gates_hbm, gates), (q_hbm, q_ref),
                (fresh_hbm, fresh_ref), (res_hbm, res_ref), (len_hbm, lengths), (moves_hbm, moves),
            ]
        )
    ]
    for copy in copies:
        copy.start()
    copies[0].wait()
    copies[1].wait()
    top, tokens = routes.shape
    lane = lax.broadcasted_iota(jnp.int32, (1, ext_ref.shape[1]), 1)
    turn = jnp.where(lane >= n_dp, 1, 0) + jnp.where(lane >= 2 * n_dp, 1, 0)
    name = lane - n_dp * turn
    for t in range(tokens):
        share = jnp.zeros(lane.shape, F32)
        for k in range(top):
            share = jnp.where(name == routes[k, t], gates[k, t], share)
        high = share.astype(BF16).astype(F32)
        middle = (share - high).astype(BF16).astype(F32)
        low = share - high - middle
        share = jnp.where(turn == 0, high, jnp.where(turn == 1, middle, low))
        ext_ref[t : t + 1, :] = jnp.where(lane < 3 * n_dp, share, 0.0)
    for copy in copies[2:]:
        copy.wait()
    for t in range(tokens):
        info_ref[t : t + 1, :] = jnp.full((1, LANES), lengths[t], jnp.int32)
    dp = lax.axis_index("dp")
    rel = moves[lax.axis_index("expert"), dp] ^ dp
    info_ref[tokens : tokens + 1, :] = jnp.full((1, LANES), rel, jnp.int32)
    model, width = q_ref.shape[1], fresh_ref.shape[1]
    row_ref[:, :model] = q_ref[0:1, :]
    row_ref[:, model : model + width] = fresh_ref[0:1, :]
    row_ref[:, model + width : 2 * model + width] = res_ref[0:1, :]
    row_ref[:, 2 * model + width :] = ext_ref[0:1, :].astype(BF16)


def local_kernel(
    n_dp, kv_heads, info_ref, q_ref, fresh_ref, moves_hbm, cache_ref,
    att_ref, to_ref, q_scr, moves, moves_sem,
):
    parts, tokens, part = att_ref.shape
    goals = pltpu.make_async_copy(moves_hbm, moves, moves_sem)
    goals.start()
    per = part // HD
    jobs = []
    for t in range(1, tokens):

        def put(head, row, t=t):
            att_ref[head // per, t : t + 1, (head % per) * HD : (head % per + 1) * HD] = row

        jobs.append(
            (
                q_ref[t : t + 1, :], fresh_ref[t : t + 1, :], q_scr.at[t], cache_ref.at[t],
                info_ref[t : t + 1, 0:1], put,
            )
        )
    attend_cache(attend(jobs, kv_heads), kv_heads)
    for s in range(parts):
        att_ref[s, 0:1, :] = jnp.zeros((1, part), F32)
    goals.wait()
    dp = lax.axis_index("dp")
    ex = lax.axis_index("expert")
    for r in range(n_dp):
        for s in range(parts):
            side = 1 if s else 0
            to = ((moves[ex ^ s, dp ^ r ^ side] ^ dp ^ side) * parts + s) * tokens
            at = r * parts + s
            to_ref[at : at + 1, :] = jnp.full((1, LANES), to, jnp.int32)
    source = 0
    for d in range(n_dp):
        source = jnp.where(moves[ex, d] == dp, d, source)
    to_ref[n_dp * parts : n_dp * parts + 1, :] = jnp.full((1, LANES), source ^ dp, jnp.int32)


def in_hbm(array):
    return pltpu.with_memory_space_constraint(array, pltpu.HBM)


def moved_kernel(n_dp, n_ex, kv_heads, width, *refs):
    info_ref = refs[0]
    rows = refs[1 : 1 + n_dp]
    att_ref, cache_ref, res_ref, ext_ref = refs[1 + n_dp : 5 + n_dp]
    outs = refs[5 + n_dp : 5 + n_dp + n_ex]
    base_ref, ext_out, row_scr, q_scr, full = refs[5 + n_dp + n_ex :]
    ex = lax.axis_index("expert")
    tokens = res_ref.shape[0]
    rel = info_ref[tokens : tokens + 1, 0:1]
    row = rows[0][...].astype(F32)
    for r in range(1, n_dp):
        row = jnp.where(rel == r, rows[r][...].astype(F32), row)
    row_scr[...] = row
    model = res_ref.shape[1]
    full[...] = att_ref[...]
    part = full.shape[2]
    per = part // HD

    def put(head, value):
        full[head // per, 0:1, (head % per) * HD : (head % per + 1) * HD] = value

    job = (row_scr[:, :model], row_scr[:, model : model + width], q_scr, cache_ref.at[0], None, put)
    attend_cache(attend([job], kv_heads), kv_heads)
    for s in range(n_ex):
        outs[s][...] = full[s ^ ex].astype(BF16)
    first = lax.broadcasted_iota(jnp.int32, (res_ref.shape[0], 1), 0) == 0
    base_ref[...] = jnp.where(first, row_scr[:, model + width : 2 * model + width], res_ref[...].astype(F32))
    ext_out[...] = jnp.where(first, row_scr[:, 2 * model + width :], ext_ref[...])


def project_kernel(n_ex, *refs):
    blocks, w_ref, outs, lhs = refs[:n_ex], refs[n_ex], refs[n_ex + 1 : -1], refs[-1]
    tokens = blocks[0].shape[0]
    for s in range(n_ex):
        lhs[s * tokens : (s + 1) * tokens, :] = blocks[s][...].astype(F32)
    left = lhs[...].astype(BF16)
    model = w_ref.shape[1]
    chunk = min(1024, model)
    for at in range(0, model, chunk):
        out = jnp.dot(left, w_ref[:, at : at + chunk], preferred_element_type=F32)
        for s in range(n_ex):
            outs[s][:, at : at + chunk] = out[s * tokens : (s + 1) * tokens, :].astype(outs[s].dtype)


def norm_kernel(n_ex, n_dp, *refs):
    parts, base_ref, ext_ref, gain_ref = refs[:n_ex], *refs[n_ex : n_ex + 3]
    hid_ref, pay_ref = refs[n_ex + 3 :]
    hidden = base_ref[...]
    for s in range(n_ex):
        hidden = hidden + parts[s][...].astype(F32)
    hid_ref[...] = hidden
    model = hidden.shape[1]
    mean = jnp.mean(hidden * hidden, axis=-1, keepdims=True) + NORM_EPS
    normed = hidden * lax.rsqrt(mean) * gain_ref[...]
    pay_ref[:, :model] = normed.astype(BF16)
    ext = ext_ref[...]
    root = jnp.sqrt(mean)
    high = root.astype(BF16).astype(F32)
    middle = (root - high).astype(BF16).astype(F32)
    low = root - high - middle
    lane = lax.broadcasted_iota(jnp.int32, ext.shape, 1)
    at = 3 * n_dp
    ext = jnp.where(lane == at, high, ext)
    ext = jnp.where(lane == at + 1, middle, ext)
    ext = jnp.where(lane == at + 2, low, ext)
    pay_ref[:, model:] = ext.astype(BF16)


def hand_kernel(source, to):
    to[...] = source[...]


def expert_kernel(n_dp, n_ex, tokens, *refs):
    to_ref = refs[0]
    pieces = refs[1 : 1 + n_dp]
    gate_ref, up_ref, down_ref, gain_ref, hid_ref = refs[1 + n_dp : 6 + n_dp]
    outs = refs[6 + n_dp : 6 + 2 * n_dp]
    real_ref, lhs, act_scr, new_scr = refs[6 + 2 * n_dp :]
    dp = lax.axis_index("dp")
    model = gain_ref.shape[1]
    rows = n_ex * tokens
    coef = []
    rel = to_ref[n_dp * n_ex : n_dp * n_ex + 1, 0:1]
    carried = jnp.zeros((1, pieces[0].shape[1]), F32)
    for r in range(n_dp):
        lhs[r * rows : (r + 1) * rows, :] = pieces[r][:, :model]
        ext = pieces[r][:, model:].astype(F32)
        lane = lax.broadcasted_iota(jnp.int32, ext.shape, 1)
        mine = (lane == dp) | (lane == dp + n_dp) | (lane == dp + 2 * n_dp)
        coef.append(jnp.sum(jnp.where(mine, ext, 0.0), axis=-1, keepdims=True))
        carried = jnp.where(rel == r, pieces[r][0:tokens, :].astype(F32)[0:1, :], carried)
    tail = carried[:, model:]
    lane = lax.broadcasted_iota(jnp.int32, tail.shape, 1)
    root = jnp.sum(
        jnp.where((lane >= 3 * n_dp) & (lane < 3 * n_dp + 3), tail, 0.0), axis=-1, keepdims=True
    )
    first = lax.broadcasted_iota(jnp.int32, (tokens, 1), 0) == 0
    real_ref[...] = jnp.where(first, carried[:, :model] * root / gain_ref[...], hid_ref[...])
    x = lhs[...]
    gate = jnp.dot(x, gate_ref[0], preferred_element_type=F32)
    up = jnp.dot(x, up_ref[0], preferred_element_type=F32)
    act = gate / (1.0 + jnp.exp(-gate)) * up
    for r in range(n_dp):
        act_scr[r * rows : (r + 1) * rows, :] = coef[r] * act[r * rows : (r + 1) * rows, :]
    new_scr[...] = act_scr[...]
    for r in range(n_dp):
        for s in range(n_ex):
            to = to_ref[r * n_ex + s : r * n_ex + s + 1, 0:1][0, 0]
            at = (r * n_ex + s) * tokens
            new_scr[pl.ds(to, 1), :] = act_scr[at : at + 1, :]
    left = new_scr[...].astype(BF16)
    chunk = min(1024, model)
    for at in range(0, model, chunk):
        out = jnp.dot(left, down_ref[0, :, at : at + chunk], preferred_element_type=F32)
        for r in range(n_dp):
            for s in range(n_ex):
                first_row = (r * n_ex + s) * tokens
                outs[r][s, :, at : at + chunk] = out[first_row : first_row + tokens, :].astype(BF16)


def per_device(
    query, fresh_kv, cache, lengths, moves, residual, out_weight, norm_gain,
    w_gate, w_up, w_down, routes, gates,
):
    n_dp = lax.axis_size("dp")
    n_ex = lax.axis_size("expert")
    tokens, model = query.shape
    width = fresh_kv.shape[1] // 2
    kv_heads = width // HD
    part = out_weight.shape[0]
    context = cache.shape[1]
    shape = jax.ShapeDtypeStruct

    ext_width = -(-(3 * n_dp + 3) // LANES) * LANES
    top_count = routes.shape[1]
    small = (query, fresh_kv, residual, routes.T, gates.T, lengths, moves)
    row, q_in, fresh_in, res_in, ext, info = call(
        functools.partial(entry_kernel, n_dp),
        [
            shape((1, 2 * model + 2 * width + ext_width), BF16),
            shape(query.shape, BF16),
            shape(fresh_kv.shape, BF16),
            shape(residual.shape, BF16),
            shape((tokens, ext_width), F32),
            shape((2 * tokens, LANES), jnp.int32),
        ],
        [spec(pltpu.HBM)] * len(small),
        scratch=[
            pltpu.SMEM((top_count, tokens), jnp.int32),
            pltpu.SMEM((top_count, tokens), F32),
            pltpu.SMEM(lengths.shape, jnp.int32),
            pltpu.SMEM(moves.shape, jnp.int32),
            pltpu.SemaphoreType.DMA((len(small),)),
        ],
        limit=4 << 20,
        flops=COVER,
        moved=tokens * model * 4,
    )(*map(in_hbm, small))
    turns = dp_turns(n_dp)

    def over_dp(array, turn):
        return lax.ppermute(array, "dp", [(j, j ^ turn) for j in range(n_dp)])

    rows = {0: row}
    for turn in reversed(turns):
        for r in list(rows):
            rows[r ^ turn] = over_dp(rows[r], turn)
    rows = [rows[r] for r in range(n_dp)]

    att, targets = call(
        functools.partial(local_kernel, n_dp, kv_heads),
        [
            shape((n_ex, tokens, part), F32),
            shape((n_dp * n_ex + 8, LANES), jnp.int32),
        ],
        [spec()] * 3 + [spec(pltpu.HBM), spec()],
        scratch=[
            pltpu.VMEM((tokens, model // HD, HD), F32),
            pltpu.SMEM(moves.shape, jnp.int32),
            pltpu.SemaphoreType.DMA(()),
        ],
        limit=4 << 20,
        flops=4 * tokens * model * context,
        moved=cache.size * 2,
    )(info, q_in, fresh_in, in_hbm(moves), cache)

    moved = call(
        functools.partial(moved_kernel, n_dp, n_ex, kv_heads, 2 * width),
        [shape((tokens, part), BF16)] * n_ex
        + [shape((tokens, model), F32), shape((tokens, ext_width), F32)],
        [spec()] * (n_dp + 5),
        scratch=[
            pltpu.VMEM(row.shape, F32),
            pltpu.VMEM((model // HD, HD), F32),
            pltpu.VMEM((n_ex, tokens, part), F32),
        ],
        limit=6 << 20,
        flops=COVER,
        moved=cache.size // tokens * 2,
    )(info, *rows, att, cache, res_in, ext)
    blocks = crossed_exchange(moved[:n_ex], n_dp, n_ex)
    base, ext_all = moved[n_ex:]

    partials = call(
        functools.partial(project_kernel, n_ex),
        [shape((tokens, model), F32)] + [shape((tokens, model), BF16)] * (n_ex - 1),
        [spec()] * (n_ex + 1),
        scratch=[pltpu.VMEM((n_ex * tokens, part), F32)],
        limit=4 << 20,
        flops=2 * n_ex * tokens * part * model,
        moved=out_weight.size * 2,
    )(*blocks, out_weight)
    partials = crossed_exchange(partials, n_dp, n_ex)

    hidden, payload = call(
        functools.partial(norm_kernel, n_ex, n_dp),
        [shape((tokens, model), F32), shape((tokens, model + ext_width), BF16)],
        [spec()] * (n_ex + 3),
        limit=4 << 20,
        flops=COVER,
        moved=tokens * model * 16,
    )(*partials, base, ext_all, norm_gain[None])
    gathered = crossed_exchange([payload] * n_ex, n_dp, n_ex)
    top, last = turns[-1], n_ex - 1
    near = over_dp(payload, top)
    handed = call(hand_kernel, shape(payload.shape, BF16), [spec()], limit=1 << 20)(gathered[last])
    far = over_dp(handed, top)
    rest = over_dp(jnp.stack(gathered[1:last]), top)
    pieces = {
        0: jnp.concatenate(gathered, axis=0),
        top: jnp.concatenate([near] + [rest[s] for s in range(n_ex - 2)] + [far], axis=0),
    }
    for turn in reversed(turns[:-1]):
        for r in list(pieces):
            pieces[r ^ turn] = over_dp(pieces[r], turn)

    group_rows = n_ex * tokens
    all_rows = n_dp * group_rows
    hidden_units = w_down.shape[1]
    weights_bytes = (w_gate.size + w_up.size + w_down.size) * 2
    done = call(
        functools.partial(expert_kernel, n_dp, n_ex, tokens),
        [shape((n_ex, tokens, model), BF16)] * n_dp + [shape((tokens, model), F32)],
        [spec()] * (n_dp + 6),
        scratch=[
            pltpu.VMEM((all_rows, model), BF16),
            pltpu.VMEM((all_rows, hidden_units), F32),
            pltpu.VMEM((all_rows, hidden_units), F32),
        ],
        limit=(8 << 20) + all_rows * model * 8,
        flops=6 * all_rows * model * hidden_units,
        moved=weights_bytes,
    )(targets, *[pieces[r] for r in range(n_dp)], w_gate, w_up, w_down, norm_gain[None], hidden)
    terms = {r: [done[r]] for r in range(n_dp)}
    reach = {0: 0}
    for i, turn in enumerate(turns):
        reach |= {r ^ turn: mark | 1 << i for r, mark in reach.items()}
    real = done[n_dp]

    def added(arrays):
        return functools.reduce(jnp.add, [array.astype(F32) for array in arrays])

    for i, turn in enumerate(turns[:-1]):
        far = {r: r ^ turn for r in terms if reach[r] >> i & 1}
        for r in sorted(far, key=lambda r: -reach[r]):
            whole = terms.pop(r)
            whole = whole[0] if len(whole) == 1 else added(whole).astype(BF16)
            terms[far[r]].append(over_dp(whole, turn))

    def across(at):
        return over_dp(added([t[at] for t in terms[top]]).astype(BF16), top)

    first = across(slice(2, n_ex))
    second = across(1)
    near = across(0)
    first = added([t[2:] for t in terms[0]] + [first]).astype(BF16)
    second = added([t[1] for t in terms[0]] + [second]).astype(BF16)
    near = added([t[0] for t in terms[0]] + [near])
    back = crossed_exchange([near, second] + [first[s] for s in range(n_ex - 2)], n_dp, n_ex)
    total = real
    for s in range(n_ex):
        total = total + back[s].astype(F32)
    return total.astype(BF16)


def solution(mesh):
    placed = (
        P(("groups", "dp", "expert"), None),
        P(("groups", "dp", "expert"), None),
        P(("groups", "dp", "expert"), None, None),
        P(("groups", "dp", "expert")),
        P("groups", None),
        P(("groups", "dp", "expert"), None),
        P("expert", None),
        P(),
        P("dp", None, "expert"),
        P("dp", None, "expert"),
        P("dp", "expert", None),
        P(("groups", "dp", "expert"), None),
        P(("groups", "dp", "expert"), None),
    )

    return jax.shard_map(
        per_device,
        mesh=mesh,
        in_specs=placed,
        out_specs=P(("groups", "dp", "expert"), None),
        check_vma=False,
    )
```

```python
import functools

import jax
import jax.numpy as jnp
from jax import lax
from jax.experimental import pallas as pl
from jax.experimental.pallas import tpu as pltpu
from jax.sharding import PartitionSpec as P


HD = 128
LANES = 128
NORM_EPS = 1e-06
F32 = jnp.float32
BF16 = jnp.bfloat16
COVER = 10**10


def dp_turns(n_dp):
    return [(1 << b) | 1 for b in range(n_dp.bit_length() - 1)]


def crossed_exchange(blocks, n_dp, n_ex):
    moved = list(blocks)
    for step in range(n_ex - 1, 0, -1):
        pairs = [
            (d * n_ex + e, (d ^ 1) * n_ex + (e ^ step)) for d in range(n_dp) for e in range(n_ex)
        ]
        moved[step] = lax.ppermute(blocks[step], ("dp", "expert"), pairs)
    return moved


def spec(space=pltpu.VMEM):
    return pl.BlockSpec(memory_space=space)


def call(kernel, outs, ins, scratch=(), limit=None, flops=0, moved=0):
    many = isinstance(outs, (list, tuple))
    return pl.pallas_call(
        kernel,
        out_shape=outs,
        in_specs=ins,
        out_specs=[spec()] * len(outs) if many else spec(),
        scratch_shapes=list(scratch),
        compiler_params=pltpu.CompilerParams(vmem_limit_bytes=limit),
        cost_estimate=pl.CostEstimate(flops=flops, bytes_accessed=moved, transcendentals=0),
    )


def attend(jobs, kv_heads):
    chains = []
    for q_row, _, q_scr, _, _, _ in jobs:
        heads = q_row.shape[1] // HD
        for h in range(heads):
            q_scr[h : h + 1, :] = q_row[:, h * HD : (h + 1) * HD].astype(F32)
    for job in jobs:
        q_row, fresh_row, q_scr, _, _, _ = job
        group = q_row.shape[1] // HD // kv_heads
        for g in range(kv_heads):
            q = q_scr[g * group : (g + 1) * group, :]
            own_key = fresh_row[:, g * HD : (g + 1) * HD].astype(F32)
            own = jnp.sum(q * own_key, axis=-1, keepdims=True) * HD ** (-0.5)
            chains.append([job, g, group, q.astype(BF16), own])
    return chains


def attend_cache(chains, kv_heads):
    width = kv_heads * HD
    all_scores = []
    for (_, _, _, cache, _, _), g, _, q, _ in chains:
        keys = cache[:, g * HD : (g + 1) * HD]
        all_scores.append(
            lax.dot_general(q, keys, (((1,), (1,)), ((), ())), preferred_element_type=F32)
            * HD ** (-0.5)
        )
    parts = []
    for scores, ((_, _, _, _, length, _), _, _, _, own) in zip(all_scores, chains):
        if length is not None:
            valid = lax.broadcasted_iota(jnp.int32, scores.shape, 1) < length
            scores = jnp.where(valid, scores, -1e30)
        top_cache = jnp.max(scores, axis=-1, keepdims=True)
        weights = jnp.exp(scores - top_cache)
        if length is not None:
            weights = jnp.where(valid, weights, 0.0)
        total = jnp.sum(weights, axis=-1, keepdims=True)
        top = jnp.maximum(top_cache, own)
        parts.append((weights.astype(BF16), total, jnp.exp(top_cache - top), jnp.exp(own - top)))
    mixes = []
    for (weights, _, _, _), ((_, _, _, cache, _, _), g, _, _, _) in zip(parts, chains):
        values = cache[:, width + g * HD : width + (g + 1) * HD]
        mixes.append(jnp.dot(weights, values, preferred_element_type=F32))
    for mixed, (_, total, cache_factor, own_factor), (job, g, group, _, _) in zip(
        mixes, parts, chains
    ):
        _, fresh_row, _, _, _, put = job
        own_value = fresh_row[:, width + g * HD : width + (g + 1) * HD].astype(F32)
        done = (cache_factor * mixed + own_factor * own_value) / (
            cache_factor * total + own_factor
        )
        for j in range(group):
            put(g * group + j, done[j : j + 1, :])


def entry_kernel(
    n_dp, q_hbm, fresh_hbm, res_hbm, routes_hbm, gates_hbm, len_hbm, moves_hbm,
    row_ref, q_ref, fresh_ref, res_ref, ext_ref, info_ref, routes, gates, lengths, moves, sems,
):
    copies = [
        pltpu.make_async_copy(source, to, sems.at[i])
        for i, (source, to) in enumerate(
            [
                (routes_hbm, routes), (gates_hbm, gates), (q_hbm, q_ref),
                (fresh_hbm, fresh_ref), (res_hbm, res_ref), (len_hbm, lengths), (moves_hbm, moves),
            ]
        )
    ]
    for copy in copies:
        copy.start()
    copies[0].wait()
    copies[1].wait()
    top, tokens = routes.shape
    lane = lax.broadcasted_iota(jnp.int32, (1, ext_ref.shape[1]), 1)
    turn = jnp.where(lane >= n_dp, 1, 0) + jnp.where(lane >= 2 * n_dp, 1, 0)
    name = lane - n_dp * turn
    for t in range(tokens):
        share = jnp.zeros(lane.shape, F32)
        for k in range(top):
            share = jnp.where(name == routes[k, t], gates[k, t], share)
        high = share.astype(BF16).astype(F32)
        middle = (share - high).astype(BF16).astype(F32)
        low = share - high - middle
        share = jnp.where(turn == 0, high, jnp.where(turn == 1, middle, low))
        ext_ref[t : t + 1, :] = jnp.where(lane < 3 * n_dp, share, 0.0)
    for copy in copies[2:]:
        copy.wait()
    for t in range(tokens):
        info_ref[t : t + 1, :] = jnp.full((1, LANES), lengths[t], jnp.int32)
    dp = lax.axis_index("dp")
    rel = moves[lax.axis_index("expert"), dp] ^ dp
    info_ref[tokens : tokens + 1, :] = jnp.full((1, LANES), rel, jnp.int32)
    model, width = q_ref.shape[1], fresh_ref.shape[1]
    row_ref[:, :model] = q_ref[0:1, :]
    row_ref[:, model : model + width] = fresh_ref[0:1, :]
    row_ref[:, model + width : 2 * model + width] = res_ref[0:1, :]
    row_ref[:, 2 * model + width :] = ext_ref[0:1, :].astype(BF16)


def local_kernel(
    n_dp, kv_heads, info_ref, q_ref, fresh_ref, moves_hbm, cache_ref,
    att_ref, to_ref, q_scr, moves, moves_sem,
):
    parts, tokens, part = att_ref.shape
    goals = pltpu.make_async_copy(moves_hbm, moves, moves_sem)
    goals.start()
    per = part // HD
    jobs = []
    for t in range(1, tokens):

        def put(head, row, t=t):
            att_ref[head // per, t : t + 1, (head % per) * HD : (head % per + 1) * HD] = row

        jobs.append(
            (
                q_ref[t : t + 1, :], fresh_ref[t : t + 1, :], q_scr.at[t], cache_ref.at[t],
                info_ref[t : t + 1, 0:1], put,
            )
        )
    attend_cache(attend(jobs, kv_heads), kv_heads)
    for s in range(parts):
        att_ref[s, 0:1, :] = jnp.zeros((1, part), F32)
    goals.wait()
    dp = lax.axis_index("dp")
    ex = lax.axis_index("expert")
    for r in range(n_dp):
        for s in range(parts):
            side = 1 if s else 0
            to = ((moves[ex ^ s, dp ^ r ^ side] ^ dp ^ side) * parts + s) * tokens
            at = r * parts + s
            to_ref[at : at + 1, :] = jnp.full((1, LANES), to, jnp.int32)
    source = 0
    for d in range(n_dp):
        source = jnp.where(moves[ex, d] == dp, d, source)
    to_ref[n_dp * parts : n_dp * parts + 1, :] = jnp.full((1, LANES), source ^ dp, jnp.int32)


def in_hbm(array):
    return pltpu.with_memory_space_constraint(array, pltpu.HBM)


def moved_kernel(n_dp, n_ex, kv_heads, width, *refs):
    info_ref = refs[0]
    rows = refs[1 : 1 + n_dp]
    att_ref, cache_ref, res_ref, ext_ref = refs[1 + n_dp : 5 + n_dp]
    outs = refs[5 + n_dp : 5 + n_dp + n_ex]
    base_ref, ext_out, row_scr, q_scr, full = refs[5 + n_dp + n_ex :]
    ex = lax.axis_index("expert")
    tokens = res_ref.shape[0]
    rel = info_ref[tokens : tokens + 1, 0:1]
    row = rows[0][...].astype(F32)
    for r in range(1, n_dp):
        row = jnp.where(rel == r, rows[r][...].astype(F32), row)
    row_scr[...] = row
    model = res_ref.shape[1]
    full[...] = att_ref[...]
    part = full.shape[2]
    per = part // HD

    def put(head, value):
        full[head // per, 0:1, (head % per) * HD : (head % per + 1) * HD] = value

    job = (row_scr[:, :model], row_scr[:, model : model + width], q_scr, cache_ref.at[0], None, put)
    attend_cache(attend([job], kv_heads), kv_heads)
    for s in range(n_ex):
        outs[s][...] = full[s ^ ex].astype(BF16)
    first = lax.broadcasted_iota(jnp.int32, (res_ref.shape[0], 1), 0) == 0
    base_ref[...] = jnp.where(first, row_scr[:, model + width : 2 * model + width], res_ref[...].astype(F32))
    ext_out[...] = jnp.where(first, row_scr[:, 2 * model + width :], ext_ref[...])


def project_kernel(n_ex, *refs):
    blocks, w_ref, outs, lhs = refs[:n_ex], refs[n_ex], refs[n_ex + 1 : -1], refs[-1]
    tokens = blocks[0].shape[0]
    for s in range(n_ex):
        lhs[s * tokens : (s + 1) * tokens, :] = blocks[s][...].astype(F32)
    left = lhs[...].astype(BF16)
    model = w_ref.shape[1]
    chunk = min(1024, model)
    for at in range(0, model, chunk):
        out = jnp.dot(left, w_ref[:, at : at + chunk], preferred_element_type=F32)
        for s in range(n_ex):
            outs[s][:, at : at + chunk] = out[s * tokens : (s + 1) * tokens, :].astype(outs[s].dtype)


def norm_kernel(n_ex, n_dp, *refs):
    parts, base_ref, ext_ref, gain_ref = refs[:n_ex], *refs[n_ex : n_ex + 3]
    hid_ref, pay_ref = refs[n_ex + 3 :]
    hidden = base_ref[...]
    for s in range(n_ex):
        hidden = hidden + parts[s][...].astype(F32)
    hid_ref[...] = hidden
    model = hidden.shape[1]
    mean = jnp.mean(hidden * hidden, axis=-1, keepdims=True) + NORM_EPS
    normed = hidden * lax.rsqrt(mean) * gain_ref[...]
    pay_ref[:, :model] = normed.astype(BF16)
    ext = ext_ref[...]
    root = jnp.sqrt(mean)
    high = root.astype(BF16).astype(F32)
    middle = (root - high).astype(BF16).astype(F32)
    low = root - high - middle
    lane = lax.broadcasted_iota(jnp.int32, ext.shape, 1)
    at = 3 * n_dp
    ext = jnp.where(lane == at, high, ext)
    ext = jnp.where(lane == at + 1, middle, ext)
    ext = jnp.where(lane == at + 2, low, ext)
    pay_ref[:, model:] = ext.astype(BF16)


def add_kernel(at, block_ref, *refs):
    total = block_ref[...].astype(F32)
    for ref in refs[:-1]:
        total = total + ref[at].astype(F32)
    refs[-1][...] = total.astype(refs[-1].dtype)


def hand_kernel(source, to):
    to[...] = source[...]


def expert_kernel(n_dp, n_ex, tokens, *refs):
    to_ref = refs[0]
    pieces = refs[1 : 1 + n_dp]
    gate_ref, up_ref, down_ref, gain_ref, hid_ref = refs[1 + n_dp : 6 + n_dp]
    outs = refs[6 + n_dp : 6 + 2 * n_dp]
    real_ref, lhs, act_scr, new_scr = refs[6 + 2 * n_dp :]
    dp = lax.axis_index("dp")
    model = gain_ref.shape[1]
    rows = n_ex * tokens
    coef = []
    rel = to_ref[n_dp * n_ex : n_dp * n_ex + 1, 0:1]
    carried = jnp.zeros((1, pieces[0].shape[1]), F32)
    for r in range(n_dp):
        lhs[r * rows : (r + 1) * rows, :] = pieces[r][:, :model]
        ext = pieces[r][:, model:].astype(F32)
        lane = lax.broadcasted_iota(jnp.int32, ext.shape, 1)
        mine = (lane == dp) | (lane == dp + n_dp) | (lane == dp + 2 * n_dp)
        coef.append(jnp.sum(jnp.where(mine, ext, 0.0), axis=-1, keepdims=True))
        carried = jnp.where(rel == r, pieces[r][0:tokens, :].astype(F32)[0:1, :], carried)
    tail = carried[:, model:]
    lane = lax.broadcasted_iota(jnp.int32, tail.shape, 1)
    root = jnp.sum(
        jnp.where((lane >= 3 * n_dp) & (lane < 3 * n_dp + 3), tail, 0.0), axis=-1, keepdims=True
    )
    first = lax.broadcasted_iota(jnp.int32, (tokens, 1), 0) == 0
    real_ref[...] = jnp.where(first, carried[:, :model] * root / gain_ref[...], hid_ref[...])
    x = lhs[...]
    gate = jnp.dot(x, gate_ref[0], preferred_element_type=F32)
    up = jnp.dot(x, up_ref[0], preferred_element_type=F32)
    act = gate / (1.0 + jnp.exp(-gate)) * up
    for r in range(n_dp):
        act_scr[r * rows : (r + 1) * rows, :] = coef[r] * act[r * rows : (r + 1) * rows, :]
    new_scr[...] = act_scr[...]
    for r in range(n_dp):
        for s in range(n_ex):
            to = to_ref[r * n_ex + s : r * n_ex + s + 1, 0:1][0, 0]
            at = (r * n_ex + s) * tokens
            new_scr[pl.ds(to, 1), :] = act_scr[at : at + 1, :]
    left = new_scr[...].astype(BF16)
    chunk = min(1024, model)
    for at in range(0, model, chunk):
        out = jnp.dot(left, down_ref[0, :, at : at + chunk], preferred_element_type=F32)
        for r in range(n_dp):
            for s in range(n_ex):
                first_row = (r * n_ex + s) * tokens
                outs[r][s, :, at : at + chunk] = out[first_row : first_row + tokens, :].astype(BF16)


def per_device(
    query, fresh_kv, cache, lengths, moves, residual, out_weight, norm_gain,
    w_gate, w_up, w_down, routes, gates,
):
    n_dp = lax.axis_size("dp")
    n_ex = lax.axis_size("expert")
    tokens, model = query.shape
    width = fresh_kv.shape[1] // 2
    kv_heads = width // HD
    part = out_weight.shape[0]
    context = cache.shape[1]
    shape = jax.ShapeDtypeStruct

    ext_width = -(-(3 * n_dp + 3) // LANES) * LANES
    top_count = routes.shape[1]
    small = (query, fresh_kv, residual, routes.T, gates.T, lengths, moves)
    row, q_in, fresh_in, res_in, ext, info = call(
        functools.partial(entry_kernel, n_dp),
        [
            shape((1, 2 * model + 2 * width + ext_width), BF16),
            shape(query.shape, BF16),
            shape(fresh_kv.shape, BF16),
            shape(residual.shape, BF16),
            shape((tokens, ext_width), F32),
            shape((2 * tokens, LANES), jnp.int32),
        ],
        [spec(pltpu.HBM)] * len(small),
        scratch=[
            pltpu.SMEM((top_count, tokens), jnp.int32),
            pltpu.SMEM((top_count, tokens), F32),
            pltpu.SMEM(lengths.shape, jnp.int32),
            pltpu.SMEM(moves.shape, jnp.int32),
            pltpu.SemaphoreType.DMA((len(small),)),
        ],
        limit=4 << 20,
        flops=COVER,
        moved=tokens * model * 4,
    )(*map(in_hbm, small))
    turns = dp_turns(n_dp)

    def over_dp(array, turn):
        return lax.ppermute(array, "dp", [(j, j ^ turn) for j in range(n_dp)])

    rows = [row] + [over_dp(row, r) for r in range(n_dp - 1, 0, -1)][::-1]

    att, targets = call(
        functools.partial(local_kernel, n_dp, kv_heads),
        [
            shape((n_ex, tokens, part), F32),
            shape((n_dp * n_ex + 8, LANES), jnp.int32),
        ],
        [spec()] * 3 + [spec(pltpu.HBM), spec()],
        scratch=[
            pltpu.VMEM((tokens, model // HD, HD), F32),
            pltpu.SMEM(moves.shape, jnp.int32),
            pltpu.SemaphoreType.DMA(()),
        ],
        limit=4 << 20,
        flops=4 * tokens * model * context,
        moved=cache.size * 2,
    )(info, q_in, fresh_in, in_hbm(moves), cache)

    moved = call(
        functools.partial(moved_kernel, n_dp, n_ex, kv_heads, 2 * width),
        [shape((tokens, part), BF16)] * n_ex
        + [shape((tokens, model), F32), shape((tokens, ext_width), F32)],
        [spec()] * (n_dp + 5),
        scratch=[
            pltpu.VMEM(row.shape, F32),
            pltpu.VMEM((model // HD, HD), F32),
            pltpu.VMEM((n_ex, tokens, part), F32),
        ],
        limit=6 << 20,
        flops=COVER,
        moved=cache.size // tokens * 2,
    )(info, *rows, att, cache, res_in, ext)
    blocks = crossed_exchange(moved[:n_ex], n_dp, n_ex)
    base, ext_all = moved[n_ex:]

    partials = call(
        functools.partial(project_kernel, n_ex),
        [shape((tokens, model), F32)] + [shape((tokens, model), BF16)] * (n_ex - 1),
        [spec()] * (n_ex + 1),
        scratch=[pltpu.VMEM((n_ex * tokens, part), F32)],
        limit=4 << 20,
        flops=2 * n_ex * tokens * part * model,
        moved=out_weight.size * 2,
    )(*blocks, out_weight)
    partials = crossed_exchange(partials, n_dp, n_ex)

    hidden, payload = call(
        functools.partial(norm_kernel, n_ex, n_dp),
        [shape((tokens, model), F32), shape((tokens, model + ext_width), BF16)],
        [spec()] * (n_ex + 3),
        limit=4 << 20,
        flops=COVER,
        moved=tokens * model * 16,
    )(*partials, base, ext_all, norm_gain[None])
    gathered = crossed_exchange([payload] * n_ex, n_dp, n_ex)
    top, last = turns[-1], n_ex - 1
    near = over_dp(payload, top)
    handed = call(hand_kernel, shape(payload.shape, BF16), [spec()], limit=1 << 20)(gathered[last])
    far = over_dp(handed, top)
    rest = over_dp(jnp.stack(gathered[1:last]), top)
    pieces = {
        0: jnp.concatenate(gathered, axis=0),
        top: jnp.concatenate([near] + [rest[s] for s in range(n_ex - 2)] + [far], axis=0),
    }
    for turn in reversed(turns[:-1]):
        for r in list(pieces):
            pieces[r ^ turn] = over_dp(pieces[r], turn)

    group_rows = n_ex * tokens
    all_rows = n_dp * group_rows
    hidden_units = w_down.shape[1]
    weights_bytes = (w_gate.size + w_up.size + w_down.size) * 2
    done = call(
        functools.partial(expert_kernel, n_dp, n_ex, tokens),
        [shape((n_ex, tokens, model), BF16)] * n_dp + [shape((tokens, model), F32)],
        [spec()] * (n_dp + 6),
        scratch=[
            pltpu.VMEM((all_rows, model), BF16),
            pltpu.VMEM((all_rows, hidden_units), F32),
            pltpu.VMEM((all_rows, hidden_units), F32),
        ],
        limit=(8 << 20) + all_rows * model * 8,
        flops=6 * all_rows * model * hidden_units,
        moved=weights_bytes,
    )(targets, *[pieces[r] for r in range(n_dp)], w_gate, w_up, w_down, norm_gain[None], hidden)
    terms = {r: [done[r]] for r in range(n_dp)}
    reach = {0: 0}
    for i, turn in enumerate(turns):
        reach |= {r ^ turn: mark | 1 << i for r, mark in reach.items()}
    real = done[n_dp]

    def added(arrays):
        return functools.reduce(jnp.add, [array.astype(F32) for array in arrays])

    for i, turn in enumerate(turns[:-1]):
        far = {r: r ^ turn for r in terms if reach[r] >> i & 1}
        for r in sorted(far, key=lambda r: -reach[r]):
            whole = terms.pop(r)
            whole = whole[0] if len(whole) == 1 else added(whole).astype(BF16)
            terms[far[r]].append(over_dp(whole, turn))

    def across(at):
        return over_dp(added([t[at] for t in terms[top]]).astype(BF16), top)

    arrived = [across(s) for s in range(n_ex)]
    mixed = [
        call(
            functools.partial(add_kernel, s),
            shape((tokens, model), BF16 if s else F32),
            [spec()] * (len(terms[0]) + 1),
            limit=1 << 20,
        )(arrived[s], *terms[0])
        for s in range(n_ex)
    ]
    back = crossed_exchange(mixed, n_dp, n_ex)
    total = real
    for s in range(n_ex):
        total = total + back[s].astype(F32)
    return total.astype(BF16)


def solution(mesh):
    placed = (
        P(("groups", "dp", "expert"), None),
        P(("groups", "dp", "expert"), None),
        P(("groups", "dp", "expert"), None, None),
        P(("groups", "dp", "expert")),
        P("groups", None),
        P(("groups", "dp", "expert"), None),
        P("expert", None),
        P(),
        P("dp", None, "expert"),
        P("dp", None, "expert"),
        P("dp", "expert", None),
        P(("groups", "dp", "expert"), None),
        P(("groups", "dp", "expert"), None),
    )

    return jax.shard_map(
        per_device,
        mesh=mesh,
        in_specs=placed,
        out_specs=P(("groups", "dp", "expert"), None),
        check_vma=False,
    )
```

```python
import functools

import jax
import jax.numpy as jnp
from jax import lax
from jax.experimental import pallas as pl
from jax.experimental.pallas import tpu as pltpu
from jax.sharding import PartitionSpec as P


HD = 128
LANES = 128
NORM_EPS = 1e-06
F32 = jnp.float32
BF16 = jnp.bfloat16
COVER = 10**10


def dp_turns(n_dp):
    return [(1 << b) | 1 for b in range(n_dp.bit_length() - 1)]


def crossed_exchange(blocks, n_dp, n_ex):
    moved = list(blocks)
    for step in range(n_ex - 1, 0, -1):
        pairs = [
            (d * n_ex + e, (d ^ 1) * n_ex + (e ^ step)) for d in range(n_dp) for e in range(n_ex)
        ]
        moved[step] = lax.ppermute(blocks[step], ("dp", "expert"), pairs)
    return moved


def spec(space=pltpu.VMEM):
    return pl.BlockSpec(memory_space=space)


def call(kernel, outs, ins, scratch=(), limit=None, flops=0, moved=0):
    many = isinstance(outs, (list, tuple))
    return pl.pallas_call(
        kernel,
        out_shape=outs,
        in_specs=ins,
        out_specs=[spec()] * len(outs) if many else spec(),
        scratch_shapes=list(scratch),
        compiler_params=pltpu.CompilerParams(vmem_limit_bytes=limit),
        cost_estimate=pl.CostEstimate(flops=flops, bytes_accessed=moved, transcendentals=0),
    )


def attend(jobs, kv_heads):
    chains = []
    for q_row, _, q_scr, _, _, _ in jobs:
        heads = q_row.shape[1] // HD
        for h in range(heads):
            q_scr[h : h + 1, :] = q_row[:, h * HD : (h + 1) * HD].astype(F32)
    for job in jobs:
        q_row, fresh_row, q_scr, _, _, _ = job
        group = q_row.shape[1] // HD // kv_heads
        for g in range(kv_heads):
            q = q_scr[g * group : (g + 1) * group, :]
            own_key = fresh_row[:, g * HD : (g + 1) * HD].astype(F32)
            own = jnp.sum(q * own_key, axis=-1, keepdims=True) * HD ** (-0.5)
            chains.append([job, g, group, q.astype(BF16), own])
    return chains


def attend_cache(chains, kv_heads):
    width = kv_heads * HD
    all_scores = []
    for (_, _, _, cache, _, _), g, _, q, _ in chains:
        keys = cache[:, g * HD : (g + 1) * HD]
        all_scores.append(
            lax.dot_general(q, keys, (((1,), (1,)), ((), ())), preferred_element_type=F32)
            * HD ** (-0.5)
        )
    parts = []
    for scores, ((_, _, _, _, length, _), _, _, _, own) in zip(all_scores, chains):
        if length is not None:
            valid = lax.broadcasted_iota(jnp.int32, scores.shape, 1) < length
            scores = jnp.where(valid, scores, -1e30)
        top_cache = jnp.max(scores, axis=-1, keepdims=True)
        weights = jnp.exp(scores - top_cache)
        if length is not None:
            weights = jnp.where(valid, weights, 0.0)
        total = jnp.sum(weights, axis=-1, keepdims=True)
        top = jnp.maximum(top_cache, own)
        parts.append((weights.astype(BF16), total, jnp.exp(top_cache - top), jnp.exp(own - top)))
    mixes = []
    for (weights, _, _, _), ((_, _, _, cache, _, _), g, _, _, _) in zip(parts, chains):
        values = cache[:, width + g * HD : width + (g + 1) * HD]
        mixes.append(jnp.dot(weights, values, preferred_element_type=F32))
    for mixed, (_, total, cache_factor, own_factor), (job, g, group, _, _) in zip(
        mixes, parts, chains
    ):
        _, fresh_row, _, _, _, put = job
        own_value = fresh_row[:, width + g * HD : width + (g + 1) * HD].astype(F32)
        done = (cache_factor * mixed + own_factor * own_value) / (
            cache_factor * total + own_factor
        )
        for j in range(group):
            put(g * group + j, done[j : j + 1, :])


def entry_kernel(
    n_dp, q_hbm, fresh_hbm, res_hbm, routes_hbm, gates_hbm, len_hbm, moves_hbm,
    row_ref, q_ref, fresh_ref, res_ref, ext_ref, info_ref, routes, gates, lengths, moves, sems,
):
    copies = [
        pltpu.make_async_copy(source, to, sems.at[i])
        for i, (source, to) in enumerate(
            [
                (routes_hbm, routes), (gates_hbm, gates), (q_hbm, q_ref),
                (fresh_hbm, fresh_ref), (res_hbm, res_ref), (len_hbm, lengths), (moves_hbm, moves),
            ]
        )
    ]
    for copy in copies:
        copy.start()
    copies[0].wait()
    copies[1].wait()
    top, tokens = routes.shape
    lane = lax.broadcasted_iota(jnp.int32, (1, ext_ref.shape[1]), 1)
    turn = jnp.where(lane >= n_dp, 1, 0) + jnp.where(lane >= 2 * n_dp, 1, 0)
    name = lane - n_dp * turn
    for t in range(tokens):
        share = jnp.zeros(lane.shape, F32)
        for k in range(top):
            share = jnp.where(name == routes[k, t], gates[k, t], share)
        high = share.astype(BF16).astype(F32)
        middle = (share - high).astype(BF16).astype(F32)
        low = share - high - middle
        share = jnp.where(turn == 0, high, jnp.where(turn == 1, middle, low))
        ext_ref[t : t + 1, :] = jnp.where(lane < 3 * n_dp, share, 0.0)
    for copy in copies[2:]:
        copy.wait()
    for t in range(tokens):
        info_ref[t : t + 1, :] = jnp.full((1, LANES), lengths[t], jnp.int32)
    dp = lax.axis_index("dp")
    rel = moves[lax.axis_index("expert"), dp] ^ dp
    info_ref[tokens : tokens + 1, :] = jnp.full((1, LANES), rel, jnp.int32)
    model, width = q_ref.shape[1], fresh_ref.shape[1]
    row_ref[:, :model] = q_ref[0:1, :]
    row_ref[:, model : model + width] = fresh_ref[0:1, :]
    row_ref[:, model + width : 2 * model + width] = res_ref[0:1, :]
    row_ref[:, 2 * model + width :] = ext_ref[0:1, :].astype(BF16)


def local_kernel(
    n_dp, kv_heads, info_ref, q_ref, fresh_ref, moves_hbm, cache_ref,
    att_ref, to_ref, q_scr, moves, moves_sem,
):
    parts, tokens, part = att_ref.shape
    goals = pltpu.make_async_copy(moves_hbm, moves, moves_sem)
    goals.start()
    per = part // HD
    jobs = []
    for t in range(1, tokens):

        def put(head, row, t=t):
            att_ref[head // per, t : t + 1, (head % per) * HD : (head % per + 1) * HD] = row

        jobs.append(
            (
                q_ref[t : t + 1, :], fresh_ref[t : t + 1, :], q_scr.at[t], cache_ref.at[t],
                info_ref[t : t + 1, 0:1], put,
            )
        )
    attend_cache(attend(jobs, kv_heads), kv_heads)
    for s in range(parts):
        att_ref[s, 0:1, :] = jnp.zeros((1, part), F32)
    goals.wait()
    dp = lax.axis_index("dp")
    ex = lax.axis_index("expert")
    for r in range(n_dp):
        for s in range(parts):
            side = 1 if s else 0
            to = ((moves[ex ^ s, dp ^ r ^ side] ^ dp ^ side) * parts + s) * tokens
            at = r * parts + s
            to_ref[at : at + 1, :] = jnp.full((1, LANES), to, jnp.int32)
    source = 0
    for d in range(n_dp):
        source = jnp.where(moves[ex, d] == dp, d, source)
    to_ref[n_dp * parts : n_dp * parts + 1, :] = jnp.full((1, LANES), source ^ dp, jnp.int32)


def in_hbm(array):
    return pltpu.with_memory_space_constraint(array, pltpu.HBM)


def moved_kernel(n_dp, n_ex, kv_heads, width, *refs):
    info_ref = refs[0]
    rows = refs[1 : 1 + n_dp]
    att_ref, cache_ref, res_ref, ext_ref = refs[1 + n_dp : 5 + n_dp]
    outs = refs[5 + n_dp : 5 + n_dp + n_ex]
    base_ref, ext_out, row_scr, q_scr, full = refs[5 + n_dp + n_ex :]
    ex = lax.axis_index("expert")
    tokens = res_ref.shape[0]
    rel = info_ref[tokens : tokens + 1, 0:1]
    row = rows[0][...].astype(F32)
    for r in range(1, n_dp):
        row = jnp.where(rel == r, rows[r][...].astype(F32), row)
    row_scr[...] = row
    model = res_ref.shape[1]
    full[...] = att_ref[...]
    part = full.shape[2]
    per = part // HD

    def put(head, value):
        full[head // per, 0:1, (head % per) * HD : (head % per + 1) * HD] = value

    job = (row_scr[:, :model], row_scr[:, model : model + width], q_scr, cache_ref.at[0], None, put)
    attend_cache(attend([job], kv_heads), kv_heads)
    for s in range(n_ex):
        outs[s][...] = full[s ^ ex].astype(BF16)
    first = lax.broadcasted_iota(jnp.int32, (res_ref.shape[0], 1), 0) == 0
    base_ref[...] = jnp.where(first, row_scr[:, model + width : 2 * model + width], res_ref[...].astype(F32))
    ext_out[...] = jnp.where(first, row_scr[:, 2 * model + width :], ext_ref[...])


def project_kernel(n_ex, *refs):
    blocks, w_ref, outs, lhs = refs[:n_ex], refs[n_ex], refs[n_ex + 1 : -1], refs[-1]
    tokens = blocks[0].shape[0]
    for s in range(n_ex):
        lhs[s * tokens : (s + 1) * tokens, :] = blocks[s][...].astype(F32)
    left = lhs[...].astype(BF16)
    model = w_ref.shape[1]
    chunk = min(1024, model)
    for at in range(0, model, chunk):
        out = jnp.dot(left, w_ref[:, at : at + chunk], preferred_element_type=F32)
        for s in range(n_ex):
            outs[s][:, at : at + chunk] = out[s * tokens : (s + 1) * tokens, :].astype(outs[s].dtype)


def norm_kernel(n_ex, n_dp, *refs):
    parts, base_ref, ext_ref, gain_ref = refs[:n_ex], *refs[n_ex : n_ex + 3]
    hid_ref, pay_ref = refs[n_ex + 3 :]
    hidden = base_ref[...]
    for s in range(n_ex):
        hidden = hidden + parts[s][...].astype(F32)
    hid_ref[...] = hidden
    model = hidden.shape[1]
    mean = jnp.mean(hidden * hidden, axis=-1, keepdims=True) + NORM_EPS
    normed = hidden * lax.rsqrt(mean) * gain_ref[...]
    pay_ref[:, :model] = normed.astype(BF16)
    ext = ext_ref[...]
    root = jnp.sqrt(mean)
    high = root.astype(BF16).astype(F32)
    middle = (root - high).astype(BF16).astype(F32)
    low = root - high - middle
    lane = lax.broadcasted_iota(jnp.int32, ext.shape, 1)
    at = 3 * n_dp
    ext = jnp.where(lane == at, high, ext)
    ext = jnp.where(lane == at + 1, middle, ext)
    ext = jnp.where(lane == at + 2, low, ext)
    pay_ref[:, model:] = ext.astype(BF16)


def add_kernel(at, block, block_ref, *refs):
    total = block_ref[block].astype(F32)
    for ref in refs[:-1]:
        total = total + ref[at].astype(F32)
    refs[-1][...] = total.astype(refs[-1].dtype)


def middle_kernel(*refs):
    blocks, others, own = refs[:-2], refs[-2], refs[-1]
    for to, at in ((others, 1), (own, 0)):
        for i in range(to.shape[0]):
            total = blocks[0][at + i].astype(F32)
            for block in blocks[1:]:
                total = total + block[at + i].astype(F32)
            to[i] = total.astype(to.dtype)


def hand_kernel(source, to):
    to[...] = source[...]


def expert_kernel(n_dp, n_ex, tokens, *refs):
    to_ref = refs[0]
    pieces = refs[1 : 1 + n_dp]
    gate_ref, up_ref, down_ref, gain_ref, hid_ref = refs[1 + n_dp : 6 + n_dp]
    bodies, heads = refs[6 + n_dp : 6 + 2 * n_dp], refs[6 + 2 * n_dp : 6 + 3 * n_dp]
    real_ref, lhs, act_scr, new_scr = refs[6 + 3 * n_dp :]
    dp = lax.axis_index("dp")
    model = gain_ref.shape[1]
    rows = n_ex * tokens
    coef = []
    rel = to_ref[n_dp * n_ex : n_dp * n_ex + 1, 0:1]
    carried = jnp.zeros((1, pieces[0].shape[1]), F32)
    for r in range(n_dp):
        lhs[r * rows : (r + 1) * rows, :] = pieces[r][:, :model]
        ext = pieces[r][:, model:].astype(F32)
        lane = lax.broadcasted_iota(jnp.int32, ext.shape, 1)
        mine = (lane == dp) | (lane == dp + n_dp) | (lane == dp + 2 * n_dp)
        coef.append(jnp.sum(jnp.where(mine, ext, 0.0), axis=-1, keepdims=True))
        carried = jnp.where(rel == r, pieces[r][0:tokens, :].astype(F32)[0:1, :], carried)
    tail = carried[:, model:]
    lane = lax.broadcasted_iota(jnp.int32, tail.shape, 1)
    root = jnp.sum(
        jnp.where((lane >= 3 * n_dp) & (lane < 3 * n_dp + 3), tail, 0.0), axis=-1, keepdims=True
    )
    first = lax.broadcasted_iota(jnp.int32, (tokens, 1), 0) == 0
    real_ref[...] = jnp.where(first, carried[:, :model] * root / gain_ref[...], hid_ref[...])
    x = lhs[...]
    gate = jnp.dot(x, gate_ref[0], preferred_element_type=F32)
    up = jnp.dot(x, up_ref[0], preferred_element_type=F32)
    act = gate / (1.0 + jnp.exp(-gate)) * up
    for r in range(n_dp):
        act_scr[r * rows : (r + 1) * rows, :] = coef[r] * act[r * rows : (r + 1) * rows, :]
    new_scr[...] = act_scr[...]
    for r in range(n_dp):
        for s in range(n_ex):
            to = to_ref[r * n_ex + s : r * n_ex + s + 1, 0:1][0, 0]
            at = (r * n_ex + s) * tokens
            new_scr[pl.ds(to, 1), :] = act_scr[at : at + 1, :]
    left = new_scr[...].astype(BF16)
    chunk = min(1024, model)
    for at in range(0, model, chunk):
        out = jnp.dot(left, down_ref[0, :, at : at + chunk], preferred_element_type=F32)
        for r in range(n_dp):
            for s in range(n_ex):
                first_row = (r * n_ex + s) * tokens
                block = out[first_row : first_row + tokens, :].astype(BF16)
                if s < n_ex - 1:
                    bodies[r][s, :, at : at + chunk] = block
                else:
                    heads[r][0, :, at : at + chunk] = block


def per_device(
    query, fresh_kv, cache, lengths, moves, residual, out_weight, norm_gain,
    w_gate, w_up, w_down, routes, gates,
):
    n_dp = lax.axis_size("dp")
    n_ex = lax.axis_size("expert")
    tokens, model = query.shape
    width = fresh_kv.shape[1] // 2
    kv_heads = width // HD
    part = out_weight.shape[0]
    context = cache.shape[1]
    shape = jax.ShapeDtypeStruct

    ext_width = -(-(3 * n_dp + 3) // LANES) * LANES
    top_count = routes.shape[1]
    small = (query, fresh_kv, residual, routes.T, gates.T, lengths, moves)
    row, q_in, fresh_in, res_in, ext, info = call(
        functools.partial(entry_kernel, n_dp),
        [
            shape((1, 2 * model + 2 * width + ext_width), BF16),
            shape(query.shape, BF16),
            shape(fresh_kv.shape, BF16),
            shape(residual.shape, BF16),
            shape((tokens, ext_width), F32),
            shape((2 * tokens, LANES), jnp.int32),
        ],
        [spec(pltpu.HBM)] * len(small),
        scratch=[
            pltpu.SMEM((top_count, tokens), jnp.int32),
            pltpu.SMEM((top_count, tokens), F32),
            pltpu.SMEM(lengths.shape, jnp.int32),
            pltpu.SMEM(moves.shape, jnp.int32),
            pltpu.SemaphoreType.DMA((len(small),)),
        ],
        limit=4 << 20,
        flops=COVER,
        moved=tokens * model * 4,
    )(*map(in_hbm, small))
    turns = dp_turns(n_dp)

    def over_dp(array, turn):
        return lax.ppermute(array, "dp", [(j, j ^ turn) for j in range(n_dp)])

    rows = [row] + [over_dp(row, r) for r in range(n_dp - 1, 0, -1)][::-1]

    att, targets = call(
        functools.partial(local_kernel, n_dp, kv_heads),
        [
            shape((n_ex, tokens, part), F32),
            shape((n_dp * n_ex + 8, LANES), jnp.int32),
        ],
        [spec()] * 3 + [spec(pltpu.HBM), spec()],
        scratch=[
            pltpu.VMEM((tokens, model // HD, HD), F32),
            pltpu.SMEM(moves.shape, jnp.int32),
            pltpu.SemaphoreType.DMA(()),
        ],
        limit=4 << 20,
        flops=4 * tokens * model * context,
        moved=cache.size * 2,
    )(info, q_in, fresh_in, in_hbm(moves), cache)

    moved = call(
        functools.partial(moved_kernel, n_dp, n_ex, kv_heads, 2 * width),
        [shape((tokens, part), BF16)] * n_ex
        + [shape((tokens, model), F32), shape((tokens, ext_width), F32)],
        [spec()] * (n_dp + 5),
        scratch=[
            pltpu.VMEM(row.shape, F32),
            pltpu.VMEM((model // HD, HD), F32),
            pltpu.VMEM((n_ex, tokens, part), F32),
        ],
        limit=6 << 20,
        flops=COVER,
        moved=cache.size // tokens * 2,
    )(info, *rows, att, cache, res_in, ext)
    blocks = crossed_exchange(moved[:n_ex], n_dp, n_ex)
    base, ext_all = moved[n_ex:]

    partials = call(
        functools.partial(project_kernel, n_ex),
        [shape((tokens, model), F32)] + [shape((tokens, model), BF16)] * (n_ex - 1),
        [spec()] * (n_ex + 1),
        scratch=[pltpu.VMEM((n_ex * tokens, part), F32)],
        limit=4 << 20,
        flops=2 * n_ex * tokens * part * model,
        moved=out_weight.size * 2,
    )(*blocks, out_weight)
    partials = crossed_exchange(partials, n_dp, n_ex)

    hidden, payload = call(
        functools.partial(norm_kernel, n_ex, n_dp),
        [shape((tokens, model), F32), shape((tokens, model + ext_width), BF16)],
        [spec()] * (n_ex + 3),
        limit=4 << 20,
        flops=COVER,
        moved=tokens * model * 16,
    )(*partials, base, ext_all, norm_gain[None])
    gathered = crossed_exchange([payload] * n_ex, n_dp, n_ex)
    top, last = turns[-1], n_ex - 1
    near = over_dp(payload, top)
    handed = call(hand_kernel, shape(payload.shape, BF16), [spec()], limit=1 << 20)(gathered[last])
    far = over_dp(handed, top)
    rest = over_dp(jnp.stack(gathered[1:last]), top)
    pieces = {
        0: jnp.concatenate(gathered, axis=0),
        top: jnp.concatenate([near] + [rest[s] for s in range(n_ex - 2)] + [far], axis=0),
    }
    for turn in reversed(turns[:-1]):
        for r in list(pieces):
            pieces[r ^ turn] = over_dp(pieces[r], turn)

    group_rows = n_ex * tokens
    all_rows = n_dp * group_rows
    hidden_units = w_down.shape[1]
    weights_bytes = (w_gate.size + w_up.size + w_down.size) * 2
    done = call(
        functools.partial(expert_kernel, n_dp, n_ex, tokens),
        [shape((n_ex - 1, tokens, model), BF16)] * n_dp
        + [shape((1, tokens, model), BF16)] * n_dp
        + [shape((tokens, model), F32)],
        [spec()] * (n_dp + 6),
        scratch=[
            pltpu.VMEM((all_rows, model), BF16),
            pltpu.VMEM((all_rows, hidden_units), F32),
            pltpu.VMEM((all_rows, hidden_units), F32),
        ],
        limit=(8 << 20) + all_rows * model * 8,
        flops=6 * all_rows * model * hidden_units,
        moved=weights_bytes,
    )(targets, *[pieces[r] for r in range(n_dp)], w_gate, w_up, w_down, norm_gain[None], hidden)
    terms = {r: [(done[r], done[n_dp + r])] for r in range(n_dp)}
    reach = {0: 0}
    for i, turn in enumerate(turns):
        reach |= {r ^ turn: mark | 1 << i for r, mark in reach.items()}
    real = done[2 * n_dp]

    def added(arrays):
        return functools.reduce(jnp.add, [array.astype(F32) for array in arrays])

    for i, turn in enumerate(turns[:-1]):
        far = {r: r ^ turn for r in terms if reach[r] >> i & 1}
        for r in sorted(far, key=lambda r: -reach[r]):
            body, head = zip(*terms.pop(r))
            got = []
            for arrays in (head, body):
                whole = arrays[0] if len(arrays) == 1 else added(arrays).astype(BF16)
                got.append(over_dp(whole, turn))
            terms[far[r]].append((got[1], got[0]))

    body, head = zip(*terms[top])
    arrived = {last: (over_dp(added(head).astype(BF16), top), 0)}
    summed = call(
        middle_kernel,
        [shape((count, tokens, model), BF16) for count in (last - 1, 1)],
        [spec()] * len(body),
        limit=1 << 20,
    )(*body)
    for start, stop, blocks in ((1, last, summed[0]), (0, 1, summed[1])):
        got = over_dp(blocks, top)
        arrived |= {s: (got, s - start) for s in range(start, stop)}
    body, head = zip(*terms[0])
    mixed = [
        call(
            functools.partial(add_kernel, 0 if s == last else s, arrived[s][1]),
            shape((tokens, model), BF16 if s else F32),
            [spec()] * (len(body) + 1),
            limit=1 << 20,
        )(arrived[s][0], *(head if s == last else body))
        for s in range(n_ex)
    ]
    back = crossed_exchange(mixed, n_dp, n_ex)
    total = real
    for s in range(n_ex):
        total = total + back[s].astype(F32)
    return total.astype(BF16)


def solution(mesh):
    placed = (
        P(("groups", "dp", "expert"), None),
        P(("groups", "dp", "expert"), None),
        P(("groups", "dp", "expert"), None, None),
        P(("groups", "dp", "expert")),
        P("groups", None),
        P(("groups", "dp", "expert"), None),
        P("expert", None),
        P(),
        P("dp", None, "expert"),
        P("dp", None, "expert"),
        P("dp", "expert", None),
        P(("groups", "dp", "expert"), None),
        P(("groups", "dp", "expert"), None),
    )

    return jax.shard_map(
        per_device,
        mesh=mesh,
        in_specs=placed,
        out_specs=P(("groups", "dp", "expert"), None),
        check_vma=False,
    )
```

```python
import functools

import jax
import jax.numpy as jnp
from jax import lax
from jax.experimental import pallas as pl
from jax.experimental.pallas import tpu as pltpu
from jax.sharding import PartitionSpec as P


HD = 128
LANES = 128
NORM_EPS = 1e-06
F32 = jnp.float32
BF16 = jnp.bfloat16
COVER = 10**10


def dp_turns(n_dp):
    return [(1 << b) | 1 for b in range(n_dp.bit_length() - 1)]


def crossed_exchange(blocks, n_dp, n_ex):
    moved = list(blocks)
    for step in range(n_ex - 1, 0, -1):
        pairs = [
            (d * n_ex + e, (d ^ 1) * n_ex + (e ^ step)) for d in range(n_dp) for e in range(n_ex)
        ]
        moved[step] = lax.ppermute(blocks[step], ("dp", "expert"), pairs)
    return moved


def spec(space=pltpu.VMEM):
    return pl.BlockSpec(memory_space=space)


def call(kernel, outs, ins, scratch=(), limit=None, flops=0, moved=0):
    many = isinstance(outs, (list, tuple))
    return pl.pallas_call(
        kernel,
        out_shape=outs,
        in_specs=ins,
        out_specs=[spec()] * len(outs) if many else spec(),
        scratch_shapes=list(scratch),
        compiler_params=pltpu.CompilerParams(vmem_limit_bytes=limit),
        cost_estimate=pl.CostEstimate(flops=flops, bytes_accessed=moved, transcendentals=0),
    )


def attend(jobs, kv_heads):
    chains = []
    for q_row, _, q_scr, _, _, _ in jobs:
        heads = q_row.shape[1] // HD
        for h in range(heads):
            q_scr[h : h + 1, :] = q_row[:, h * HD : (h + 1) * HD].astype(F32)
    for job in jobs:
        q_row, fresh_row, q_scr, _, _, _ = job
        group = q_row.shape[1] // HD // kv_heads
        for g in range(kv_heads):
            q = q_scr[g * group : (g + 1) * group, :]
            own_key = fresh_row[:, g * HD : (g + 1) * HD].astype(F32)
            own = jnp.sum(q * own_key, axis=-1, keepdims=True) * HD ** (-0.5)
            chains.append([job, g, group, q.astype(BF16), own])
    return chains


def attend_cache(chains, kv_heads):
    width = kv_heads * HD
    all_scores = []
    for (_, _, _, cache, _, _), g, _, q, _ in chains:
        keys = cache[:, g * HD : (g + 1) * HD]
        all_scores.append(
            lax.dot_general(q, keys, (((1,), (1,)), ((), ())), preferred_element_type=F32)
            * HD ** (-0.5)
        )
    parts = []
    for scores, ((_, _, _, _, length, _), _, _, _, own) in zip(all_scores, chains):
        if length is not None:
            valid = lax.broadcasted_iota(jnp.int32, scores.shape, 1) < length
            scores = jnp.where(valid, scores, -1e30)
        top_cache = jnp.max(scores, axis=-1, keepdims=True)
        weights = jnp.exp(scores - top_cache)
        if length is not None:
            weights = jnp.where(valid, weights, 0.0)
        total = jnp.sum(weights, axis=-1, keepdims=True)
        top = jnp.maximum(top_cache, own)
        parts.append((weights.astype(BF16), total, jnp.exp(top_cache - top), jnp.exp(own - top)))
    mixes = []
    for (weights, _, _, _), ((_, _, _, cache, _, _), g, _, _, _) in zip(parts, chains):
        values = cache[:, width + g * HD : width + (g + 1) * HD]
        mixes.append(jnp.dot(weights, values, preferred_element_type=F32))
    for mixed, (_, total, cache_factor, own_factor), (job, g, group, _, _) in zip(
        mixes, parts, chains
    ):
        _, fresh_row, _, _, _, put = job
        own_value = fresh_row[:, width + g * HD : width + (g + 1) * HD].astype(F32)
        done = (cache_factor * mixed + own_factor * own_value) / (
            cache_factor * total + own_factor
        )
        for j in range(group):
            put(g * group + j, done[j : j + 1, :])


def entry_kernel(
    n_dp, q_hbm, fresh_hbm, res_hbm, routes_hbm, gates_hbm, len_hbm, moves_hbm,
    row_ref, q_ref, fresh_ref, res_ref, ext_ref, info_ref, routes, gates, lengths, moves, sems,
):
    copies = [
        pltpu.make_async_copy(source, to, sems.at[i])
        for i, (source, to) in enumerate(
            [
                (routes_hbm, routes), (gates_hbm, gates), (q_hbm, q_ref),
                (fresh_hbm, fresh_ref), (res_hbm, res_ref), (len_hbm, lengths), (moves_hbm, moves),
            ]
        )
    ]
    for copy in copies:
        copy.start()
    copies[0].wait()
    copies[1].wait()
    top, tokens = routes.shape
    lane = lax.broadcasted_iota(jnp.int32, (1, ext_ref.shape[1]), 1)
    turn = jnp.where(lane >= n_dp, 1, 0) + jnp.where(lane >= 2 * n_dp, 1, 0)
    name = lane - n_dp * turn
    for t in range(tokens):
        share = jnp.zeros(lane.shape, F32)
        for k in range(top):
            share = jnp.where(name == routes[k, t], gates[k, t], share)
        high = share.astype(BF16).astype(F32)
        middle = (share - high).astype(BF16).astype(F32)
        low = share - high - middle
        share = jnp.where(turn == 0, high, jnp.where(turn == 1, middle, low))
        ext_ref[t : t + 1, :] = jnp.where(lane < 3 * n_dp, share, 0.0)
    for copy in copies[2:]:
        copy.wait()
    for t in range(tokens):
        info_ref[t : t + 1, :] = jnp.full((1, LANES), lengths[t], jnp.int32)
    dp = lax.axis_index("dp")
    rel = moves[lax.axis_index("expert"), dp] ^ dp
    info_ref[tokens : tokens + 1, :] = jnp.full((1, LANES), rel, jnp.int32)
    model, width = q_ref.shape[1], fresh_ref.shape[1]
    row_ref[:, :model] = q_ref[0:1, :]
    row_ref[:, model : model + width] = fresh_ref[0:1, :]
    row_ref[:, model + width : 2 * model + width] = res_ref[0:1, :]
    row_ref[:, 2 * model + width :] = ext_ref[0:1, :].astype(BF16)


def local_kernel(
    n_dp, kv_heads, info_ref, q_ref, fresh_ref, moves_hbm, cache_ref,
    att_ref, to_ref, q_scr, moves, moves_sem,
):
    parts, tokens, part = att_ref.shape
    goals = pltpu.make_async_copy(moves_hbm, moves, moves_sem)
    goals.start()
    per = part // HD
    jobs = []
    for t in range(1, tokens):

        def put(head, row, t=t):
            att_ref[head // per, t : t + 1, (head % per) * HD : (head % per + 1) * HD] = row

        jobs.append(
            (
                q_ref[t : t + 1, :], fresh_ref[t : t + 1, :], q_scr.at[t], cache_ref.at[t],
                info_ref[t : t + 1, 0:1], put,
            )
        )
    attend_cache(attend(jobs, kv_heads), kv_heads)
    for s in range(parts):
        att_ref[s, 0:1, :] = jnp.zeros((1, part), F32)
    goals.wait()
    dp = lax.axis_index("dp")
    ex = lax.axis_index("expert")
    for r in range(n_dp):
        for s in range(parts):
            side = 1 if s else 0
            to = ((moves[ex ^ s, dp ^ r ^ side] ^ dp ^ side) * parts + s) * tokens
            at = r * parts + s
            to_ref[at : at + 1, :] = jnp.full((1, LANES), to, jnp.int32)
    source = 0
    for d in range(n_dp):
        source = jnp.where(moves[ex, d] == dp, d, source)
    to_ref[n_dp * parts : n_dp * parts + 1, :] = jnp.full((1, LANES), source ^ dp, jnp.int32)


def in_hbm(array):
    return pltpu.with_memory_space_constraint(array, pltpu.HBM)


def moved_kernel(n_dp, n_ex, kv_heads, width, *refs):
    info_ref = refs[0]
    rows = refs[1 : 1 + n_dp]
    att_ref, cache_ref, res_ref, ext_ref = refs[1 + n_dp : 5 + n_dp]
    outs = refs[5 + n_dp : 5 + n_dp + n_ex]
    base_ref, ext_out, row_scr, q_scr, full = refs[5 + n_dp + n_ex :]
    ex = lax.axis_index("expert")
    tokens = res_ref.shape[0]
    rel = info_ref[tokens : tokens + 1, 0:1]
    row = rows[0][...].astype(F32)
    for r in range(1, n_dp):
        row = jnp.where(rel == r, rows[r][...].astype(F32), row)
    row_scr[...] = row
    model = res_ref.shape[1]
    full[...] = att_ref[...]
    part = full.shape[2]
    per = part // HD

    def put(head, value):
        full[head // per, 0:1, (head % per) * HD : (head % per + 1) * HD] = value

    job = (row_scr[:, :model], row_scr[:, model : model + width], q_scr, cache_ref.at[0], None, put)
    attend_cache(attend([job], kv_heads), kv_heads)
    for s in range(n_ex):
        outs[s][...] = full[s ^ ex].astype(BF16)
    first = lax.broadcasted_iota(jnp.int32, (res_ref.shape[0], 1), 0) == 0
    base_ref[...] = jnp.where(first, row_scr[:, model + width : 2 * model + width], res_ref[...].astype(F32))
    ext_out[...] = jnp.where(first, row_scr[:, 2 * model + width :], ext_ref[...])


def project_kernel(n_ex, *refs):
    blocks, w_ref, outs, lhs = refs[:n_ex], refs[n_ex], refs[n_ex + 1 : -1], refs[-1]
    tokens = blocks[0].shape[0]
    for s in range(n_ex):
        lhs[s * tokens : (s + 1) * tokens, :] = blocks[s][...].astype(F32)
    left = lhs[...].astype(BF16)
    model = w_ref.shape[1]
    chunk = min(1024, model)
    for at in range(0, model, chunk):
        out = jnp.dot(left, w_ref[:, at : at + chunk], preferred_element_type=F32)
        for s in range(n_ex):
            outs[s][:, at : at + chunk] = out[s * tokens : (s + 1) * tokens, :].astype(outs[s].dtype)


def norm_kernel(n_ex, n_dp, *refs):
    parts, base_ref, ext_ref, gain_ref = refs[:n_ex], *refs[n_ex : n_ex + 3]
    hid_ref, pay_ref = refs[n_ex + 3 :]
    hidden = base_ref[...]
    for s in range(n_ex):
        hidden = hidden + parts[s][...].astype(F32)
    hid_ref[...] = hidden
    model = hidden.shape[1]
    mean = jnp.mean(hidden * hidden, axis=-1, keepdims=True) + NORM_EPS
    normed = hidden * lax.rsqrt(mean) * gain_ref[...]
    pay_ref[:, :model] = normed.astype(BF16)
    ext = ext_ref[...]
    root = jnp.sqrt(mean)
    high = root.astype(BF16).astype(F32)
    middle = (root - high).astype(BF16).astype(F32)
    low = root - high - middle
    lane = lax.broadcasted_iota(jnp.int32, ext.shape, 1)
    at = 3 * n_dp
    ext = jnp.where(lane == at, high, ext)
    ext = jnp.where(lane == at + 1, middle, ext)
    ext = jnp.where(lane == at + 2, low, ext)
    pay_ref[:, model:] = ext.astype(BF16)


def add_kernel(at, block, block_ref, *refs):
    total = block_ref[block].astype(F32)
    for ref in refs[:-1]:
        total = total + ref[at].astype(F32)
    refs[-1][...] = total.astype(refs[-1].dtype)


def hand_kernel(source, to):
    to[...] = source[...]


def expert_kernel(n_dp, n_ex, tokens, *refs):
    to_ref = refs[0]
    pieces = refs[1 : 1 + n_dp]
    gate_ref, up_ref, down_ref, gain_ref, hid_ref = refs[1 + n_dp : 6 + n_dp]
    outs = refs[6 + n_dp : 6 + 2 * n_dp]
    real_ref, act_scr, new_scr = refs[6 + 2 * n_dp :]
    dp = lax.axis_index("dp")
    model = gain_ref.shape[1]
    rows = n_ex * tokens
    coef = []
    rel = to_ref[n_dp * n_ex : n_dp * n_ex + 1, 0:1]
    carried = jnp.zeros((1, pieces[0].shape[1]), F32)
    for r in range(n_dp):
        ext = pieces[r][:, model:].astype(F32)
        lane = lax.broadcasted_iota(jnp.int32, ext.shape, 1)
        mine = (lane == dp) | (lane == dp + n_dp) | (lane == dp + 2 * n_dp)
        coef.append(jnp.sum(jnp.where(mine, ext, 0.0), axis=-1, keepdims=True))
        carried = jnp.where(rel == r, pieces[r][0:tokens, :].astype(F32)[0:1, :], carried)
    tail = carried[:, model:]
    lane = lax.broadcasted_iota(jnp.int32, tail.shape, 1)
    root = jnp.sum(
        jnp.where((lane >= 3 * n_dp) & (lane < 3 * n_dp + 3), tail, 0.0), axis=-1, keepdims=True
    )
    first = lax.broadcasted_iota(jnp.int32, (tokens, 1), 0) == 0
    real_ref[...] = jnp.where(first, carried[:, :model] * root / gain_ref[...], hid_ref[...])
    x = jnp.concatenate([piece[:, :model] for piece in pieces], axis=0)
    gate = jnp.dot(x, gate_ref[0], preferred_element_type=F32)
    up = jnp.dot(x, up_ref[0], preferred_element_type=F32)
    act = gate / (1.0 + jnp.exp(-gate)) * up
    for r in range(n_dp):
        act_scr[r * rows : (r + 1) * rows, :] = coef[r] * act[r * rows : (r + 1) * rows, :]
    new_scr[...] = act_scr[...]
    for r in range(n_dp):
        for s in range(n_ex):
            to = to_ref[r * n_ex + s : r * n_ex + s + 1, 0:1][0, 0]
            at = (r * n_ex + s) * tokens
            new_scr[pl.ds(to, 1), :] = act_scr[at : at + 1, :]
    left = new_scr[...].astype(BF16)
    chunk = min(1024, model)
    for at in range(0, model, chunk):
        out = jnp.dot(left, down_ref[0, :, at : at + chunk], preferred_element_type=F32)
        for r in range(n_dp):
            for s in range(n_ex):
                first_row = (r * n_ex + s) * tokens
                outs[r][s, :, at : at + chunk] = out[first_row : first_row + tokens, :].astype(BF16)


def per_device(
    query, fresh_kv, cache, lengths, moves, residual, out_weight, norm_gain,
    w_gate, w_up, w_down, routes, gates,
):
    n_dp = lax.axis_size("dp")
    n_ex = lax.axis_size("expert")
    tokens, model = query.shape
    width = fresh_kv.shape[1] // 2
    kv_heads = width // HD
    part = out_weight.shape[0]
    context = cache.shape[1]
    shape = jax.ShapeDtypeStruct

    ext_width = -(-(3 * n_dp + 3) // LANES) * LANES
    top_count = routes.shape[1]
    small = (query, fresh_kv, residual, routes.T, gates.T, lengths, moves)
    row, q_in, fresh_in, res_in, ext, info = call(
        functools.partial(entry_kernel, n_dp),
        [
            shape((1, 2 * model + 2 * width + ext_width), BF16),
            shape(query.shape, BF16),
            shape(fresh_kv.shape, BF16),
            shape(residual.shape, BF16),
            shape((tokens, ext_width), F32),
            shape((2 * tokens, LANES), jnp.int32),
        ],
        [spec(pltpu.HBM)] * len(small),
        scratch=[
            pltpu.SMEM((top_count, tokens), jnp.int32),
            pltpu.SMEM((top_count, tokens), F32),
            pltpu.SMEM(lengths.shape, jnp.int32),
            pltpu.SMEM(moves.shape, jnp.int32),
            pltpu.SemaphoreType.DMA((len(small),)),
        ],
        limit=4 << 20,
        flops=COVER,
        moved=tokens * model * 4,
    )(*map(in_hbm, small))
    turns = dp_turns(n_dp)

    def over_dp(array, turn):
        return lax.ppermute(array, "dp", [(j, j ^ turn) for j in range(n_dp)])

    rows = [row] + [over_dp(row, r) for r in range(n_dp - 1, 0, -1)][::-1]

    att, targets = call(
        functools.partial(local_kernel, n_dp, kv_heads),
        [
            shape((n_ex, tokens, part), F32),
            shape((n_dp * n_ex + 8, LANES), jnp.int32),
        ],
        [spec()] * 3 + [spec(pltpu.HBM), spec()],
        scratch=[
            pltpu.VMEM((tokens, model // HD, HD), F32),
            pltpu.SMEM(moves.shape, jnp.int32),
            pltpu.SemaphoreType.DMA(()),
        ],
        limit=4 << 20,
        flops=4 * tokens * model * context,
        moved=cache.size * 2,
    )(info, q_in, fresh_in, in_hbm(moves), cache)

    moved = call(
        functools.partial(moved_kernel, n_dp, n_ex, kv_heads, 2 * width),
        [shape((tokens, part), BF16)] * n_ex
        + [shape((tokens, model), F32), shape((tokens, ext_width), F32)],
        [spec()] * (n_dp + 5),
        scratch=[
            pltpu.VMEM(row.shape, F32),
            pltpu.VMEM((model // HD, HD), F32),
            pltpu.VMEM((n_ex, tokens, part), F32),
        ],
        limit=6 << 20,
        flops=COVER,
        moved=cache.size // tokens * 2,
    )(info, *rows, att, cache, res_in, ext)
    blocks = crossed_exchange(moved[:n_ex], n_dp, n_ex)
    base, ext_all = moved[n_ex:]

    partials = call(
        functools.partial(project_kernel, n_ex),
        [shape((tokens, model), F32)] + [shape((tokens, model), BF16)] * (n_ex - 1),
        [spec()] * (n_ex + 1),
        scratch=[pltpu.VMEM((n_ex * tokens, part), F32)],
        limit=4 << 20,
        flops=2 * n_ex * tokens * part * model,
        moved=out_weight.size * 2,
    )(*blocks, out_weight)
    partials = crossed_exchange(partials, n_dp, n_ex)

    hidden, payload = call(
        functools.partial(norm_kernel, n_ex, n_dp),
        [shape((tokens, model), F32), shape((tokens, model + ext_width), BF16)],
        [spec()] * (n_ex + 3),
        limit=4 << 20,
        flops=COVER,
        moved=tokens * model * 16,
    )(*partials, base, ext_all, norm_gain[None])
    gathered = crossed_exchange([payload] * n_ex, n_dp, n_ex)
    top, last = turns[-1], n_ex - 1
    near = over_dp(payload, top)
    handed = call(hand_kernel, shape(payload.shape, BF16), [spec()], limit=1 << 20)(gathered[last])
    far = over_dp(handed, top)
    rest = over_dp(jnp.stack(gathered[1:last]), top)
    pieces = {
        0: jnp.concatenate(gathered, axis=0),
        top: jnp.concatenate([near] + [rest[s] for s in range(n_ex - 2)] + [far], axis=0),
    }
    for turn in reversed(turns[:-1]):
        for r in list(pieces):
            pieces[r ^ turn] = over_dp(pieces[r], turn)

    group_rows = n_ex * tokens
    all_rows = n_dp * group_rows
    hidden_units = w_down.shape[1]
    weights_bytes = (w_gate.size + w_up.size + w_down.size) * 2
    done = call(
        functools.partial(expert_kernel, n_dp, n_ex, tokens),
        [shape((n_ex, tokens, model), BF16)] * n_dp + [shape((tokens, model), F32)],
        [spec()] * (n_dp + 6),
        scratch=[
            pltpu.VMEM((all_rows, hidden_units), F32),
            pltpu.VMEM((all_rows, hidden_units), F32),
        ],
        limit=(8 << 20) + all_rows * model * 8,
        flops=6 * all_rows * model * hidden_units,
        moved=weights_bytes,
    )(targets, *[pieces[r] for r in range(n_dp)], w_gate, w_up, w_down, norm_gain[None], hidden)
    terms = {r: [done[r]] for r in range(n_dp)}
    reach = {0: 0}
    for i, turn in enumerate(turns):
        reach |= {r ^ turn: mark | 1 << i for r, mark in reach.items()}
    real = done[n_dp]

    def added(arrays):
        return functools.reduce(jnp.add, [array.astype(F32) for array in arrays])

    for i, turn in enumerate(turns[:-1]):
        far = {r: r ^ turn for r in terms if reach[r] >> i & 1}
        for r in sorted(far, key=lambda r: -reach[r]):
            whole = terms.pop(r)
            whole = whole[0] if len(whole) == 1 else added(whole).astype(BF16)
            terms[far[r]].append(over_dp(whole, turn))

    def across(at):
        return over_dp(added([t[at] for t in terms[top]]).astype(BF16), top)

    arrived = {}
    for blocks in ([last], range(1, last), [0]):
        got = across(slice(blocks[0], blocks[-1] + 1))
        arrived |= {s: (got, s - blocks[0]) for s in blocks}
    mixed = [
        call(
            functools.partial(add_kernel, s, arrived[s][1]),
            shape((tokens, model), BF16 if s else F32),
            [spec()] * (len(terms[0]) + 1),
            limit=1 << 20,
        )(arrived[s][0], *terms[0])
        for s in range(n_ex)
    ]
    back = crossed_exchange(mixed, n_dp, n_ex)
    total = real
    for s in range(n_ex):
        total = total + back[s].astype(F32)
    return total.astype(BF16)


def solution(mesh):
    placed = (
        P(("groups", "dp", "expert"), None),
        P(("groups", "dp", "expert"), None),
        P(("groups", "dp", "expert"), None, None),
        P(("groups", "dp", "expert")),
        P("groups", None),
        P(("groups", "dp", "expert"), None),
        P("expert", None),
        P(),
        P("dp", None, "expert"),
        P("dp", None, "expert"),
        P("dp", "expert", None),
        P(("groups", "dp", "expert"), None),
        P(("groups", "dp", "expert"), None),
    )

    return jax.shard_map(
        per_device,
        mesh=mesh,
        in_specs=placed,
        out_specs=P(("groups", "dp", "expert"), None),
        check_vma=False,
    )
```

```python
import functools

import jax
import jax.numpy as jnp
from jax import lax
from jax.experimental import pallas as pl
from jax.experimental.pallas import tpu as pltpu
from jax.sharding import PartitionSpec as P


HD = 128
LANES = 128
NORM_EPS = 1e-06
F32 = jnp.float32
BF16 = jnp.bfloat16
COVER = 10**10


def dp_turns(n_dp):
    return [(1 << b) | 1 for b in range(n_dp.bit_length() - 1)]


def crossed_exchange(blocks, n_dp, n_ex):
    moved = list(blocks)
    for step in range(n_ex - 1, 0, -1):
        pairs = [
            (d * n_ex + e, (d ^ 1) * n_ex + (e ^ step)) for d in range(n_dp) for e in range(n_ex)
        ]
        moved[step] = lax.ppermute(blocks[step], ("dp", "expert"), pairs)
    return moved


def spec(space=pltpu.VMEM):
    return pl.BlockSpec(memory_space=space)


def call(kernel, outs, ins, scratch=(), limit=None, flops=0, moved=0):
    many = isinstance(outs, (list, tuple))
    return pl.pallas_call(
        kernel,
        out_shape=outs,
        in_specs=ins,
        out_specs=[spec()] * len(outs) if many else spec(),
        scratch_shapes=list(scratch),
        compiler_params=pltpu.CompilerParams(vmem_limit_bytes=limit),
        cost_estimate=pl.CostEstimate(flops=flops, bytes_accessed=moved, transcendentals=0),
    )


def attend(jobs, kv_heads):
    chains = []
    for q_row, _, q_scr, _, _, _ in jobs:
        heads = q_row.shape[1] // HD
        for h in range(heads):
            q_scr[h : h + 1, :] = q_row[:, h * HD : (h + 1) * HD].astype(F32)
    for job in jobs:
        q_row, fresh_row, q_scr, _, _, _ = job
        group = q_row.shape[1] // HD // kv_heads
        for g in range(kv_heads):
            q = q_scr[g * group : (g + 1) * group, :]
            own_key = fresh_row[:, g * HD : (g + 1) * HD].astype(F32)
            own = jnp.sum(q * own_key, axis=-1, keepdims=True) * HD ** (-0.5)
            chains.append([job, g, group, q.astype(BF16), own])
    return chains


def attend_cache(chains, kv_heads):
    width = kv_heads * HD
    all_scores = []
    for (_, _, _, cache, _, _), g, _, q, _ in chains:
        keys = cache[:, g * HD : (g + 1) * HD]
        all_scores.append(
            lax.dot_general(q, keys, (((1,), (1,)), ((), ())), preferred_element_type=F32)
            * HD ** (-0.5)
        )
    parts = []
    for scores, ((_, _, _, _, length, _), _, _, _, own) in zip(all_scores, chains):
        if length is not None:
            valid = lax.broadcasted_iota(jnp.int32, scores.shape, 1) < length
            scores = jnp.where(valid, scores, -1e30)
        top_cache = jnp.max(scores, axis=-1, keepdims=True)
        weights = jnp.exp(scores - top_cache)
        if length is not None:
            weights = jnp.where(valid, weights, 0.0)
        total = jnp.sum(weights, axis=-1, keepdims=True)
        top = jnp.maximum(top_cache, own)
        parts.append((weights.astype(BF16), total, jnp.exp(top_cache - top), jnp.exp(own - top)))
    mixes = []
    for (weights, _, _, _), ((_, _, _, cache, _, _), g, _, _, _) in zip(parts, chains):
        values = cache[:, width + g * HD : width + (g + 1) * HD]
        mixes.append(jnp.dot(weights, values, preferred_element_type=F32))
    for mixed, (_, total, cache_factor, own_factor), (job, g, group, _, _) in zip(
        mixes, parts, chains
    ):
        _, fresh_row, _, _, _, put = job
        own_value = fresh_row[:, width + g * HD : width + (g + 1) * HD].astype(F32)
        done = (cache_factor * mixed + own_factor * own_value) / (
            cache_factor * total + own_factor
        )
        for j in range(group):
            put(g * group + j, done[j : j + 1, :])


def entry_kernel(
    n_dp, q_hbm, fresh_hbm, res_hbm, routes_hbm, gates_hbm, len_hbm, moves_hbm,
    row_ref, q_ref, fresh_ref, res_ref, ext_ref, info_ref, routes, gates, lengths, moves, sems,
):
    copies = [
        pltpu.make_async_copy(source, to, sems.at[i])
        for i, (source, to) in enumerate(
            [
                (routes_hbm, routes), (gates_hbm, gates), (q_hbm, q_ref),
                (fresh_hbm, fresh_ref), (res_hbm, res_ref), (len_hbm, lengths), (moves_hbm, moves),
            ]
        )
    ]
    for copy in copies:
        copy.start()
    copies[0].wait()
    copies[1].wait()
    top, tokens = routes.shape
    lane = lax.broadcasted_iota(jnp.int32, (1, ext_ref.shape[1]), 1)
    turn = jnp.where(lane >= n_dp, 1, 0) + jnp.where(lane >= 2 * n_dp, 1, 0)
    name = lane - n_dp * turn
    for t in range(tokens):
        share = jnp.zeros(lane.shape, F32)
        for k in range(top):
            share = jnp.where(name == routes[k, t], gates[k, t], share)
        high = share.astype(BF16).astype(F32)
        middle = (share - high).astype(BF16).astype(F32)
        low = share - high - middle
        share = jnp.where(turn == 0, high, jnp.where(turn == 1, middle, low))
        ext_ref[t : t + 1, :] = jnp.where(lane < 3 * n_dp, share, 0.0)
    for copy in copies[2:]:
        copy.wait()
    for t in range(tokens):
        info_ref[t : t + 1, :] = jnp.full((1, LANES), lengths[t], jnp.int32)
    dp = lax.axis_index("dp")
    rel = moves[lax.axis_index("expert"), dp] ^ dp
    info_ref[tokens : tokens + 1, :] = jnp.full((1, LANES), rel, jnp.int32)
    model, width = q_ref.shape[1], fresh_ref.shape[1]
    row_ref[:, :model] = q_ref[0:1, :]
    row_ref[:, model : model + width] = fresh_ref[0:1, :]
    row_ref[:, model + width : 2 * model + width] = res_ref[0:1, :]
    row_ref[:, 2 * model + width :] = ext_ref[0:1, :].astype(BF16)


def local_kernel(
    n_dp, kv_heads, info_ref, q_ref, fresh_ref, moves_hbm, cache_ref,
    att_ref, to_ref, q_scr, moves, moves_sem,
):
    parts, tokens, part = att_ref.shape
    goals = pltpu.make_async_copy(moves_hbm, moves, moves_sem)
    goals.start()
    per = part // HD
    jobs = []
    for t in range(1, tokens):

        def put(head, row, t=t):
            att_ref[head // per, t : t + 1, (head % per) * HD : (head % per + 1) * HD] = row

        jobs.append(
            (
                q_ref[t : t + 1, :], fresh_ref[t : t + 1, :], q_scr.at[t], cache_ref.at[t],
                info_ref[t : t + 1, 0:1], put,
            )
        )
    attend_cache(attend(jobs, kv_heads), kv_heads)
    for s in range(parts):
        att_ref[s, 0:1, :] = jnp.zeros((1, part), F32)
    goals.wait()
    dp = lax.axis_index("dp")
    ex = lax.axis_index("expert")
    for r in range(n_dp):
        for s in range(parts):
            side = 1 if s else 0
            to = ((moves[ex ^ s, dp ^ r ^ side] ^ dp ^ side) * parts + s) * tokens
            at = r * parts + s
            to_ref[at : at + 1, :] = jnp.full((1, LANES), to, jnp.int32)
    source = 0
    for d in range(n_dp):
        source = jnp.where(moves[ex, d] == dp, d, source)
    to_ref[n_dp * parts : n_dp * parts + 1, :] = jnp.full((1, LANES), source ^ dp, jnp.int32)


def in_hbm(array):
    return pltpu.with_memory_space_constraint(array, pltpu.HBM)


def moved_kernel(n_dp, n_ex, kv_heads, width, *refs):
    info_ref = refs[0]
    rows = refs[1 : 1 + n_dp]
    att_ref, cache_ref, res_ref, ext_ref = refs[1 + n_dp : 5 + n_dp]
    outs = refs[5 + n_dp : 5 + n_dp + n_ex]
    base_ref, ext_out, row_scr, q_scr, full = refs[5 + n_dp + n_ex :]
    ex = lax.axis_index("expert")
    tokens = res_ref.shape[0]
    rel = info_ref[tokens : tokens + 1, 0:1]
    row = rows[0][...].astype(F32)
    for r in range(1, n_dp):
        row = jnp.where(rel == r, rows[r][...].astype(F32), row)
    row_scr[...] = row
    model = res_ref.shape[1]
    full[...] = att_ref[...]
    part = full.shape[2]
    per = part // HD

    def put(head, value):
        full[head // per, 0:1, (head % per) * HD : (head % per + 1) * HD] = value

    job = (row_scr[:, :model], row_scr[:, model : model + width], q_scr, cache_ref.at[0], None, put)
    attend_cache(attend([job], kv_heads), kv_heads)
    for s in range(n_ex):
        outs[s][...] = full[s ^ ex].astype(BF16)
    first = lax.broadcasted_iota(jnp.int32, (res_ref.shape[0], 1), 0) == 0
    base_ref[...] = jnp.where(first, row_scr[:, model + width : 2 * model + width], res_ref[...].astype(F32))
    ext_out[...] = jnp.where(first, row_scr[:, 2 * model + width :], ext_ref[...])


def project_kernel(n_ex, *refs):
    blocks, w_ref, outs, lhs = refs[:n_ex], refs[n_ex], refs[n_ex + 1 : -1], refs[-1]
    tokens = blocks[0].shape[0]
    for s in range(n_ex):
        lhs[s * tokens : (s + 1) * tokens, :] = blocks[s][...].astype(F32)
    left = lhs[...].astype(BF16)
    model = w_ref.shape[1]
    chunk = min(1024, model)
    for at in range(0, model, chunk):
        out = jnp.dot(left, w_ref[:, at : at + chunk], preferred_element_type=F32)
        for s in range(n_ex):
            outs[s][:, at : at + chunk] = out[s * tokens : (s + 1) * tokens, :].astype(outs[s].dtype)


def norm_kernel(n_ex, n_dp, *refs):
    parts, base_ref, ext_ref, gain_ref = refs[:n_ex], *refs[n_ex : n_ex + 3]
    hid_ref, pay_ref = refs[n_ex + 3 :]
    hidden = base_ref[...]
    for s in range(n_ex):
        hidden = hidden + parts[s][...].astype(F32)
    hid_ref[...] = hidden
    model = hidden.shape[1]
    mean = jnp.mean(hidden * hidden, axis=-1, keepdims=True) + NORM_EPS
    normed = hidden * lax.rsqrt(mean) * gain_ref[...]
    pay_ref[:, :model] = normed.astype(BF16)
    ext = ext_ref[...]
    root = jnp.sqrt(mean)
    high = root.astype(BF16).astype(F32)
    middle = (root - high).astype(BF16).astype(F32)
    low = root - high - middle
    lane = lax.broadcasted_iota(jnp.int32, ext.shape, 1)
    at = 3 * n_dp
    ext = jnp.where(lane == at, high, ext)
    ext = jnp.where(lane == at + 1, middle, ext)
    ext = jnp.where(lane == at + 2, low, ext)
    pay_ref[:, model:] = ext.astype(BF16)


def add_kernel(at, block, block_ref, *refs):
    total = block_ref[block].astype(F32)
    for ref in refs[:-1]:
        total = total + ref[at].astype(F32)
    refs[-1][...] = total.astype(refs[-1].dtype)


def hand_kernel(source, to):
    to[...] = source[...]


def expert_kernel(n_dp, n_ex, tokens, *refs):
    to_ref = refs[0]
    pieces = refs[1 : 1 + n_dp]
    gate_ref, up_ref, down_ref, gain_ref, hid_ref = refs[1 + n_dp : 6 + n_dp]
    outs = refs[6 + n_dp : 6 + 2 * n_dp]
    real_ref, lhs, act_scr, new_scr = refs[6 + 2 * n_dp :]
    dp = lax.axis_index("dp")
    model = gain_ref.shape[1]
    rows = n_ex * tokens
    coef = []
    rel = to_ref[n_dp * n_ex : n_dp * n_ex + 1, 0:1]
    carried = jnp.zeros((1, pieces[0].shape[1]), F32)
    for r in range(n_dp):
        lhs[r * rows : (r + 1) * rows, :] = pieces[r][:, :model]
        ext = pieces[r][:, model:].astype(F32)
        lane = lax.broadcasted_iota(jnp.int32, ext.shape, 1)
        mine = (lane == dp) | (lane == dp + n_dp) | (lane == dp + 2 * n_dp)
        coef.append(jnp.sum(jnp.where(mine, ext, 0.0), axis=-1, keepdims=True))
        carried = jnp.where(rel == r, pieces[r][0:tokens, :].astype(F32)[0:1, :], carried)
    tail = carried[:, model:]
    lane = lax.broadcasted_iota(jnp.int32, tail.shape, 1)
    root = jnp.sum(
        jnp.where((lane >= 3 * n_dp) & (lane < 3 * n_dp + 3), tail, 0.0), axis=-1, keepdims=True
    )
    first = lax.broadcasted_iota(jnp.int32, (tokens, 1), 0) == 0
    real_ref[...] = jnp.where(first, carried[:, :model] * root / gain_ref[...], hid_ref[...])
    x = lhs[...]
    gate = jnp.dot(x, gate_ref[0], preferred_element_type=F32)
    up = jnp.dot(x, up_ref[0], preferred_element_type=F32)
    act = gate / (1.0 + jnp.exp(-gate)) * up
    for r in range(n_dp):
        act_scr[r * rows : (r + 1) * rows, :] = coef[r] * act[r * rows : (r + 1) * rows, :]
    new_scr[...] = act_scr[...]
    for r in range(n_dp):
        for s in range(n_ex):
            to = to_ref[r * n_ex + s : r * n_ex + s + 1, 0:1][0, 0]
            at = (r * n_ex + s) * tokens
            new_scr[pl.ds(to, 1), :] = act_scr[at : at + 1, :]
    left = new_scr[...].astype(BF16)
    chunk = min(1024, model)
    for at in range(0, model, chunk):
        out = jnp.dot(left, down_ref[0, :, at : at + chunk], preferred_element_type=F32)
        for r in range(n_dp):
            for s in range(n_ex):
                first_row = (r * n_ex + s) * tokens
                outs[r][s, :, at : at + chunk] = out[first_row : first_row + tokens, :].astype(BF16)


def per_device(
    query, fresh_kv, cache, lengths, moves, residual, out_weight, norm_gain,
    w_gate, w_up, w_down, routes, gates,
):
    n_dp = lax.axis_size("dp")
    n_ex = lax.axis_size("expert")
    tokens, model = query.shape
    width = fresh_kv.shape[1] // 2
    kv_heads = width // HD
    part = out_weight.shape[0]
    context = cache.shape[1]
    shape = jax.ShapeDtypeStruct

    ext_width = -(-(3 * n_dp + 3) // LANES) * LANES
    top_count = routes.shape[1]
    small = (query, fresh_kv, residual, routes.T, gates.T, lengths, moves)
    row, q_in, fresh_in, res_in, ext, info = call(
        functools.partial(entry_kernel, n_dp),
        [
            shape((1, 2 * model + 2 * width + ext_width), BF16),
            shape(query.shape, BF16),
            shape(fresh_kv.shape, BF16),
            shape(residual.shape, BF16),
            shape((tokens, ext_width), F32),
            shape((2 * tokens, LANES), jnp.int32),
        ],
        [spec(pltpu.HBM)] * len(small),
        scratch=[
            pltpu.SMEM((top_count, tokens), jnp.int32),
            pltpu.SMEM((top_count, tokens), F32),
            pltpu.SMEM(lengths.shape, jnp.int32),
            pltpu.SMEM(moves.shape, jnp.int32),
            pltpu.SemaphoreType.DMA((len(small),)),
        ],
        limit=4 << 20,
        flops=COVER,
        moved=tokens * model * 4,
    )(*map(in_hbm, small))
    turns = dp_turns(n_dp)

    def over_dp(array, turn):
        return lax.ppermute(array, "dp", [(j, j ^ turn) for j in range(n_dp)])

    rows = [row] + [over_dp(row, r) for r in range(n_dp - 1, 0, -1)][::-1]

    att, targets = call(
        functools.partial(local_kernel, n_dp, kv_heads),
        [
            shape((n_ex, tokens, part), F32),
            shape((n_dp * n_ex + 8, LANES), jnp.int32),
        ],
        [spec()] * 3 + [spec(pltpu.HBM), spec()],
        scratch=[
            pltpu.VMEM((tokens, model // HD, HD), F32),
            pltpu.SMEM(moves.shape, jnp.int32),
            pltpu.SemaphoreType.DMA(()),
        ],
        limit=4 << 20,
        flops=4 * tokens * model * context,
        moved=cache.size * 2,
    )(info, q_in, fresh_in, in_hbm(moves), cache)

    moved = call(
        functools.partial(moved_kernel, n_dp, n_ex, kv_heads, 2 * width),
        [shape((tokens, part), BF16)] * n_ex
        + [shape((tokens, model), F32), shape((tokens, ext_width), F32)],
        [spec()] * (n_dp + 5),
        scratch=[
            pltpu.VMEM(row.shape, F32),
            pltpu.VMEM((model // HD, HD), F32),
            pltpu.VMEM((n_ex, tokens, part), F32),
        ],
        limit=6 << 20,
        flops=COVER,
        moved=cache.size // tokens * 2,
    )(info, *rows, att, cache, res_in, ext)
    blocks = crossed_exchange(moved[:n_ex], n_dp, n_ex)
    base, ext_all = moved[n_ex:]

    partials = call(
        functools.partial(project_kernel, n_ex),
        [shape((tokens, model), F32)] + [shape((tokens, model), BF16)] * (n_ex - 1),
        [spec()] * (n_ex + 1),
        scratch=[pltpu.VMEM((n_ex * tokens, part), F32)],
        limit=4 << 20,
        flops=2 * n_ex * tokens * part * model,
        moved=out_weight.size * 2,
    )(*blocks, out_weight)
    partials = crossed_exchange(partials, n_dp, n_ex)

    hidden, payload = call(
        functools.partial(norm_kernel, n_ex, n_dp),
        [shape((tokens, model), F32), shape((tokens, model + ext_width), BF16)],
        [spec()] * (n_ex + 3),
        limit=4 << 20,
        flops=COVER,
        moved=tokens * model * 16,
    )(*partials, base, ext_all, norm_gain[None])
    gathered = crossed_exchange([payload] * n_ex, n_dp, n_ex)
    top, last = turns[-1], n_ex - 1
    near = over_dp(payload, top)
    handed = call(hand_kernel, shape(payload.shape, BF16), [spec()], limit=1 << 20)(gathered[last])
    far = over_dp(handed, top)
    rest = over_dp(jnp.stack(gathered[1:last]), top)
    pieces = {
        0: jnp.concatenate(gathered, axis=0),
        top: jnp.concatenate([near] + [rest[s] for s in range(n_ex - 2)] + [far], axis=0),
    }
    for turn in reversed(turns[:-1]):
        for r in list(pieces):
            pieces[r ^ turn] = over_dp(pieces[r], turn)

    group_rows = n_ex * tokens
    all_rows = n_dp * group_rows
    hidden_units = w_down.shape[1]
    weights_bytes = (w_gate.size + w_up.size + w_down.size) * 2
    done = call(
        functools.partial(expert_kernel, n_dp, n_ex, tokens),
        [shape((n_ex, tokens, model), BF16)] * n_dp + [shape((tokens, model), F32)],
        [spec()] * (n_dp + 6),
        scratch=[
            pltpu.VMEM((all_rows, model), BF16),
            pltpu.VMEM((all_rows, hidden_units), F32),
            pltpu.VMEM((all_rows, hidden_units), F32),
        ],
        limit=(8 << 20) + all_rows * model * 8,
        flops=6 * all_rows * model * hidden_units,
        moved=weights_bytes,
    )(targets, *[pieces[r] for r in range(n_dp)], w_gate, w_up, w_down, norm_gain[None], hidden)
    terms = {r: [done[r]] for r in range(n_dp)}
    reach = {0: 0}
    for i, turn in enumerate(turns):
        reach |= {r ^ turn: mark | 1 << i for r, mark in reach.items()}
    real = done[n_dp]

    def added(arrays):
        return functools.reduce(jnp.add, [array.astype(F32) for array in arrays])

    for i, turn in enumerate(turns[:-1]):
        far = {r: r ^ turn for r in terms if reach[r] >> i & 1}
        for r in sorted(far, key=lambda r: -reach[r]):
            whole = terms.pop(r)
            whole = whole[0] if len(whole) == 1 else added(whole).astype(BF16)
            terms[far[r]].append(over_dp(whole, turn))

    def across(at):
        return over_dp(added([t[at] for t in terms[top]]).astype(BF16), top)

    arrived = {}
    for blocks in ([last], range(last)):
        got = across(slice(blocks[0], blocks[-1] + 1))
        arrived |= {s: (got, s - blocks[0]) for s in blocks}
    mixed = [
        call(
            functools.partial(add_kernel, s, arrived[s][1]),
            shape((tokens, model), BF16 if s else F32),
            [spec()] * (len(terms[0]) + 1),
            limit=1 << 20,
        )(arrived[s][0], *terms[0])
        for s in range(n_ex)
    ]
    back = crossed_exchange(mixed, n_dp, n_ex)
    total = real
    for s in range(n_ex):
        total = total + back[s].astype(F32)
    return total.astype(BF16)


def solution(mesh):
    placed = (
        P(("groups", "dp", "expert"), None),
        P(("groups", "dp", "expert"), None),
        P(("groups", "dp", "expert"), None, None),
        P(("groups", "dp", "expert")),
        P("groups", None),
        P(("groups", "dp", "expert"), None),
        P("expert", None),
        P(),
        P("dp", None, "expert"),
        P("dp", None, "expert"),
        P("dp", "expert", None),
        P(("groups", "dp", "expert"), None),
        P(("groups", "dp", "expert"), None),
    )

    return jax.shard_map(
        per_device,
        mesh=mesh,
        in_specs=placed,
        out_specs=P(("groups", "dp", "expert"), None),
        check_vma=False,
    )
```
